256 devices in a mesh: slide: 8 (over x, core), tile: 32 (over y, z).
Axes of the slice: x: 4, y: 4, z: 8, core: 2. Of those that a mesh axis runs over, the one named last changes fastest.
Arguments:
- features: bfloat16 [8, 2048, 16, 16, 128], P('slide', 'tile'), may hold values from -6 to 6
- tissue_count: int32 [8, 32], P('slide', 'tile'), may hold values from 0 to 64, as said below
- neighbors: int32 [8, 2048, 8], P('slide', 'tile'), may hold values from -1 to 2047, as said below
- worker_perm: int32 [8, 32], P('slide'), may hold values from 0 to 31, each once within a row
- rotation: int32 [8], P('slide'), may hold values from 0 to 1023
- kernel: bfloat16 [9, 128], replicated, may hold values from -2 to 2
- gain: float32 [128], replicated, may hold values from 0.1 to 1.9
- w_in: bfloat16 [128, 512], replicated, may hold values from -0.5 to 0.5
- w_out: bfloat16 [512, 128], replicated, may hold values from -0.25 to 0.25
- cotangent: float32 [8, 1024, 128], P('slide', 'tile'), may hold values from -0.3 to 0.3
Outputs:
- embed: float32 [8, 1024, 128], P('slide', 'tile')
- grad_kernel: float32 [9, 128], replicated
- grad_gain: float32 [128], replicated
- grad_in: float32 [128, 512], replicated
- grad_out: float32 [512, 128], replicated
The draws below stay inside these ranges and needn't reach their ends.
Inputs may be any that keep to these rules, and one draw needn't show every extreme that they name: `tissue_count`: in each group the counts sum to 1024. `neighbors`: each entry is -1 or the slot number q * 64 + j of a tissue slot (j below tissue_count of q) of an owner q equal to the slot's own owner or next to it in the same group; slots at or past their owner's count have -1 everywhere.
All inputs are finite; a program needn't handle non-finite values.
Results may differ from the reference program's by a relative error of at most 0.00065.
Values may be sent and summed in bfloat16 or wider, within the bound.
A program may use at most 64 MiB of HBM per device.

```python
import math
import jax
import jax.numpy as jnp
from jax import lax

C = 128
HID = 512
P_SIZE = 16
WORK_DEV = 32
TILES_DEV = 64
GROUPS = 8
SLOTS = 2048
WORKS = 1024
N_TILE = 32


def counts_helper(key):
    keys = jax.random.split(jax.random.fold_in(key, 11), GROUPS)

    def one_group(group_key):
        first_key, second_key, third_key = jax.random.split(group_key, 3)
        half = N_TILE // 2
        spread = jax.random.randint(first_key, (half,), -WORK_DEV, WORK_DEV + 1)
        forced = jax.random.randint(second_key, (), 0, half)
        spread = jnp.where(jnp.arange(half) == forced, WORK_DEV, spread)
        paired = jnp.concatenate([WORK_DEV + spread, WORK_DEV - spread])
        return jax.random.permutation(third_key, paired)
    return jax.vmap(one_group)(keys).astype(jnp.int32)


def draw_tissue_count(key, part):
    return counts_helper(key)


def draw_neighbors(key, part):
    counts = counts_helper(key)
    first_key, second_key, third_key = jax.random.split(jax.random.fold_in(key, 23), 3)
    shape = (GROUPS, N_TILE, TILES_DEV, 8)
    offset = jax.random.randint(first_key, shape, -1, 2)
    owner = jnp.arange(N_TILE)[None, :, None, None] + offset
    inside = (owner >= 0) & (owner < N_TILE)
    safe_owner = jnp.clip(owner, 0, N_TILE - 1)
    theirs = jax.vmap(lambda table, where_at: table[where_at])(counts, safe_owner)
    chosen = jax.random.randint(second_key, shape, 0, 1048576) % jnp.maximum(theirs, 1)
    keep = jax.random.randint(third_key, shape, 0, 4) > 0
    mine = jnp.arange(TILES_DEV)[None, None, :, None] < counts[:, :, None, None]
    usable = inside & (theirs > 0) & keep & mine
    result = jnp.where(usable, safe_owner * TILES_DEV + chosen, -1)
    return result.reshape(GROUPS, SLOTS, 8).astype(jnp.int32)


def draw_features(key, part):
    first_key, second_key = jax.random.split(jax.random.fold_in(key, 37), 2)
    shape = (GROUPS, SLOTS, P_SIZE, P_SIZE, C)
    means = 0.8 * jax.random.normal(first_key, (GROUPS, SLOTS, 1, 1, C), jnp.float32)
    rough = jax.random.normal(second_key, shape, jnp.float32)
    return jnp.clip(means + rough, -6.0, 6.0).astype(jnp.bfloat16)


def set_ends(entries, rng, least, top_value):
    index_at = [jax.random.randint(jax.random.fold_in(rng, axis), (), 0, length) for axis, length in enumerate(entries.shape)]
    main_axis = entries.shape.index(max(entries.shape))
    next_to = index_at[:main_axis] + [(index_at[main_axis] + 1) % entries.shape[main_axis]] + index_at[main_axis + 1:]
    return entries.at[tuple(index_at)].set(least).at[tuple(next_to)].set(top_value)


def block_scale(rng, extent, cuts, low, high):
    def one(dim, blocks):
        draws = jax.random.uniform(jax.random.fold_in(jax.random.fold_in(rng, 6), dim), (blocks,), jnp.float32, low / len(cuts), high / len(cuts))
        return jnp.repeat(jnp.exp(draws), extent[dim] // blocks).reshape((-1,) + (1,) * (len(extent) - dim - 1))

    factor_of = one(*cuts[0])
    for cut in cuts[1:]:
        factor_of = factor_of * one(*cut)
    return factor_of


def normal_values(rng, extent, deviation, most, shards=(), kind=jnp.bfloat16):
    values = jax.random.normal(rng, extent, jnp.float32) * deviation
    if len(shards) > 0:
        values = block_scale(rng, extent, shards, -0.22, 0.18) * values
    return jnp.clip(values, min=-most, max=most).astype(kind)


def setup_inputs(seed: int = 0) -> dict:
    key_of = jax.random.split(jax.random.key(seed), 11)
    return {
        "features": draw_features(jax.random.fold_in(key_of[10], 71), 0),
        "tissue_count": draw_tissue_count(jax.random.fold_in(key_of[10], 71), 0),
        "neighbors": draw_neighbors(jax.random.fold_in(key_of[10], 71), 0),
        "worker_perm": jax.vmap(lambda own: jax.random.permutation(own, N_TILE))(jax.random.split(key_of[3], GROUPS)).reshape((GROUPS, N_TILE)).astype(jnp.int32),
        "rotation": set_ends(jax.random.randint(key_of[4], (GROUPS,), 0, WORKS), jax.random.fold_in(key_of[4], 1), 0, WORKS - 1).astype(jnp.int32),
        "kernel": normal_values(key_of[5], (9, C), 9 ** -0.5, 2.0),
        "gain": jnp.clip(1.0 + 0.18 * jax.random.normal(key_of[6], (C,), jnp.float32), 0.1, 1.9),
        "w_in": normal_values(key_of[7], (C, HID), C ** -0.5, 0.5),
        "w_out": normal_values(key_of[8], (HID, C), HID ** -0.5, 0.25),
        "cotangent": normal_values(key_of[9], (GROUPS, WORKS, C), 0.05, 0.3, ((0, 8), (1, 32)), jnp.float32),
    }


def border_rows(tiles):
    return jnp.stack([tiles[:, 0], tiles[:, -1], tiles[:, :, 0], tiles[:, :, -1]], axis=1)

def assemble(center, borders, index):
    side = center.shape[1]

    def pick(column, which):
        chosen = index[:, column]
        rows = jnp.take(borders[:, which], jnp.maximum(chosen, 0), axis=0)
        return jnp.where((chosen >= 0)[:, None, None], rows, jnp.zeros_like(rows))
    upper = pick(0, 1)
    lower = pick(1, 0)
    left_col = pick(2, 3)
    right_col = pick(3, 2)
    upper_left = pick(4, 1)[:, side - 1]
    upper_right = pick(5, 1)[:, 0]
    lower_left = pick(6, 0)[:, side - 1]
    lower_right = pick(7, 0)[:, 0]
    top = jnp.concatenate([upper_left[:, None], upper, upper_right[:, None]], axis=1)
    bottom = jnp.concatenate([lower_left[:, None], lower, lower_right[:, None]], axis=1)
    middle = jnp.concatenate([left_col[:, :, None], center, right_col[:, :, None]], axis=2)
    return jnp.concatenate([top[:, None], middle, bottom[:, None]], axis=1)

def gelu_value(before):
    return 0.5 * before * (1.0 + lax.erf(before * 0.7071067811865476))

def gelu_slope(before):
    return 0.5 * (1.0 + lax.erf(before * 0.7071067811865476)) + before * jnp.exp(-0.5 * before * before) * 0.3989422804014327

def block_section(padded, cot_rows, kernel, gain, w_in, w_out):
    count = padded.shape[0]
    side = padded.shape[1] - 2
    chans = padded.shape[3]
    pixels = side * side
    kernel_wide = kernel.astype(jnp.float32)
    shifted = [padded[:, row:row + side, col:col + side, :] for row in range(3) for col in range(3)]
    depth = shifted[0].astype(jnp.float32) * kernel_wide[0]
    for offset in range(1, 9):
        depth = depth + shifted[offset].astype(jnp.float32) * kernel_wide[offset]
    depth = depth.reshape(count * pixels, chans)
    channel_mean = lax.optimization_barrier(jnp.mean(depth, axis=1, keepdims=True))
    centered = depth - channel_mean
    inverse = lax.rsqrt(lax.optimization_barrier(jnp.mean(centered * centered, axis=1, keepdims=True)) + 1e-06)
    unit_values = centered * inverse
    normed = (unit_values * gain).astype(jnp.bfloat16)
    before = jnp.dot(normed, w_in, preferred_element_type=jnp.float32)
    hidden = before.shape[1]
    activated = gelu_value(before).astype(jnp.bfloat16)
    projected = jnp.dot(activated, w_out, preferred_element_type=jnp.float32)
    center = padded[:, 1:side + 1, 1:side + 1, :].astype(jnp.float32).reshape(count * pixels, chans)
    embed = lax.optimization_barrier(jnp.mean((center + projected).reshape(count, pixels, chans), axis=1))
    grad_embed = cot_rows / pixels
    act_sum = lax.optimization_barrier(jnp.sum(activated.reshape(count, pixels, hidden).astype(jnp.float32), axis=1))
    grad_out = jnp.dot(act_sum.T, grad_embed, precision=lax.Precision.HIGHEST)
    grad_act = jnp.dot(grad_embed, w_out.astype(jnp.float32).T, precision=lax.Precision.HIGHEST)
    grad_before = (grad_act[:, None, :] * gelu_slope(before).reshape(count, pixels, hidden)).astype(jnp.bfloat16)
    grad_before = grad_before.reshape(count * pixels, hidden)
    grad_in = jnp.dot(normed.T, grad_before, preferred_element_type=jnp.float32)
    grad_normed = jnp.dot(grad_before, w_in.T, preferred_element_type=jnp.float32)
    grad_gain = lax.optimization_barrier(jnp.sum(grad_normed * unit_values, axis=0))
    grad_unit = grad_normed * gain
    grad_depth = inverse * (grad_unit - lax.optimization_barrier(jnp.mean(grad_unit, axis=1, keepdims=True)) - unit_values * lax.optimization_barrier(jnp.mean(grad_unit * unit_values, axis=1, keepdims=True)))
    grad_depth = grad_depth.reshape(count, side, side, chans)
    grad_kernel = jnp.stack([lax.optimization_barrier(jnp.sum(grad_depth * shifted[offset].astype(jnp.float32), axis=(0, 1, 2))) for offset in range(9)])
    return (embed, (grad_kernel, grad_gain, grad_in, grad_out))

def run_blocks(padded, cot_rows, kernel, gain, w_in, w_out, size):
    count = padded.shape[0]
    group = math.gcd(count, size)
    chans = padded.shape[3]
    hidden = w_in.shape[1]
    stacked = padded.reshape((count // group, group) + padded.shape[1:])
    cot_stack = cot_rows.reshape(count // group, group, cot_rows.shape[1])
    initial = (jnp.zeros((9, chans), jnp.float32), jnp.zeros((chans,), jnp.float32), jnp.zeros((chans, hidden), jnp.float32), jnp.zeros((hidden, chans), jnp.float32))

    def advance(carry, item):
        embed, grads = block_section(item[0], item[1], kernel, gain, w_in, w_out)
        return (jax.tree.map(lambda left, right: left + right, carry, grads), embed)
    totals, embeds = lax.scan(advance, initial, (stacked, cot_stack))
    return (embeds.reshape(count, chans), totals)

def reference(features, tissue_count, neighbors, worker_perm, rotation, kernel, gain, w_in, w_out, cotangent):
    slots = jnp.arange(TILES_DEV, dtype=jnp.int32)
    embeds = []
    totals = None
    for group in range(GROUPS):
        counts = tissue_count[group]
        start = jnp.cumsum(counts, dtype=jnp.int32) - counts
        valid = slots[None, :] < counts[:, None]
        shifted_rank = jnp.mod(start[:, None] + slots[None, :] + rotation[group], WORKS)
        worker = worker_perm[group][jnp.mod(shifted_rank, N_TILE)]
        position = worker * WORK_DEV + shifted_rank // N_TILE
        target = jnp.where(valid, position, WORKS).reshape(-1).astype(jnp.int32)
        source = jnp.zeros((WORKS,), jnp.int32).at[target].set(jnp.arange(SLOTS, dtype=jnp.int32), mode='drop')
        owned = features[group]
        padded = assemble(owned, border_rows(owned), neighbors[group])[source]
        embed, grads = run_blocks(padded, cotangent[group], kernel, gain, w_in, w_out, 16)
        embeds.append(embed)
        if totals is None:
            totals = grads
        else:
            totals = jax.tree.map(lambda left, right: left + right, totals, grads)
    return (jnp.stack(embeds), totals[0], totals[1], totals[2], totals[3])
```

```python
import functools

import jax
import jax.numpy as jnp
from jax import lax
from jax.experimental import pallas as pl
from jax.experimental.pallas import tpu as pltpu
from jax.sharding import PartitionSpec as P

C = 128
HID = 512
S = 16
W = S + 2
G = 8
ROWS = 2
SLOTS = 64
WORK = 32
PEERS = 32
NZ, NY = 8, 4
NX = 4
GROUP_TOTAL = PEERS * WORK
PARTS = 4
MESH = pl.DeviceIdType.MESH
HIGHEST = lax.Precision.HIGHEST


def to_tile(index):
    return dict(device_id={"tile": index}, device_id_type=MESH)


def to_slide(index):
    return dict(device_id={"slide": index}, device_id_type=MESH)


def exchange_kernel(count_ref, feat_ref, cot_ref, strips_ref, rows_ref, mine, block, wide, keep_sem,
                    send_l, recv_l, send_r, recv_r, send_z, recv_z, send_y, recv_y, row_sem):
    me = lax.axis_index("tile")
    y, z = me // NZ, me % NZ
    right, left = (me + 1) % PEERS, (me + PEERS - 1) % PEERS
    z_peers = [y * NZ + (z + d) % NZ for d in range(1, NZ)]
    y_peers = [((y + d) % NY) * NZ + z for d in range(1, NY)]

    barrier = pltpu.get_barrier_semaphore()
    for peer in z_peers + y_peers + [right, left]:
        pl.semaphore_signal(barrier, inc=1, **to_tile(peer))
    pl.semaphore_wait(barrier, NZ + NY)

    block[0:WORK, :] = cot_ref[...]
    block[WORK:, :] = jnp.full((8, C), count_ref[0, 0].astype(jnp.float32), jnp.float32)
    own_rows = pltpu.make_async_copy(block, rows_ref.at[me], row_sem)
    own_rows.start()
    z_copies = []
    for d in range(1, NZ):
        z_copies.append(pltpu.make_async_remote_copy(
            src_ref=block, dst_ref=rows_ref.at[me], send_sem=send_z.at[d - 1], recv_sem=recv_z.at[d - 1],
            **to_tile(z_peers[d - 1])))
        z_copies[-1].start()

    copies = []
    per = SLOTS // PARTS
    for part in range(PARTS):
        def one(i, _):
            t = part * per + i
            mine[t, 0] = feat_ref[t, 0]
            mine[t, 1] = feat_ref[t, S - 1]
            for row in range(S):
                wide[pl.ds(row * S, S), :] = feat_ref[t, row].astype(jnp.float32)
            mine[t, 2] = wide[pl.ds(0, S, stride=S), :].astype(jnp.bfloat16)
            mine[t, 3] = wide[pl.ds(S - 1, S, stride=S), :].astype(jnp.bfloat16)
            return 0

        lax.fori_loop(0, per, one, 0)
        span = pl.ds(part * per, per)
        keep = pltpu.make_async_copy(mine.at[span], strips_ref.at[pl.ds(SLOTS + part * per, per)], keep_sem.at[part])
        to_right = pltpu.make_async_remote_copy(
            src_ref=mine.at[span], dst_ref=strips_ref.at[span],
            send_sem=send_r.at[part], recv_sem=recv_r.at[part], **to_tile(right))
        to_left = pltpu.make_async_remote_copy(
            src_ref=mine.at[span], dst_ref=strips_ref.at[pl.ds(2 * SLOTS + part * per, per)],
            send_sem=send_l.at[part], recv_sem=recv_l.at[part], **to_tile(left))
        for copy in (keep, to_right, to_left):
            copy.start()
            copies.append(copy)

    own_rows.wait()
    for copy in z_copies:
        copy.wait_recv()
    y_copies = []
    slab = rows_ref.at[pl.ds(y * NZ, NZ)]
    for d in range(1, NY):
        y_copies.append(pltpu.make_async_remote_copy(
            src_ref=slab, dst_ref=slab, send_sem=send_y.at[d - 1], recv_sem=recv_y.at[d - 1],
            **to_tile(y_peers[d - 1])))
        y_copies[-1].start()
    for copy in z_copies:
        copy.wait_send()
    for copy in y_copies + copies:
        copy.wait()


def exchange(count, feat, cot):
    dma = pltpu.SemaphoreType.DMA
    return pl.pallas_call(
        exchange_kernel,
        in_specs=[
            pl.BlockSpec(memory_space=pltpu.SMEM),
            pl.BlockSpec(memory_space=pltpu.VMEM),
            pl.BlockSpec(memory_space=pltpu.VMEM),
        ],
        out_specs=[pl.BlockSpec(memory_space=pl.ANY)] * 2,
        out_shape=[
            jax.ShapeDtypeStruct((3 * SLOTS, 4, S, C), jnp.bfloat16),
            jax.ShapeDtypeStruct((PEERS, WORK + 8, C), jnp.float32),
        ],
        scratch_shapes=[
            pltpu.VMEM((SLOTS, 4, S, C), jnp.bfloat16),
            pltpu.VMEM((WORK + 8, C), jnp.float32),
            pltpu.VMEM((S * S, C), jnp.float32),
            dma((PARTS,)), dma((PARTS,)), dma((PARTS,)), dma((PARTS,)), dma((PARTS,)),
            dma((NZ - 1,)), dma((NZ - 1,)), dma((NY - 1,)), dma((NY - 1,)), dma,
        ],
        compiler_params=pltpu.CompilerParams(
            collective_id=0, has_side_effects=True, vmem_limit_bytes=32 << 20),
        name="exchange",
    )(count, feat, cot)


def compute_kernel(nb_ref, counts_ref, perm_ref, turn_ref, feat_ref, strips_ref, rows_ref, taps_ref, gain_ref,
                   w_in_ref, w_in_t_ref, w_out_ref, send_ref, go_ref, gi_ref, small_ref, where_ref,
                   pad, ge, ga, act, cen, gk, gg, taps):
    g = pl.program_id(0)
    me = lax.axis_index("tile")
    count = counts_ref[me]
    turn = turn_ref[0]
    base = (me - 1) * SLOTS

    def start_of(owner):
        return lax.fori_loop(0, owner, lambda q, s: s + counts_ref[q], jnp.int32(0))

    @pl.when(g == 0)
    def _():
        gk[...] = jnp.zeros_like(gk)
        gg[...] = jnp.zeros_like(gg)
        gi_ref[...] = jnp.zeros_like(gi_ref)
        act[...] = jnp.zeros_like(act)
        cen[...] = jnp.zeros_like(cen)
        ge[...] = jnp.zeros_like(ge)
        for k in range(9):
            taps[k] = jnp.broadcast_to(taps_ref[k:k + 1, :].astype(jnp.float32), (G, C))
        first = start_of(me) + turn

        def row(i, _):
            rank = (first + i) & (GROUP_TOTAL - 1)
            worker = perm_ref[rank & (PEERS - 1)]
            ge[pl.ds(i, 1), :] = rows_ref[worker, pl.ds(rank >> 5, 1), :] * (1.0 / (S * S))
            return 0

        lax.fori_loop(0, count, row, 0)
        ga[...] = lax.dot_general(ge[...], w_out_ref[...].astype(jnp.float32), (((1,), (1,)), ((), ())),
                                  precision=HIGHEST, preferred_element_type=jnp.float32)

    @pl.when(g * G < count)
    def _():
        for t in range(G):
            for y in range(S):
                pad[pl.ds(((y + 1) * W + 1) * G + t, S, stride=G), :] = feat_ref[t, y].astype(jnp.float32)

            def strip(k, which):
                n = nb_ref[(g * G + t) * 8 + k]
                ok = n >= 0
                x = strips_ref[jnp.where(ok, n - base, 0), which].astype(jnp.float32)
                return jnp.where(ok, x, 0.0)

            pad[pl.ds(1 * G + t, S, stride=G), :] = strip(0, 1)
            pad[pl.ds(((S + 1) * W + 1) * G + t, S, stride=G), :] = strip(1, 0)
            pad[pl.ds(W * G + t, S, stride=G * W), :] = strip(2, 3)
            pad[pl.ds((W + S + 1) * G + t, S, stride=G * W), :] = strip(3, 2)
            pad[pl.ds(t, 1), :] = strip(4, 1)[S - 1:S]
            pad[pl.ds((S + 1) * G + t, 1), :] = strip(5, 1)[0:1]
            pad[pl.ds((S + 1) * W * G + t, 1), :] = strip(6, 0)[S - 1:S]
            pad[pl.ds(((S + 1) * W + S + 1) * G + t, 1), :] = strip(7, 0)[0:1]

        gain = gain_ref[...]
        mine = pl.ds(pl.multiple_of(g * G, G), G)
        slope_scale = ga[mine, :]
        n = ROWS * S * G

        def window(y, a, b):
            rows = [pad[pl.ds(((y + r + a) * W + b) * G, S * G), :] for r in range(ROWS)]
            return jnp.concatenate(rows, axis=0).reshape(ROWS * S, G, C)

        sub = lax.broadcasted_iota(jnp.int32, (G, n), 0)
        col = lax.broadcasted_iota(jnp.int32, (G, n), 1)
        select = jnp.where((col & (G - 1)) == sub, 1.0, 0.0).astype(jnp.bfloat16)

        def chunk(c, carry):
            act_sum, centre = carry
            y = c * ROWS
            depth = None
            for a in range(3):
                for b in range(3):
                    x = window(y, a, b)
                    if a == 1 and b == 1:
                        centre = centre + jnp.sum(x, axis=0)
                    term = x * taps[3 * a + b][None]
                    depth = term if depth is None else depth + term
            depth = depth.reshape(n, C)
            centered = depth - jnp.mean(depth, axis=1, keepdims=True)
            inverse = lax.rsqrt(jnp.mean(centered * centered, axis=1, keepdims=True) + 1e-06)
            unit = centered * inverse
            normed = (unit * gain).astype(jnp.bfloat16)
            acts, grads = [], []
            half = HID // 2
            for h in range(0, HID, half):
                v = jnp.dot(normed, w_in_ref[:, h:h + half], preferred_element_type=jnp.float32)
                share = 0.5 * (1.0 + lax.erf(v * 0.7071067811865476))
                slope = share + v * (jnp.exp(-0.5 * v * v) * 0.3989422804014327)
                acts.append((v * share).astype(jnp.bfloat16))
                scaled = slope.reshape(ROWS * S, G, half) * slope_scale[None, :, h:h + half]
                grads.append(scaled.reshape(n, half).astype(jnp.bfloat16))
            act_sum = act_sum + jnp.dot(select, jnp.concatenate(acts, axis=1), preferred_element_type=jnp.float32)
            grad_before = jnp.concatenate(grads, axis=1)
            gi_ref[...] += lax.dot_general(normed, grad_before, (((0,), (0,)), ((), ())),
                                           preferred_element_type=jnp.float32)
            grad_normed = jnp.dot(grad_before, w_in_t_ref[...], preferred_element_type=jnp.float32)
            product = grad_normed * unit
            gg[...] += jnp.sum(product.reshape(ROWS * S, G, C), axis=0)
            grad_unit = grad_normed * gain
            grad_depth = inverse * (
                grad_unit
                - jnp.mean(grad_unit, axis=1, keepdims=True)
                - unit * jnp.mean(product * gain, axis=1, keepdims=True)
            )
            grad_depth = grad_depth.reshape(ROWS * S, G, C)
            for a in range(3):
                for b in range(3):
                    gk[3 * a + b] += jnp.sum(grad_depth * window(y, a, b), axis=0)
            return act_sum, centre

        act_sum, centre = lax.fori_loop(
            0, S // ROWS, chunk, (jnp.zeros((G, HID), jnp.float32), jnp.zeros((G, C), jnp.float32)))
        act[mine, :] = act_sum
        cen[mine, :] = centre

    @pl.when(g == pl.num_programs(0) - 1)
    def _():
        go_ref[...] = lax.dot_general(act[...], ge[...], (((0,), (0,)), ((), ())),
                                      precision=HIGHEST, preferred_element_type=jnp.float32)
        embed = jnp.dot(act[...], w_out_ref[...].astype(jnp.float32), precision=HIGHEST,
                        preferred_element_type=jnp.float32)
        cen[...] = (cen[...] + embed) * (1.0 / (S * S))
        small_ref[...] = jnp.zeros_like(small_ref)
        for k in range(9):
            small_ref[k:k + 1, :] = jnp.sum(gk[k], axis=0, keepdims=True)
        small_ref[9:10, :] = jnp.sum(gg[...], axis=0, keepdims=True)
        send_ref[...] = jnp.zeros_like(send_ref)
        first = start_of(me) + turn

        def out_row(i, _):
            rank = (first + i) & (GROUP_TOTAL - 1)
            worker = perm_ref[rank & (PEERS - 1)]
            send_ref[worker, pl.ds(i >> 5, 1), :] = cen[pl.ds(i, 1), :]
            return 0

        lax.fori_loop(0, count, out_row, 0)
        residue = lax.fori_loop(0, PEERS, lambda r, s: jnp.where(perm_ref[r] == me, r, s), jnp.int32(0))

        def arrival(owner, start):
            slot = (residue - start - turn) & (PEERS - 1)
            for k in range(2):
                @pl.when(slot + k * PEERS < counts_ref[owner])
                def _():
                    place = ((start + slot + k * PEERS + turn) & (GROUP_TOTAL - 1)) >> 5
                    where_ref[place] = owner
                    where_ref[WORK + place] = k
            return start + counts_ref[owner]

        lax.fori_loop(0, PEERS, arrival, jnp.int32(0))


def compute(nb, counts, perm, turn, feat, strips, rows, taps, gain, w_in, w_in_t, w_out):
    const = lambda x: pl.BlockSpec(x.shape, lambda g, *_: (0,) * x.ndim)
    outs = [
        jax.ShapeDtypeStruct((PEERS, 2, C), jnp.float32),
        jax.ShapeDtypeStruct((HID, C), jnp.float32),
        jax.ShapeDtypeStruct((C, HID), jnp.float32),
        jax.ShapeDtypeStruct((16, C), jnp.float32),
    ]
    grid_spec = pltpu.PrefetchScalarGridSpec(
        num_scalar_prefetch=4,
        grid=(SLOTS // G,),
        in_specs=[pl.BlockSpec((G, S, S, C), lambda g, *_: (g, 0, 0, 0))]
        + [const(x) for x in (strips, rows, taps, gain, w_in, w_in_t, w_out)],
        out_specs=[const(x) for x in outs] + [pl.BlockSpec(memory_space=pltpu.SMEM)],
        scratch_shapes=[
            pltpu.VMEM((W * W * G, C), jnp.float32),
            pltpu.VMEM((SLOTS, C), jnp.float32),
            pltpu.VMEM((SLOTS, HID), jnp.float32),
            pltpu.VMEM((SLOTS, HID), jnp.float32),
            pltpu.VMEM((SLOTS, C), jnp.float32),
            pltpu.VMEM((9, G, C), jnp.float32),
            pltpu.VMEM((G, C), jnp.float32),
            pltpu.VMEM((9, G, C), jnp.float32),
        ],
    )
    return pl.pallas_call(
        compute_kernel,
        grid_spec=grid_spec,
        out_shape=outs + [jax.ShapeDtypeStruct((2 * WORK,), jnp.int32)],
        compiler_params=pltpu.CompilerParams(vmem_limit_bytes=48 << 20),
        name="compute",
    )(nb, counts, perm, turn, feat, strips, rows, taps, gain, w_in, w_in_t, w_out)


UNITS = 17


def reduce_kernel(where_ref, rows_ref, go_ref, gi_ref, small_ref, embed_ref, gk_ref, gg_ref, gi_out, go_out,
                  full, result, from_core, half, from_x, piece, from_tile, landed,
                  row_send, row_recv, core_send, core_recv, x_send, x_recv, unit_send, unit_recv,
                  back_send, back_recv, x_back_send, x_back_recv, core_back_send, core_back_recv):
    me = lax.axis_index("tile")
    slide = lax.axis_index("slide")
    x, core = slide // 2, slide % 2
    partner = x * 2 + (1 - core)
    x_peers = [((x + d) % NX) for d in range(1, NX)]

    barrier = pltpu.get_barrier_semaphore()
    for d in range(1, PEERS):
        pl.semaphore_signal(barrier, inc=1, **to_tile((me + d) % PEERS))
    pl.semaphore_signal(barrier, inc=1, **to_slide(partner))
    for peer in x_peers:
        pl.semaphore_signal(barrier, inc=1, **to_slide(peer * 2 + core))

    for s in range(4):
        full[s // 2, s % 2, 0:16] = gi_ref[:, s * C:(s + 1) * C].reshape(16, 8, C)
        full[2 + s // 2, s % 2, 0:16] = go_ref[s * C:(s + 1) * C, :].reshape(16, 8, C)
    for s in range(8):
        full[s // 2, s % 2, 16] = small_ref[8 * s:8 * s + 8, :] if s < 2 else jnp.zeros((8, C), jnp.float32)

    pl.semaphore_wait(barrier, PEERS + NX - 1)

    to_core = pltpu.make_async_remote_copy(
        src_ref=full.at[:, 1 - core], dst_ref=from_core, send_sem=core_send, recv_sem=core_recv, **to_slide(partner))
    to_core.start()
    row_copies = []
    for d in range(1, PEERS):
        peer = (me + d) % PEERS
        row_copies.append(pltpu.make_async_remote_copy(
            src_ref=rows_ref.at[peer], dst_ref=landed.at[me],
            send_sem=row_send.at[d - 1], recv_sem=row_recv.at[d - 1], **to_tile(peer)))
        row_copies[-1].start()
    landed[me] = rows_ref[me]
    to_core.wait()
    half[...] = full[:, core] + from_core[...]

    x_copies = []
    for d in range(1, NX):
        x_copies.append(pltpu.make_async_remote_copy(
            src_ref=half.at[x_peers[d - 1]], dst_ref=from_x.at[d - 1],
            send_sem=x_send.at[d - 1], recv_sem=x_recv.at[d - 1], **to_slide(x_peers[d - 1] * 2 + core)))
        x_copies[-1].start()
    for copy in x_copies:
        copy.wait()
    piece[...] = half[x] + from_x[0] + from_x[1] + from_x[2]

    owners = [2 * u for u in range(16)] + [1]

    def unit_copy(u):
        return pltpu.make_async_remote_copy(
            src_ref=piece.at[u], dst_ref=from_tile.at[me],
            send_sem=unit_send.at[u], recv_sem=unit_recv.at[me], **to_tile(owners[u]))

    def back_copy(u, d):
        return pltpu.make_async_remote_copy(
            src_ref=result.at[x, core, u], dst_ref=result.at[x, core, u],
            send_sem=back_send.at[d - 1], recv_sem=back_recv.at[u], **to_tile((me + d) % PEERS))

    for u in range(UNITS):
        @pl.when(me != owners[u])
        def _():
            unit_copy(u).start()
    for u in range(UNITS):
        @pl.when(me == owners[u])
        def _():
            from_tile[owners[u]] = piece[u]
            for q in range(PEERS):
                if q != owners[u]:
                    pltpu.make_async_remote_copy(
                        src_ref=piece.at[u], dst_ref=from_tile.at[q],
                        send_sem=unit_send.at[u], recv_sem=unit_recv.at[q], **to_tile(q)).wait_recv()
            result[x, core, u] = jnp.sum(from_tile[...], axis=0)
            for d in range(1, PEERS):
                back_copy(u, d).start()
    for u in range(UNITS):
        @pl.when(me != owners[u])
        def _():
            unit_copy(u).wait_send()
            back_copy(u, 1).wait_recv()

    to_partner = []

    def forward(k, where):
        to_partner.append(pltpu.make_async_remote_copy(
            src_ref=result.at[where, core], dst_ref=result.at[where, core],
            send_sem=core_back_send.at[k], recv_sem=core_back_recv.at[k], **to_slide(partner)))
        to_partner[-1].start()

    x_back = []
    for d in range(1, NX):
        x_back.append(pltpu.make_async_remote_copy(
            src_ref=result.at[x, core], dst_ref=result.at[x, core],
            send_sem=x_back_send.at[d - 1], recv_sem=x_back_recv.at[d - 1], **to_slide(x_peers[d - 1] * 2 + core)))
        x_back[-1].start()
    forward(0, x)
    for copy in row_copies:
        copy.wait()
    for j in range(WORK):
        embed_ref[j:j + 1, :] = landed[where_ref[j], pl.ds(where_ref[WORK + j], 1), :]
    for d in range(1, NX):
        x_back[d - 1].wait_recv()
        forward(d, (x + NX - d) % NX)
    for copy in x_back:
        copy.wait_send()
    for u in range(UNITS):
        @pl.when(me == owners[u])
        def _():
            for d in range(1, PEERS):
                back_copy(u, d).wait_send()
    for copy in to_partner:
        copy.wait()

    for s in range(4):
        gi_out[:, s * C:(s + 1) * C] = result[s // 2, s % 2, 0:16].reshape(C, C)
        go_out[s * C:(s + 1) * C, :] = result[2 + s // 2, s % 2, 0:16].reshape(C, C)
    gk_ref[0:8, :] = result[0, 0, 16]
    gk_ref[8:9, :] = result[0, 1, 16, 0:1]
    gg_ref[...] = result[0, 1, 16, 1:2]


def reduce(where, rows, go, gi, small):
    dma = pltpu.SemaphoreType.DMA
    f32 = jnp.float32
    vmem = pl.BlockSpec(memory_space=pltpu.VMEM)
    return pl.pallas_call(
        reduce_kernel,
        in_specs=[pl.BlockSpec(memory_space=pltpu.SMEM)] + [vmem] * 4,
        out_specs=[vmem] * 5,
        out_shape=[
            jax.ShapeDtypeStruct((WORK, C), f32),
            jax.ShapeDtypeStruct((9, C), f32),
            jax.ShapeDtypeStruct((1, C), f32),
            jax.ShapeDtypeStruct((C, HID), f32),
            jax.ShapeDtypeStruct((HID, C), f32),
        ],
        scratch_shapes=[
            pltpu.VMEM((NX, 2, UNITS, 8, C), f32),
            pltpu.VMEM((NX, 2, UNITS, 8, C), f32),
            pltpu.VMEM((NX, UNITS, 8, C), f32),
            pltpu.VMEM((NX, UNITS, 8, C), f32),
            pltpu.VMEM((NX - 1, UNITS, 8, C), f32),
            pltpu.VMEM((UNITS, 8, C), f32),
            pltpu.VMEM((PEERS, 8, C), f32),
            pltpu.VMEM((PEERS, 2, C), f32),
            dma((PEERS - 1,)), dma((PEERS - 1,)), dma, dma, dma((NX - 1,)), dma((NX - 1,)),
            dma((UNITS,)), dma((PEERS,)), dma((PEERS - 1,)), dma((UNITS,)),
            dma((NX - 1,)), dma((NX - 1,)), dma((NX,)), dma((NX,)),
        ],
        compiler_params=pltpu.CompilerParams(
            collective_id=1, has_side_effects=True, vmem_limit_bytes=32 << 20),
        name="reduce",
    )(where, rows, go, gi, small)


def local(features, tissue_count, neighbors, worker_perm, rotation, kernel, gain, w_in, w_out, cotangent):
    feat = features[0]
    strips, rows = exchange(tissue_count, feat, cotangent[0])
    counts = rows[:, WORK, 0].astype(jnp.int32)
    send, go, gi, small, where = compute(
        neighbors.reshape(-1), counts, worker_perm[0], rotation, feat, strips, rows,
        kernel, gain[None], w_in, w_in.T, w_out)
    embed, grad_kernel, grad_gain, grad_in, grad_out = reduce(where, send, go, gi, small)
    return embed[None], grad_kernel, grad_gain[0], grad_in, grad_out


def solution(mesh):
    placed = (
        P("slide", "tile", None, None, None),
        P("slide", "tile"),
        P("slide", "tile", None),
        P("slide", None),
        P("slide"),
        P(),
        P(),
        P(),
        P(),
        P("slide", "tile", None),
    )
    return jax.shard_map(
        local,
        mesh=mesh,
        in_specs=placed,
        out_specs=(P("slide", "tile", None), P(), P(), P(), P()),
        check_vma=False,
    )
```

```python
import functools

import jax
import jax.numpy as jnp
from jax import lax
from jax.experimental import pallas as pl
from jax.experimental.pallas import tpu as pltpu
from jax.sharding import PartitionSpec as P

C = 128
HID = 512
S = 16
W = S + 2
G = 8
ROWS = 16
SLOTS = 64
WORK = 32
PEERS = 32
NZ, NY = 8, 4
NX = 4
GROUP_TOTAL = PEERS * WORK
PARTS = 4
MESH = pl.DeviceIdType.MESH
HIGHEST = lax.Precision.HIGHEST


def to_tile(index):
    return dict(device_id={"tile": index}, device_id_type=MESH)


def to_slide(index):
    return dict(device_id={"slide": index}, device_id_type=MESH)


def exchange_kernel(count_ref, feat_ref, cot_ref, strips_ref, rows_ref, mine, block, wide, keep_sem,
                    send_l, recv_l, send_r, recv_r, send_z, recv_z, send_y, recv_y, row_sem):
    me = lax.axis_index("tile")
    y, z = me // NZ, me % NZ
    right, left = (me + 1) % PEERS, (me + PEERS - 1) % PEERS
    z_peers = [y * NZ + (z + d) % NZ for d in range(1, NZ)]
    y_peers = [((y + d) % NY) * NZ + z for d in range(1, NY)]

    barrier = pltpu.get_barrier_semaphore()
    for peer in z_peers + y_peers + [right, left]:
        pl.semaphore_signal(barrier, inc=1, **to_tile(peer))
    pl.semaphore_wait(barrier, NZ + NY)

    block[0:WORK, :] = cot_ref[...]
    block[WORK:, :] = jnp.full((8, C), count_ref[0, 0].astype(jnp.float32), jnp.float32)
    own_rows = pltpu.make_async_copy(block, rows_ref.at[me], row_sem)
    own_rows.start()
    z_copies = []
    for d in range(1, NZ):
        z_copies.append(pltpu.make_async_remote_copy(
            src_ref=block, dst_ref=rows_ref.at[me], send_sem=send_z.at[d - 1], recv_sem=recv_z.at[d - 1],
            **to_tile(z_peers[d - 1])))
        z_copies[-1].start()

    copies = []
    per = SLOTS // PARTS
    for part in range(PARTS):
        def one(i, _):
            t = part * per + i
            mine[t, 0] = feat_ref[t, 0]
            mine[t, 1] = feat_ref[t, S - 1]
            for row in range(S):
                wide[pl.ds(row * S, S), :] = feat_ref[t, row].astype(jnp.float32)
            mine[t, 2] = wide[pl.ds(0, S, stride=S), :].astype(jnp.bfloat16)
            mine[t, 3] = wide[pl.ds(S - 1, S, stride=S), :].astype(jnp.bfloat16)
            return 0

        lax.fori_loop(0, per, one, 0)
        span = pl.ds(part * per, per)
        keep = pltpu.make_async_copy(mine.at[span], strips_ref.at[pl.ds(SLOTS + part * per, per)], keep_sem.at[part])
        to_right = pltpu.make_async_remote_copy(
            src_ref=mine.at[span], dst_ref=strips_ref.at[span],
            send_sem=send_r.at[part], recv_sem=recv_r.at[part], **to_tile(right))
        to_left = pltpu.make_async_remote_copy(
            src_ref=mine.at[span], dst_ref=strips_ref.at[pl.ds(2 * SLOTS + part * per, per)],
            send_sem=send_l.at[part], recv_sem=recv_l.at[part], **to_tile(left))
        for copy in (keep, to_right, to_left):
            copy.start()
            copies.append(copy)

    own_rows.wait()
    for copy in z_copies:
        copy.wait_recv()
    y_copies = []
    slab = rows_ref.at[pl.ds(y * NZ, NZ)]
    for d in range(1, NY):
        y_copies.append(pltpu.make_async_remote_copy(
            src_ref=slab, dst_ref=slab, send_sem=send_y.at[d - 1], recv_sem=recv_y.at[d - 1],
            **to_tile(y_peers[d - 1])))
        y_copies[-1].start()
    for copy in z_copies:
        copy.wait_send()
    for copy in y_copies + copies:
        copy.wait()


def exchange(count, feat, cot):
    dma = pltpu.SemaphoreType.DMA
    return pl.pallas_call(
        exchange_kernel,
        in_specs=[
            pl.BlockSpec(memory_space=pltpu.SMEM),
            pl.BlockSpec(memory_space=pltpu.VMEM),
            pl.BlockSpec(memory_space=pltpu.VMEM),
        ],
        out_specs=[pl.BlockSpec(memory_space=pl.ANY)] * 2,
        out_shape=[
            jax.ShapeDtypeStruct((3 * SLOTS, 4, S, C), jnp.bfloat16),
            jax.ShapeDtypeStruct((PEERS, WORK + 8, C), jnp.float32),
        ],
        scratch_shapes=[
            pltpu.VMEM((SLOTS, 4, S, C), jnp.bfloat16),
            pltpu.VMEM((WORK + 8, C), jnp.float32),
            pltpu.VMEM((S * S, C), jnp.float32),
            dma((PARTS,)), dma((PARTS,)), dma((PARTS,)), dma((PARTS,)), dma((PARTS,)),
            dma((NZ - 1,)), dma((NZ - 1,)), dma((NY - 1,)), dma((NY - 1,)), dma,
        ],
        compiler_params=pltpu.CompilerParams(
            collective_id=0, has_side_effects=True, vmem_limit_bytes=32 << 20),
        name="exchange",
    )(count, feat, cot)


def compute_kernel(nb_ref, counts_ref, perm_ref, turn_ref, feat_ref, strips_ref, rows_ref, taps_ref, gain_ref,
                   w_in_ref, w_out_ref, send_ref, go_ref, gi_ref, small_ref, where_ref,
                   pad, ge, ga, act, cen, gk, gg, taps):
    g = pl.program_id(0)
    me = lax.axis_index("tile")
    count = counts_ref[me]
    turn = turn_ref[0]
    base = (me - 1) * SLOTS

    def start_of(owner):
        return lax.fori_loop(0, owner, lambda q, s: s + counts_ref[q], jnp.int32(0))

    @pl.when(g == 0)
    def _():
        gk[...] = jnp.zeros_like(gk)
        gg[...] = jnp.zeros_like(gg)
        gi_ref[...] = jnp.zeros_like(gi_ref)
        act[...] = jnp.zeros_like(act)
        cen[...] = jnp.zeros_like(cen)
        ge[...] = jnp.zeros_like(ge)
        for k in range(9):
            taps[k] = jnp.broadcast_to(taps_ref[k:k + 1, :].astype(jnp.float32), (G, C))
        first = start_of(me) + turn

        def row(i, _):
            rank = (first + i) & (GROUP_TOTAL - 1)
            worker = perm_ref[rank & (PEERS - 1)]
            ge[pl.ds(i, 1), :] = rows_ref[worker, pl.ds(rank >> 5, 1), :] * (1.0 / (S * S))
            return 0

        lax.fori_loop(0, count, row, 0)
        ga[...] = lax.dot_general(ge[...], w_out_ref[...].astype(jnp.float32), (((1,), (1,)), ((), ())),
                                  precision=HIGHEST, preferred_element_type=jnp.float32)

    @pl.when(g * G < count)
    def _():
        for t in range(G):
            for y in range(S):
                pad[pl.ds(((y + 1) * W + 1) * G + t, S, stride=G), :] = feat_ref[t, y].astype(jnp.float32)

            def strip(k, which):
                n = nb_ref[k, g * G + t]
                ok = n >= 0
                x = strips_ref[jnp.where(ok, n - base, 0), which].astype(jnp.float32)
                return jnp.where(ok, x, 0.0)

            pad[pl.ds(1 * G + t, S, stride=G), :] = strip(0, 1)
            pad[pl.ds(((S + 1) * W + 1) * G + t, S, stride=G), :] = strip(1, 0)
            pad[pl.ds(W * G + t, S, stride=G * W), :] = strip(2, 3)
            pad[pl.ds((W + S + 1) * G + t, S, stride=G * W), :] = strip(3, 2)
            pad[pl.ds(t, 1), :] = strip(4, 1)[S - 1:S]
            pad[pl.ds((S + 1) * G + t, 1), :] = strip(5, 1)[0:1]
            pad[pl.ds((S + 1) * W * G + t, 1), :] = strip(6, 0)[S - 1:S]
            pad[pl.ds(((S + 1) * W + S + 1) * G + t, 1), :] = strip(7, 0)[0:1]

        gain = gain_ref[...]
        mine = pl.ds(pl.multiple_of(g * G, G), G)
        slope_scale = ga[mine, :]
        n = ROWS * S * G

        def window(y, a, b):
            rows = [pad[pl.ds(((y + r + a) * W + b) * G, S * G), :] for r in range(ROWS)]
            return jnp.concatenate(rows, axis=0).reshape(ROWS * S, G, C)

        sub = lax.broadcasted_iota(jnp.int32, (G, n), 0)
        col = lax.broadcasted_iota(jnp.int32, (G, n), 1)
        select = jnp.where((col & (G - 1)) == sub, 1.0, 0.0).astype(jnp.bfloat16)

        def chunk(c, carry):
            act_sum, centre = carry
            y = c * ROWS
            depth = None
            for a in range(3):
                for b in range(3):
                    x = window(y, a, b)
                    if a == 1 and b == 1:
                        centre = centre + jnp.sum(x, axis=0)
                    term = x * taps[3 * a + b][None]
                    depth = term if depth is None else depth + term
            depth = depth.reshape(n, C)
            centered = depth - jnp.mean(depth, axis=1, keepdims=True)
            inverse = lax.rsqrt(jnp.mean(centered * centered, axis=1, keepdims=True) + 1e-06)
            unit = centered * inverse
            normed = (unit * gain).astype(jnp.bfloat16)
            acts, grads = [], []
            half = HID // 2
            for h in range(0, HID, half):
                v = jnp.dot(normed, w_in_ref[:, h:h + half], preferred_element_type=jnp.float32)
                share = 0.5 * (1.0 + lax.erf(v * 0.7071067811865476))
                slope = share + v * (jnp.exp(-0.5 * v * v) * 0.3989422804014327)
                acts.append((v * share).astype(jnp.bfloat16))
                scaled = slope.reshape(ROWS * S, G, half) * slope_scale[None, :, h:h + half]
                grads.append(scaled.reshape(n, half).astype(jnp.bfloat16))
            act_sum = act_sum + jnp.dot(select, jnp.concatenate(acts, axis=1), preferred_element_type=jnp.float32)
            grad_before = jnp.concatenate(grads, axis=1)
            gi_ref[...] += lax.dot_general(normed, grad_before, (((0,), (0,)), ((), ())),
                                           preferred_element_type=jnp.float32)
            grad_normed = lax.dot_general(grad_before, w_in_ref[...], (((1,), (1,)), ((), ())),
                                          preferred_element_type=jnp.float32)
            product = grad_normed * unit
            gg[...] += jnp.sum(product.reshape(ROWS * S, G, C), axis=0)
            grad_unit = grad_normed * gain
            grad_depth = inverse * (
                grad_unit
                - jnp.mean(grad_unit, axis=1, keepdims=True)
                - unit * jnp.mean(product * gain, axis=1, keepdims=True)
            )
            grad_depth = grad_depth.reshape(ROWS * S, G, C)
            for a in range(3):
                for b in range(3):
                    gk[3 * a + b] += jnp.sum(grad_depth * window(y, a, b), axis=0)
            return act_sum, centre

        act_sum, centre = lax.fori_loop(
            0, S // ROWS, chunk, (jnp.zeros((G, HID), jnp.float32), jnp.zeros((G, C), jnp.float32)))
        act[mine, :] = act_sum
        cen[mine, :] = centre

    @pl.when(g == pl.num_programs(0) - 1)
    def _():
        go_ref[...] = lax.dot_general(act[...], ge[...], (((0,), (0,)), ((), ())),
                                      precision=HIGHEST, preferred_element_type=jnp.float32)
        embed = jnp.dot(act[...], w_out_ref[...].astype(jnp.float32), precision=HIGHEST,
                        preferred_element_type=jnp.float32)
        cen[...] = (cen[...] + embed) * (1.0 / (S * S))
        small_ref[...] = jnp.zeros_like(small_ref)
        for k in range(9):
            small_ref[k:k + 1, :] = jnp.sum(gk[k], axis=0, keepdims=True)
        small_ref[9:10, :] = jnp.sum(gg[...], axis=0, keepdims=True)
        send_ref[...] = jnp.zeros_like(send_ref)
        first = start_of(me) + turn

        def out_row(i, _):
            rank = (first + i) & (GROUP_TOTAL - 1)
            worker = perm_ref[rank & (PEERS - 1)]
            send_ref[worker, pl.ds(i >> 5, 1), :] = cen[pl.ds(i, 1), :]
            return 0

        lax.fori_loop(0, count, out_row, 0)
        residue = lax.fori_loop(0, PEERS, lambda r, s: jnp.where(perm_ref[r] == me, r, s), jnp.int32(0))

        def arrival(owner, start):
            slot = (residue - start - turn) & (PEERS - 1)
            for k in range(2):
                @pl.when(slot + k * PEERS < counts_ref[owner])
                def _():
                    place = ((start + slot + k * PEERS + turn) & (GROUP_TOTAL - 1)) >> 5
                    where_ref[place] = owner
                    where_ref[WORK + place] = k
            return start + counts_ref[owner]

        lax.fori_loop(0, PEERS, arrival, jnp.int32(0))


def compute(nb, counts, perm, turn, feat, strips, rows, taps, gain, w_in, w_out):
    const = lambda x: pl.BlockSpec(x.shape, lambda g, *_: (0,) * x.ndim)
    outs = [
        jax.ShapeDtypeStruct((PEERS, 2, C), jnp.float32),
        jax.ShapeDtypeStruct((HID, C), jnp.float32),
        jax.ShapeDtypeStruct((C, HID), jnp.float32),
        jax.ShapeDtypeStruct((16, C), jnp.float32),
    ]
    grid_spec = pltpu.PrefetchScalarGridSpec(
        num_scalar_prefetch=4,
        grid=(SLOTS // G,),
        in_specs=[pl.BlockSpec((G, S, S, C), lambda g, *_: (g, 0, 0, 0))]
        + [const(x) for x in (strips, rows, taps, gain, w_in, w_out)],
        out_specs=[const(x) for x in outs] + [pl.BlockSpec(memory_space=pltpu.SMEM)],
        scratch_shapes=[
            pltpu.VMEM((W * W * G, C), jnp.float32),
            pltpu.VMEM((SLOTS, C), jnp.float32),
            pltpu.VMEM((SLOTS, HID), jnp.float32),
            pltpu.VMEM((SLOTS, HID), jnp.float32),
            pltpu.VMEM((SLOTS, C), jnp.float32),
            pltpu.VMEM((9, G, C), jnp.float32),
            pltpu.VMEM((G, C), jnp.float32),
            pltpu.VMEM((9, G, C), jnp.float32),
        ],
    )
    return pl.pallas_call(
        compute_kernel,
        grid_spec=grid_spec,
        out_shape=outs + [jax.ShapeDtypeStruct((2 * WORK,), jnp.int32)],
        compiler_params=pltpu.CompilerParams(vmem_limit_bytes=48 << 20),
        name="compute",
    )(nb, counts, perm, turn, feat, strips, rows, taps, gain, w_in, w_out)


UNITS = 17


def reduce_kernel(where_ref, rows_ref, go_ref, gi_ref, small_ref, embed_ref, gk_ref, gg_ref, gi_out, go_out,
                  full, result, from_core, half, from_x, piece, from_tile, landed,
                  row_send, row_recv, core_send, core_recv, x_send, x_recv, unit_send, unit_recv,
                  back_send, back_recv, x_back_send, x_back_recv, core_back_send, core_back_recv):
    me = lax.axis_index("tile")
    slide = lax.axis_index("slide")
    x, core = slide // 2, slide % 2
    partner = x * 2 + (1 - core)
    x_peers = [((x + d) % NX) for d in range(1, NX)]

    barrier = pltpu.get_barrier_semaphore()
    for d in range(1, PEERS):
        pl.semaphore_signal(barrier, inc=1, **to_tile((me + d) % PEERS))
    pl.semaphore_signal(barrier, inc=1, **to_slide(partner))
    for peer in x_peers:
        pl.semaphore_signal(barrier, inc=1, **to_slide(peer * 2 + core))

    for s in range(4):
        full[s // 2, s % 2, 0:16] = gi_ref[:, s * C:(s + 1) * C].reshape(16, 8, C)
        full[2 + s // 2, s % 2, 0:16] = go_ref[s * C:(s + 1) * C, :].reshape(16, 8, C)
    for s in range(8):
        full[s // 2, s % 2, 16] = small_ref[8 * s:8 * s + 8, :] if s < 2 else jnp.zeros((8, C), jnp.float32)

    pl.semaphore_wait(barrier, PEERS + NX - 1)

    to_core = pltpu.make_async_remote_copy(
        src_ref=full.at[:, 1 - core], dst_ref=from_core, send_sem=core_send, recv_sem=core_recv, **to_slide(partner))
    to_core.start()
    row_copies = []
    for d in range(1, PEERS):
        peer = (me + d) % PEERS
        row_copies.append(pltpu.make_async_remote_copy(
            src_ref=rows_ref.at[peer], dst_ref=landed.at[me],
            send_sem=row_send.at[d - 1], recv_sem=row_recv.at[d - 1], **to_tile(peer)))
        row_copies[-1].start()
    landed[me] = rows_ref[me]
    to_core.wait()
    half[...] = full[:, core] + from_core[...]

    x_copies = []
    for d in range(1, NX):
        x_copies.append(pltpu.make_async_remote_copy(
            src_ref=half.at[x_peers[d - 1]], dst_ref=from_x.at[d - 1],
            send_sem=x_send.at[d - 1], recv_sem=x_recv.at[d - 1], **to_slide(x_peers[d - 1] * 2 + core)))
        x_copies[-1].start()
    for copy in x_copies:
        copy.wait()
    piece[...] = half[x] + from_x[0] + from_x[1] + from_x[2]

    owners = [2 * u for u in range(16)] + [1]

    def unit_copy(u):
        return pltpu.make_async_remote_copy(
            src_ref=piece.at[u], dst_ref=from_tile.at[me],
            send_sem=unit_send.at[u], recv_sem=unit_recv.at[me], **to_tile(owners[u]))

    def back_copy(u, d):
        return pltpu.make_async_remote_copy(
            src_ref=result.at[x, core, u], dst_ref=result.at[x, core, u],
            send_sem=back_send.at[d - 1], recv_sem=back_recv.at[u], **to_tile((me + d) % PEERS))

    for u in range(UNITS):
        @pl.when(me != owners[u])
        def _():
            unit_copy(u).start()
    for u in range(UNITS):
        @pl.when(me == owners[u])
        def _():
            from_tile[owners[u]] = piece[u]
            for q in range(PEERS):
                if q != owners[u]:
                    pltpu.make_async_remote_copy(
                        src_ref=piece.at[u], dst_ref=from_tile.at[q],
                        send_sem=unit_send.at[u], recv_sem=unit_recv.at[q], **to_tile(q)).wait_recv()
            result[x, core, u] = jnp.sum(from_tile[...], axis=0)
            for d in range(1, PEERS):
                back_copy(u, d).start()
    for u in range(UNITS):
        @pl.when(me != owners[u])
        def _():
            unit_copy(u).wait_send()
            back_copy(u, 1).wait_recv()

    to_partner = []

    def forward(k, where):
        to_partner.append(pltpu.make_async_remote_copy(
            src_ref=result.at[where, core], dst_ref=result.at[where, core],
            send_sem=core_back_send.at[k], recv_sem=core_back_recv.at[k], **to_slide(partner)))
        to_partner[-1].start()

    x_back = []
    for d in range(1, NX):
        x_back.append(pltpu.make_async_remote_copy(
            src_ref=result.at[x, core], dst_ref=result.at[x, core],
            send_sem=x_back_send.at[d - 1], recv_sem=x_back_recv.at[d - 1], **to_slide(x_peers[d - 1] * 2 + core)))
        x_back[-1].start()
    forward(0, x)
    for copy in row_copies:
        copy.wait()
    for j in range(WORK):
        embed_ref[j:j + 1, :] = landed[where_ref[j], pl.ds(where_ref[WORK + j], 1), :]
    for d in range(1, NX):
        x_back[d - 1].wait_recv()
        forward(d, (x + NX - d) % NX)
    for copy in x_back:
        copy.wait_send()
    for u in range(UNITS):
        @pl.when(me == owners[u])
        def _():
            for d in range(1, PEERS):
                back_copy(u, d).wait_send()
    for copy in to_partner:
        copy.wait()

    for s in range(4):
        gi_out[:, s * C:(s + 1) * C] = result[s // 2, s % 2, 0:16].reshape(C, C)
        go_out[s * C:(s + 1) * C, :] = result[2 + s // 2, s % 2, 0:16].reshape(C, C)
    gk_ref[0:8, :] = result[0, 0, 16]
    gk_ref[8:9, :] = result[0, 1, 16, 0:1]
    gg_ref[...] = result[0, 1, 16, 1:2]


def reduce(where, rows, go, gi, small):
    dma = pltpu.SemaphoreType.DMA
    f32 = jnp.float32
    vmem = pl.BlockSpec(memory_space=pltpu.VMEM)
    return pl.pallas_call(
        reduce_kernel,
        in_specs=[pl.BlockSpec(memory_space=pltpu.SMEM)] + [vmem] * 4,
        out_specs=[vmem] * 5,
        out_shape=[
            jax.ShapeDtypeStruct((WORK, C), f32),
            jax.ShapeDtypeStruct((9, C), f32),
            jax.ShapeDtypeStruct((1, C), f32),
            jax.ShapeDtypeStruct((C, HID), f32),
            jax.ShapeDtypeStruct((HID, C), f32),
        ],
        scratch_shapes=[
            pltpu.VMEM((NX, 2, UNITS, 8, C), f32),
            pltpu.VMEM((NX, 2, UNITS, 8, C), f32),
            pltpu.VMEM((NX, UNITS, 8, C), f32),
            pltpu.VMEM((NX, UNITS, 8, C), f32),
            pltpu.VMEM((NX - 1, UNITS, 8, C), f32),
            pltpu.VMEM((UNITS, 8, C), f32),
            pltpu.VMEM((PEERS, 8, C), f32),
            pltpu.VMEM((PEERS, 2, C), f32),
            dma((PEERS - 1,)), dma((PEERS - 1,)), dma, dma, dma((NX - 1,)), dma((NX - 1,)),
            dma((UNITS,)), dma((PEERS,)), dma((PEERS - 1,)), dma((UNITS,)),
            dma((NX - 1,)), dma((NX - 1,)), dma((NX,)), dma((NX,)),
        ],
        compiler_params=pltpu.CompilerParams(
            collective_id=1, has_side_effects=True, vmem_limit_bytes=32 << 20),
        name="reduce",
    )(where, rows, go, gi, small)


def local(features, tissue_count, neighbors, worker_perm, rotation, kernel, gain, w_in, w_out, cotangent):
    feat = features[0]
    strips, rows = exchange(tissue_count, feat, cotangent[0])
    counts = rows[:, WORK, 0].astype(jnp.int32)
    send, go, gi, small, where = compute(
        neighbors[0].T, counts, worker_perm[0], rotation, feat, strips, rows,
        kernel, gain[None], w_in, w_out)
    embed, grad_kernel, grad_gain, grad_in, grad_out = reduce(where, send, go, gi, small)
    return embed[None], grad_kernel, grad_gain[0], grad_in, grad_out


def solution(mesh):
    placed = (
        P("slide", "tile", None, None, None),
        P("slide", "tile"),
        P("slide", "tile", None),
        P("slide", None),
        P("slide"),
        P(),
        P(),
        P(),
        P(),
        P("slide", "tile", None),
    )
    return jax.shard_map(
        local,
        mesh=mesh,
        in_specs=placed,
        out_specs=(P("slide", "tile", None), P(), P(), P(), P()),
        check_vma=False,
    )
```

```python
import functools

import jax
import jax.numpy as jnp
from jax import lax
from jax.experimental import pallas as pl
from jax.experimental.pallas import tpu as pltpu
from jax.sharding import PartitionSpec as P

C = 128
HID = 512
S = 16
W = S + 2
G = 8
SLOTS = 64
WORK = 32
PEERS = 32
NZ, NY = 8, 4
NX = 4
GROUP_TOTAL = PEERS * WORK
MESH = pl.DeviceIdType.MESH
HIGHEST = lax.Precision.HIGHEST


def to_tile(index):
    return dict(device_id={"tile": index}, device_id_type=MESH)


def to_slide(index):
    return dict(device_id={"slide": index}, device_id_type=MESH)


def exchange_kernel(count_ref, feat_ref, cot_ref, strips_ref, rows_ref, block, wide,
                    send_z, recv_z, send_y, recv_y, row_sem):
    me = lax.axis_index("tile")
    y, z = me // NZ, me % NZ
    z_peers = [y * NZ + (z + d) % NZ for d in range(1, NZ)]
    y_peers = [((y + d) % NY) * NZ + z for d in range(1, NY)]

    barrier = pltpu.get_barrier_semaphore()
    for peer in z_peers + y_peers:
        pl.semaphore_signal(barrier, inc=1, **to_tile(peer))
    block[0:WORK, :] = cot_ref[...]
    block[WORK:, :] = jnp.full((8, C), count_ref[0, 0].astype(jnp.float32), jnp.float32)
    own_rows = pltpu.make_async_copy(block, rows_ref.at[me], row_sem)
    own_rows.start()
    pl.semaphore_wait(barrier, NZ + NY - 2)

    z_copies = []
    for d in range(1, NZ):
        z_copies.append(pltpu.make_async_remote_copy(
            src_ref=block, dst_ref=rows_ref.at[me], send_sem=send_z.at[d - 1], recv_sem=recv_z.at[d - 1],
            **to_tile(z_peers[d - 1])))
        z_copies[-1].start()

    def one(t, _):
        strips_ref[t, 0] = feat_ref[t, 0]
        strips_ref[t, 1] = feat_ref[t, S - 1]
        for row in range(S):
            wide[pl.ds(row * S, S), :] = feat_ref[t, row].astype(jnp.float32)
        strips_ref[t, 2] = wide[pl.ds(0, S, stride=S), :].astype(jnp.bfloat16)
        strips_ref[t, 3] = wide[pl.ds(S - 1, S, stride=S), :].astype(jnp.bfloat16)
        return 0

    lax.fori_loop(0, SLOTS // 2, one, 0)
    own_rows.wait()
    for copy in z_copies:
        copy.wait_recv()
    y_copies = []
    slab = rows_ref.at[pl.ds(y * NZ, NZ)]
    for d in range(1, NY):
        y_copies.append(pltpu.make_async_remote_copy(
            src_ref=slab, dst_ref=slab, send_sem=send_y.at[d - 1], recv_sem=recv_y.at[d - 1],
            **to_tile(y_peers[d - 1])))
        y_copies[-1].start()
    lax.fori_loop(SLOTS // 2, SLOTS, one, 0)
    for copy in z_copies:
        copy.wait_send()
    for copy in y_copies:
        copy.wait()


def exchange(count, feat, cot):
    dma = pltpu.SemaphoreType.DMA
    vmem = pl.BlockSpec(memory_space=pltpu.VMEM)
    return pl.pallas_call(
        exchange_kernel,
        in_specs=[pl.BlockSpec(memory_space=pltpu.SMEM), vmem, vmem],
        out_specs=[vmem, pl.BlockSpec(memory_space=pl.ANY)],
        out_shape=[
            jax.ShapeDtypeStruct((SLOTS, 4, S, C), jnp.bfloat16),
            jax.ShapeDtypeStruct((PEERS, WORK + 8, C), jnp.float32),
        ],
        scratch_shapes=[
            pltpu.VMEM((WORK + 8, C), jnp.float32),
            pltpu.VMEM((S * S, C), jnp.float32),
            dma((NZ - 1,)), dma((NZ - 1,)), dma((NY - 1,)), dma((NY - 1,)), dma,
        ],
        compiler_params=pltpu.CompilerParams(
            collective_id=0, has_side_effects=True, vmem_limit_bytes=32 << 20),
        name="exchange",
    )(count, feat, cot)


def start_of(counts_ref, owner):
    return lax.fori_loop(0, owner, lambda q, s: s + counts_ref[q], jnp.int32(0))


def fill_centre(pad, feat_ref, t, u):
    for y in range(S):
        pad[pl.ds(((y + 1) * W + 1) * G + t, S, stride=G), :] = feat_ref[u, y].astype(jnp.float32)


def pixel_math(window, pixels, slope_scale, taps, gain, w_in_ref, gi_ref, gk, gg):
    n = pixels * G
    depth, centre = None, None
    for a in range(3):
        for b in range(3):
            x = window(a, b)
            if a == 1 and b == 1:
                centre = jnp.sum(x, axis=0)
            term = x * taps[3 * a + b][None]
            depth = term if depth is None else depth + term
    depth = depth.reshape(n, C)
    centered = depth - jnp.mean(depth, axis=1, keepdims=True)
    inverse = lax.rsqrt(jnp.mean(centered * centered, axis=1, keepdims=True) + 1e-06)
    unit = centered * inverse
    normed = (unit * gain).astype(jnp.bfloat16)
    acts, grads = [], []
    half = HID // 2
    for h in range(0, HID, half):
        v = jnp.dot(normed, w_in_ref[:, h:h + half], preferred_element_type=jnp.float32)
        share = 0.5 * (1.0 + lax.erf(v * 0.7071067811865476))
        slope = share + v * (jnp.exp(-0.5 * v * v) * 0.3989422804014327)
        acts.append((v * share).astype(jnp.bfloat16))
        scaled = slope.reshape(pixels, G, half) * slope_scale[None, :, h:h + half]
        grads.append(scaled.reshape(n, half).astype(jnp.bfloat16))
    sub = lax.broadcasted_iota(jnp.int32, (G, n), 0)
    col = lax.broadcasted_iota(jnp.int32, (G, n), 1)
    select = jnp.where((col & (G - 1)) == sub, 1.0, 0.0).astype(jnp.bfloat16)
    act_sum = jnp.dot(select, jnp.concatenate(acts, axis=1), preferred_element_type=jnp.float32)
    grad_before = jnp.concatenate(grads, axis=1)
    gi_ref[...] += lax.dot_general(normed, grad_before, (((0,), (0,)), ((), ())), preferred_element_type=jnp.float32)
    grad_normed = lax.dot_general(grad_before, w_in_ref[...], (((1,), (1,)), ((), ())),
                                  preferred_element_type=jnp.float32)
    product = grad_normed * unit
    gg[...] += jnp.sum(product.reshape(pixels, G, C), axis=0)
    grad_unit = grad_normed * gain
    grad_depth = inverse * (
        grad_unit
        - jnp.mean(grad_unit, axis=1, keepdims=True)
        - unit * jnp.mean(product * gain, axis=1, keepdims=True)
    )
    grad_depth = grad_depth.reshape(pixels, G, C)
    for a in range(3):
        for b in range(3):
            gk[3 * a + b] += jnp.sum(grad_depth * window(a, b), axis=0)
    return act_sum, centre


def inner_kernel(counts_ref, perm_ref, turn_ref, feat_ref, rows_ref, taps_ref, gain_ref, w_in_ref, w_out_ref,
                 ge, ga, act, cen, gi_ref, gk, gg, taps, pad):
    g = pl.program_id(0)
    me = lax.axis_index("tile")
    count = counts_ref[me]

    @pl.when(g == 0)
    def _():
        for ref in (gk, gg, gi_ref, act, cen, ge):
            ref[...] = jnp.zeros_like(ref)
        for k in range(9):
            taps[k] = jnp.broadcast_to(taps_ref[k:k + 1, :].astype(jnp.float32), (G, C))
        first = start_of(counts_ref, me) + turn_ref[0]

        def row(i, _):
            rank = (first + i) & (GROUP_TOTAL - 1)
            worker = perm_ref[rank & (PEERS - 1)]
            ge[pl.ds(i, 1), :] = rows_ref[worker, pl.ds(rank >> 5, 1), :] * (1.0 / (S * S))
            return 0

        lax.fori_loop(0, count, row, 0)
        ga[...] = lax.dot_general(ge[...], w_out_ref[...].astype(jnp.float32), (((1,), (1,)), ((), ())),
                                  precision=HIGHEST, preferred_element_type=jnp.float32)

    @pl.when(g * G < count)
    def _():
        for t in range(G):
            fill_centre(pad, feat_ref, t, t)
        side = S - 2

        def window(a, b):
            rows = [pad[pl.ds(((y + a) * W + 1 + b) * G, side * G), :] for y in range(1, S - 1)]
            return jnp.concatenate(rows, axis=0).reshape(side * side, G, C)

        mine = pl.ds(pl.multiple_of(g * G, G), G)
        act[mine, :], cen[mine, :] = pixel_math(
            window, side * side, ga[mine, :], taps, gain_ref[...], w_in_ref, gi_ref, gk, gg)


def whole(x):
    return pl.BlockSpec(x.shape, lambda g, *_: (0,) * len(x.shape))


def inner(counts, perm, turn, feat, rows, taps, gain, w_in, w_out):
    f32 = jnp.float32
    outs = [
        jax.ShapeDtypeStruct(shape, f32)
        for shape in ((SLOTS, C), (SLOTS, HID), (SLOTS, HID), (SLOTS, C), (C, HID), (9, G, C), (G, C), (9, G, C))
    ]
    grid_spec = pltpu.PrefetchScalarGridSpec(
        num_scalar_prefetch=3,
        grid=(SLOTS // G,),
        in_specs=[pl.BlockSpec((G, S, S, C), lambda g, *_: (g, 0, 0, 0))]
        + [whole(x) for x in (rows, taps, gain, w_in, w_out)],
        out_specs=[whole(x) for x in outs],
        scratch_shapes=[pltpu.VMEM((W * W * G, C), f32)],
    )
    return pl.pallas_call(
        inner_kernel,
        grid_spec=grid_spec,
        out_shape=outs,
        compiler_params=pltpu.CompilerParams(vmem_limit_bytes=40 << 20),
        cost_estimate=pl.CostEstimate(flops=10_000_000_000, bytes_accessed=100_000_000, transcendentals=0),
        name="inner",
    )(counts, perm, turn, feat, rows, taps, gain, w_in, w_out)


PAIR = 2


def border_kernel(nb_ref, counts_ref, perm_ref, turn_ref, feat_ref, left_ref, own_ref, right_ref, gain_ref, w_in_ref,
                  w_out_ref, ge, ga, act_in, cen_in, gi_in, gk_in, gg_in, taps,
                  send_ref, go_ref, gi_ref, small_ref, where_ref, pad, strips, act, cen, gk, gg, sems):
    g = pl.program_id(0)
    me = lax.axis_index("tile")
    count = counts_ref[me]
    turn = turn_ref[0]
    base = (me - 1) * SLOTS

    @pl.when(g == 0)
    def _():
        copies = [
            pltpu.make_async_copy(ref, strips.at[pl.ds(k * SLOTS, SLOTS)], sems.at[k])
            for k, ref in enumerate((left_ref, own_ref, right_ref))
        ]
        for copy in copies:
            copy.start()
        for ref, old in ((act, act_in), (cen, cen_in), (gi_ref, gi_in), (gk, gk_in), (gg, gg_in)):
            ref[...] = old[...]
        for copy in copies:
            copy.wait()

    @pl.when(g * PAIR * G < count)
    def _():
        for t in range(PAIR * G):
            pair_pad = pad.at[t // G]
            u = t % G
            fill_centre(pair_pad, feat_ref, u, t)

            def strip(k, which):
                n = nb_ref[k, g * PAIR * G + t]
                ok = n >= 0
                x = strips[jnp.where(ok, n - base, 0), which].astype(jnp.float32)
                return jnp.where(ok, x, 0.0)

            pair_pad[pl.ds(1 * G + u, S, stride=G), :] = strip(0, 1)
            pair_pad[pl.ds(((S + 1) * W + 1) * G + u, S, stride=G), :] = strip(1, 0)
            pair_pad[pl.ds(W * G + u, S, stride=G * W), :] = strip(2, 3)
            pair_pad[pl.ds((W + S + 1) * G + u, S, stride=G * W), :] = strip(3, 2)
            pair_pad[pl.ds(u, 1), :] = strip(4, 1)[S - 1:S]
            pair_pad[pl.ds((S + 1) * G + u, 1), :] = strip(5, 1)[0:1]
            pair_pad[pl.ds((S + 1) * W * G + u, 1), :] = strip(6, 0)[S - 1:S]
            pair_pad[pl.ds(((S + 1) * W + S + 1) * G + u, 1), :] = strip(7, 0)[0:1]

        for p in range(PAIR):
            def window(a, b):
                part = pad.at[p]
                rows = [part[pl.ds(((y + a) * W + b) * G, S * G), :] for y in (0, S - 1)]
                for x in (0, S - 1):
                    rows += [part[pl.ds(((y + a) * W + x + b) * G, G), :] for y in range(1, S - 1)]
                return jnp.concatenate(rows, axis=0).reshape(4 * S - 4, G, C)

            mine = pl.ds(pl.multiple_of((g * PAIR + p) * G, G), G)
            act_sum, centre = pixel_math(
                window, 4 * S - 4, ga[mine, :], taps, gain_ref[...], w_in_ref, gi_ref, gk, gg)
            act[mine, :] += act_sum
            cen[mine, :] += centre

    @pl.when(g == pl.num_programs(0) - 1)
    def _():
        go_ref[...] = lax.dot_general(act[...], ge[...], (((0,), (0,)), ((), ())),
                                      precision=HIGHEST, preferred_element_type=jnp.float32)
        embed = jnp.dot(act[...], w_out_ref[...].astype(jnp.float32), precision=HIGHEST,
                        preferred_element_type=jnp.float32)
        cen[...] = (cen[...] + embed) * (1.0 / (S * S))
        small_ref[...] = jnp.zeros_like(small_ref)
        for k in range(9):
            small_ref[k:k + 1, :] = jnp.sum(gk[k], axis=0, keepdims=True)
        small_ref[9:10, :] = jnp.sum(gg[...], axis=0, keepdims=True)
        send_ref[...] = jnp.zeros_like(send_ref)
        first = start_of(counts_ref, me) + turn

        def out_row(i, _):
            rank = (first + i) & (GROUP_TOTAL - 1)
            worker = perm_ref[rank & (PEERS - 1)]
            send_ref[worker, pl.ds(i >> 5, 1), :] = cen[pl.ds(i, 1), :]
            return 0

        lax.fori_loop(0, count, out_row, 0)
        residue = lax.fori_loop(0, PEERS, lambda r, s: jnp.where(perm_ref[r] == me, r, s), jnp.int32(0))

        def arrival(owner, start):
            slot = (residue - start - turn) & (PEERS - 1)
            for k in range(2):
                @pl.when(slot + k * PEERS < counts_ref[owner])
                def _():
                    place = ((start + slot + k * PEERS + turn) & (GROUP_TOTAL - 1)) >> 5
                    where_ref[place] = owner
                    where_ref[WORK + place] = k
            return start + counts_ref[owner]

        lax.fori_loop(0, PEERS, arrival, jnp.int32(0))


def border(nb, counts, perm, turn, feat, left, own, right, gain, w_in, w_out, sums):
    f32 = jnp.float32
    outs = [jax.ShapeDtypeStruct(shape, f32) for shape in ((PEERS, 2, C), (HID, C), (C, HID), (16, C))]
    grid_spec = pltpu.PrefetchScalarGridSpec(
        num_scalar_prefetch=4,
        grid=(SLOTS // (PAIR * G),),
        in_specs=[pl.BlockSpec((PAIR * G, S, S, C), lambda g, *_: (g, 0, 0, 0))]
        + [pl.BlockSpec(memory_space=pl.ANY)] * 3
        + [whole(x) for x in (gain, w_in, w_out, *sums)],
        out_specs=[whole(x) for x in outs] + [pl.BlockSpec(memory_space=pltpu.SMEM)],
        scratch_shapes=[
            pltpu.VMEM((PAIR, W * W * G, C), f32),
            pltpu.VMEM((3 * SLOTS, 4, S, C), jnp.bfloat16),
            pltpu.VMEM((SLOTS, HID), f32),
            pltpu.VMEM((SLOTS, C), f32),
            pltpu.VMEM((9, G, C), f32),
            pltpu.VMEM((G, C), f32),
            pltpu.SemaphoreType.DMA((3,)),
        ],
    )
    return pl.pallas_call(
        border_kernel,
        grid_spec=grid_spec,
        out_shape=outs + [jax.ShapeDtypeStruct((2 * WORK,), jnp.int32)],
        compiler_params=pltpu.CompilerParams(vmem_limit_bytes=40 << 20),
        name="border",
    )(nb, counts, perm, turn, feat, left, own, right, gain, w_in, w_out, *sums)


UNITS = 17


def reduce_kernel(where_ref, rows_ref, go_ref, gi_ref, small_ref, embed_ref, gk_ref, gg_ref, gi_out, go_out,
                  full, result, from_core, half, from_x, piece, from_tile, landed,
                  row_send, row_recv, core_send, core_recv, x_send, x_recv, unit_send, unit_recv,
                  back_send, back_recv, x_back_send, x_back_recv, core_back_send, core_back_recv):
    me = lax.axis_index("tile")
    slide = lax.axis_index("slide")
    x, core = slide // 2, slide % 2
    partner = x * 2 + (1 - core)
    x_peers = [((x + d) % NX) for d in range(1, NX)]

    barrier = pltpu.get_barrier_semaphore()
    for d in range(1, PEERS):
        pl.semaphore_signal(barrier, inc=1, **to_tile((me + d) % PEERS))
    pl.semaphore_signal(barrier, inc=1, **to_slide(partner))
    for peer in x_peers:
        pl.semaphore_signal(barrier, inc=1, **to_slide(peer * 2 + core))

    for s in range(4):
        full[s // 2, s % 2, 0:16] = gi_ref[:, s * C:(s + 1) * C].reshape(16, 8, C)
        full[2 + s // 2, s % 2, 0:16] = go_ref[s * C:(s + 1) * C, :].reshape(16, 8, C)
    for s in range(8):
        full[s // 2, s % 2, 16] = small_ref[8 * s:8 * s + 8, :] if s < 2 else jnp.zeros((8, C), jnp.float32)

    pl.semaphore_wait(barrier, PEERS + NX - 1)

    to_core = pltpu.make_async_remote_copy(
        src_ref=full.at[:, 1 - core], dst_ref=from_core, send_sem=core_send, recv_sem=core_recv, **to_slide(partner))
    to_core.start()
    row_copies = []
    for d in range(1, PEERS):
        peer = (me + d) % PEERS
        row_copies.append(pltpu.make_async_remote_copy(
            src_ref=rows_ref.at[peer], dst_ref=landed.at[me],
            send_sem=row_send.at[d - 1], recv_sem=row_recv.at[d - 1], **to_tile(peer)))
        row_copies[-1].start()
    landed[me] = rows_ref[me]
    to_core.wait()
    half[...] = full[:, core] + from_core[...]

    x_copies = []
    for d in range(1, NX):
        x_copies.append(pltpu.make_async_remote_copy(
            src_ref=half.at[x_peers[d - 1]], dst_ref=from_x.at[d - 1],
            send_sem=x_send.at[d - 1], recv_sem=x_recv.at[d - 1], **to_slide(x_peers[d - 1] * 2 + core)))
        x_copies[-1].start()
    for copy in x_copies:
        copy.wait()
    piece[...] = half[x] + from_x[0] + from_x[1] + from_x[2]

    owners = [2 * u for u in range(16)] + [1]

    def unit_copy(u):
        return pltpu.make_async_remote_copy(
            src_ref=piece.at[u], dst_ref=from_tile.at[me],
            send_sem=unit_send.at[u], recv_sem=unit_recv.at[me], **to_tile(owners[u]))

    def back_copy(u, d):
        return pltpu.make_async_remote_copy(
            src_ref=result.at[x, core, u], dst_ref=result.at[x, core, u],
            send_sem=back_send.at[d - 1], recv_sem=back_recv.at[u], **to_tile((me + d) % PEERS))

    for u in range(UNITS):
        @pl.when(me != owners[u])
        def _():
            unit_copy(u).start()
    for u in range(UNITS):
        @pl.when(me == owners[u])
        def _():
            from_tile[owners[u]] = piece[u]
            for q in range(PEERS):
                if q != owners[u]:
                    pltpu.make_async_remote_copy(
                        src_ref=piece.at[u], dst_ref=from_tile.at[q],
                        send_sem=unit_send.at[u], recv_sem=unit_recv.at[q], **to_tile(q)).wait_recv()
            result[x, core, u] = jnp.sum(from_tile[...], axis=0)
            for d in range(1, PEERS):
                back_copy(u, d).start()
    for u in range(UNITS):
        @pl.when(me != owners[u])
        def _():
            unit_copy(u).wait_send()
            back_copy(u, 1).wait_recv()

    to_partner = []

    def forward(k, where):
        to_partner.append(pltpu.make_async_remote_copy(
            src_ref=result.at[where, core], dst_ref=result.at[where, core],
            send_sem=core_back_send.at[k], recv_sem=core_back_recv.at[k], **to_slide(partner)))
        to_partner[-1].start()

    x_back = []
    for d in range(1, NX):
        x_back.append(pltpu.make_async_remote_copy(
            src_ref=result.at[x, core], dst_ref=result.at[x, core],
            send_sem=x_back_send.at[d - 1], recv_sem=x_back_recv.at[d - 1], **to_slide(x_peers[d - 1] * 2 + core)))
        x_back[-1].start()
    forward(0, x)
    for copy in row_copies:
        copy.wait()
    for j in range(WORK):
        embed_ref[j:j + 1, :] = landed[where_ref[j], pl.ds(where_ref[WORK + j], 1), :]
    for d in range(1, NX):
        x_back[d - 1].wait_recv()
        forward(d, (x + NX - d) % NX)
    for copy in x_back:
        copy.wait_send()
    for u in range(UNITS):
        @pl.when(me == owners[u])
        def _():
            for d in range(1, PEERS):
                back_copy(u, d).wait_send()
    for copy in to_partner:
        copy.wait()

    for s in range(4):
        gi_out[:, s * C:(s + 1) * C] = result[s // 2, s % 2, 0:16].reshape(C, C)
        go_out[s * C:(s + 1) * C, :] = result[2 + s // 2, s % 2, 0:16].reshape(C, C)
    gk_ref[0:8, :] = result[0, 0, 16]
    gk_ref[8:9, :] = result[0, 1, 16, 0:1]
    gg_ref[...] = result[0, 1, 16, 1:2]


def reduce(where, rows, go, gi, small):
    dma = pltpu.SemaphoreType.DMA
    f32 = jnp.float32
    vmem = pl.BlockSpec(memory_space=pltpu.VMEM)
    return pl.pallas_call(
        reduce_kernel,
        in_specs=[pl.BlockSpec(memory_space=pltpu.SMEM)] + [vmem] * 4,
        out_specs=[vmem] * 5,
        out_shape=[
            jax.ShapeDtypeStruct((WORK, C), f32),
            jax.ShapeDtypeStruct((9, C), f32),
            jax.ShapeDtypeStruct((1, C), f32),
            jax.ShapeDtypeStruct((C, HID), f32),
            jax.ShapeDtypeStruct((HID, C), f32),
        ],
        scratch_shapes=[
            pltpu.VMEM((NX, 2, UNITS, 8, C), f32),
            pltpu.VMEM((NX, 2, UNITS, 8, C), f32),
            pltpu.VMEM((NX, UNITS, 8, C), f32),
            pltpu.VMEM((NX, UNITS, 8, C), f32),
            pltpu.VMEM((NX - 1, UNITS, 8, C), f32),
            pltpu.VMEM((UNITS, 8, C), f32),
            pltpu.VMEM((PEERS, 8, C), f32),
            pltpu.VMEM((PEERS, 2, C), f32),
            dma((PEERS - 1,)), dma((PEERS - 1,)), dma, dma, dma((NX - 1,)), dma((NX - 1,)),
            dma((UNITS,)), dma((PEERS,)), dma((PEERS - 1,)), dma((UNITS,)),
            dma((NX - 1,)), dma((NX - 1,)), dma((NX,)), dma((NX,)),
        ],
        compiler_params=pltpu.CompilerParams(
            collective_id=1, has_side_effects=True, vmem_limit_bytes=32 << 20),
        name="reduce",
    )(where, rows, go, gi, small)


def local(features, tissue_count, neighbors, worker_perm, rotation, kernel, gain, w_in, w_out, cotangent):
    feat = features[0]
    strips, rows = exchange(tissue_count, feat, cotangent[0])
    peers = lax.axis_size("tile")
    left = lax.ppermute(strips, "tile", [(i, i + 1) for i in range(peers - 1)])
    right = lax.ppermute(strips, "tile", [(i + 1, i) for i in range(peers - 1)])
    counts = rows[:, WORK, 0].astype(jnp.int32)
    sums = inner(counts, worker_perm[0], rotation, feat, rows, kernel, gain[None], w_in, w_out)
    send, go, gi, small, where = border(
        neighbors[0].T, counts, worker_perm[0], rotation, feat, left, strips, right, gain[None], w_in, w_out, sums)
    embed, grad_kernel, grad_gain, grad_in, grad_out = reduce(where, send, go, gi, small)
    return embed[None], grad_kernel, grad_gain[0], grad_in, grad_out


def solution(mesh):
    placed = (
        P("slide", "tile", None, None, None),
        P("slide", "tile"),
        P("slide", "tile", None),
        P("slide", None),
        P("slide"),
        P(),
        P(),
        P(),
        P(),
        P("slide", "tile", None),
    )
    return jax.shard_map(
        local,
        mesh=mesh,
        in_specs=placed,
        out_specs=(P("slide", "tile", None), P(), P(), P(), P()),
        check_vma=False,
    )
```

```python
import functools

import jax
import jax.numpy as jnp
from jax import lax
from jax.experimental import pallas as pl
from jax.experimental.pallas import tpu as pltpu
from jax.sharding import PartitionSpec as P

C = 128
HID = 512
S = 16
W = S + 2
G = 8
SLOTS = 64
WORK = 32
PEERS = 32
NZ, NY = 8, 4
NX = 4
GROUP_TOTAL = PEERS * WORK
MESH = pl.DeviceIdType.MESH
HIGHEST = lax.Precision.HIGHEST


def to_tile(index):
    return dict(device_id={"tile": index}, device_id_type=MESH)


def to_slide(index):
    return dict(device_id={"slide": index}, device_id_type=MESH)


def exchange_kernel(count_ref, perm_ref, turn_ref, feat_hbm, cot_ref, strips_ref, rows_ref, counts_ref,
                    feat_ref, wide, own_count, count_all, count_smem, z_rows, outgoing, feat_sem,
                    count_send, count_recv, county_send, county_recv, send_z, recv_z, send_y, recv_y, smem_sem):
    me = lax.axis_index("tile")
    y, z = me // NZ, me % NZ
    z_peers = [y * NZ + (z + d) % NZ for d in range(1, NZ)]
    y_peers = [((y + d) % NY) * NZ + z for d in range(1, NY)]

    barrier = pltpu.get_barrier_semaphore()
    for peer in z_peers + y_peers:
        pl.semaphore_signal(barrier, inc=1, **to_tile(peer))
    quarter = SLOTS // 4
    feat_copies = [
        pltpu.make_async_copy(feat_hbm.at[pl.ds(q * quarter, quarter)], feat_ref.at[pl.ds(q * quarter, quarter)],
                              feat_sem.at[q])
        for q in range(4)
    ]
    for copy in feat_copies:
        copy.start()
    own_count[...] = jnp.full((1, C), count_ref[0, 0], jnp.int32)
    pl.semaphore_wait(barrier, NZ + NY - 2)

    def remote(src, dst, send, recv, d, peer):
        return pltpu.make_async_remote_copy(
            src_ref=src, dst_ref=dst, send_sem=send.at[d - 1], recv_sem=recv.at[d - 1], **to_tile(peer))

    count_z = [remote(own_count, count_all.at[y, z], count_send, count_recv, d, z_peers[d - 1]) for d in range(1, NZ)]
    rows_z = [remote(cot_ref, z_rows.at[z], send_z, recv_z, d, z_peers[d - 1]) for d in range(1, NZ)]
    for copy in count_z + rows_z:
        copy.start()
    count_all[y, z] = own_count[...]
    z_rows[z] = cot_ref[...]

    def one(t, _):
        strips_ref[t, 0] = feat_ref[t, 0]
        strips_ref[t, 1] = feat_ref[t, S - 1]
        for row in range(S):
            wide[pl.ds(row * S, S), :] = feat_ref[t, row].astype(jnp.float32)
        strips_ref[t, 2] = wide[pl.ds(0, S, stride=S), :].astype(jnp.bfloat16)
        strips_ref[t, 3] = wide[pl.ds(S - 1, S, stride=S), :].astype(jnp.bfloat16)
        return 0

    def strips_of(q):
        feat_copies[q].wait()
        lax.fori_loop(q * quarter, (q + 1) * quarter, one, 0)

    strips_of(0)
    strips_of(1)
    for copy in count_z:
        copy.wait_recv()
    slab = count_all.at[y]
    count_y = [remote(slab, slab, county_send, county_recv, d, y_peers[d - 1]) for d in range(1, NY)]
    for copy in count_y:
        copy.start()
    strips_of(2)

    def find(r, places):
        return tuple(jnp.where(perm_ref[0, r] == y * NZ + k, r, place) for k, place in enumerate(places))

    places = lax.fori_loop(0, PEERS, find, (jnp.int32(0),) * NZ)
    for copy in count_y:
        copy.wait_recv()
    to_smem = pltpu.make_async_copy(count_all, count_smem, smem_sem)
    to_smem.start()
    to_smem.wait()
    turn = turn_ref[0]
    for q in range(PEERS):
        counts_ref[q] = count_smem[q // NZ, q % NZ, 0, 0]
    for copy in rows_z:
        copy.wait_recv()

    def pick(owner, store):
        start = lax.fori_loop(
            0, PEERS, lambda q, t: t + jnp.where(q < owner, count_smem[q // NZ, q % NZ, 0, 0], 0), jnp.int32(0))
        for k in range(NZ):
            slot = (places[k] - start - turn) & (PEERS - 1)
            for j in range(2):
                rank = (start + slot + j * PEERS + turn) & (GROUP_TOTAL - 1)
                store(k, j, z_rows[k, pl.ds(rank >> 5, 1), :])

    rows_y = []
    for d in range(1, NY):
        def store(k, j, row):
            outgoing[d - 1, k, j:j + 1, :] = row

        pick(y_peers[d - 1], store)
        rows_y.append(remote(outgoing.at[d - 1], rows_ref.at[y], send_y, recv_y, d, y_peers[d - 1]))
        rows_y[-1].start()

    def keep(k, j, row):
        rows_ref[y, k, j:j + 1, :] = row

    pick(me, keep)
    strips_of(3)
    for copy in count_z + rows_z + count_y:
        copy.wait_send()
    for copy in rows_y:
        copy.wait()


def exchange(count, perm, turn, feat, cot):
    dma = pltpu.SemaphoreType.DMA
    vmem = pl.BlockSpec(memory_space=pltpu.VMEM)
    smem = pl.BlockSpec(memory_space=pltpu.SMEM)
    f32, i32 = jnp.float32, jnp.int32
    return pl.pallas_call(
        exchange_kernel,
        in_specs=[smem, smem, smem, pl.BlockSpec(memory_space=pl.ANY), vmem],
        out_specs=[vmem, vmem, smem],
        out_shape=[
            jax.ShapeDtypeStruct((SLOTS, 4, S, C), jnp.bfloat16),
            jax.ShapeDtypeStruct((NY, NZ, 2, C), f32),
            jax.ShapeDtypeStruct((PEERS,), i32),
        ],
        scratch_shapes=[
            pltpu.VMEM((SLOTS, S, S, C), jnp.bfloat16),
            pltpu.VMEM((S * S, C), f32),
            pltpu.VMEM((1, C), i32),
            pltpu.VMEM((NY, NZ, 1, C), i32),
            pltpu.SMEM((NY, NZ, 1, C), i32),
            pltpu.VMEM((NZ, WORK, C), f32),
            pltpu.VMEM((NY - 1, NZ, 2, C), f32),
            dma((4,)), dma((NZ - 1,)), dma((NZ - 1,)), dma((NY - 1,)), dma((NY - 1,)),
            dma((NZ - 1,)), dma((NZ - 1,)), dma((NY - 1,)), dma((NY - 1,)), dma,
        ],
        compiler_params=pltpu.CompilerParams(
            collective_id=0, has_side_effects=True, vmem_limit_bytes=56 << 20),
        name="exchange",
    )(count, perm, turn, feat, cot)


def start_of(counts_ref, owner):
    return lax.fori_loop(0, owner, lambda q, s: s + counts_ref[q], jnp.int32(0))


def fill_centre(pad, feat_ref, t, u):
    for y in range(S):
        pad[pl.ds(((y + 1) * W + 1) * G + t, S, stride=G), :] = feat_ref[u, y].astype(jnp.float32)


def pixel_math(window, pixels, slope_scale, taps, gain, w_in_ref, gi_ref, gk, gg):
    n = pixels * G
    depth, centre = None, None
    for a in range(3):
        for b in range(3):
            x = window(a, b)
            if a == 1 and b == 1:
                centre = jnp.sum(x, axis=0)
            term = x * taps[3 * a + b][None]
            depth = term if depth is None else depth + term
    depth = depth.reshape(n, C)
    centered = depth - jnp.mean(depth, axis=1, keepdims=True)
    inverse = lax.rsqrt(jnp.mean(centered * centered, axis=1, keepdims=True) + 1e-06)
    unit = centered * inverse
    normed = (unit * gain).astype(jnp.bfloat16)
    acts, grads = [], []
    half = HID // 2
    for h in range(0, HID, half):
        v = jnp.dot(normed, w_in_ref[:, h:h + half], preferred_element_type=jnp.float32)
        share = 0.5 * (1.0 + lax.erf(v * 0.7071067811865476))
        slope = share + v * (jnp.exp(-0.5 * v * v) * 0.3989422804014327)
        acts.append((v * share).astype(jnp.bfloat16))
        scaled = slope.reshape(pixels, G, half) * slope_scale[None, :, h:h + half]
        grads.append(scaled.reshape(n, half).astype(jnp.bfloat16))
    sub = lax.broadcasted_iota(jnp.int32, (G, n), 0)
    col = lax.broadcasted_iota(jnp.int32, (G, n), 1)
    select = jnp.where((col & (G - 1)) == sub, 1.0, 0.0).astype(jnp.bfloat16)
    act_sum = jnp.dot(select, jnp.concatenate(acts, axis=1), preferred_element_type=jnp.float32)
    grad_before = jnp.concatenate(grads, axis=1)
    gi_ref[...] += lax.dot_general(normed, grad_before, (((0,), (0,)), ((), ())), preferred_element_type=jnp.float32)
    grad_normed = lax.dot_general(grad_before, w_in_ref[...], (((1,), (1,)), ((), ())),
                                  preferred_element_type=jnp.float32)
    product = grad_normed * unit
    gg[...] += jnp.sum(product.reshape(pixels, G, C), axis=0)
    grad_unit = grad_normed * gain
    grad_depth = inverse * (
        grad_unit
        - jnp.mean(grad_unit, axis=1, keepdims=True)
        - unit * jnp.mean(product * gain, axis=1, keepdims=True)
    )
    grad_depth = grad_depth.reshape(pixels, G, C)
    for a in range(3):
        for b in range(3):
            gk[3 * a + b] += jnp.sum(grad_depth * window(a, b), axis=0)
    return act_sum, centre


def inner_kernel(counts_ref, perm_ref, turn_ref, feat_ref, rows_ref, taps_ref, gain_ref, w_in_ref, w_out_ref,
                 ge, ga, act, cen, gi_ref, gk, gg, taps, pad):
    g = pl.program_id(0)
    me = lax.axis_index("tile")
    count = counts_ref[me]

    @pl.when(g == 0)
    def _():
        for ref in (gk, gg, gi_ref, act, cen, ge):
            ref[...] = jnp.zeros_like(ref)
        for k in range(9):
            taps[k] = jnp.broadcast_to(taps_ref[k:k + 1, :].astype(jnp.float32), (G, C))
        first = start_of(counts_ref, me) + turn_ref[0]

        def row(i, _):
            rank = (first + i) & (GROUP_TOTAL - 1)
            worker = perm_ref[rank & (PEERS - 1)]
            ge[pl.ds(i, 1), :] = rows_ref[worker, pl.ds(i >> 5, 1), :] * (1.0 / (S * S))
            return 0

        lax.fori_loop(0, count, row, 0)
        ga[...] = lax.dot_general(ge[...], w_out_ref[...].astype(jnp.float32), (((1,), (1,)), ((), ())),
                                  precision=HIGHEST, preferred_element_type=jnp.float32)

    @pl.when(g * G < count)
    def _():
        for t in range(G):
            fill_centre(pad, feat_ref, t, t)
        side = S - 2

        def window(a, b):
            rows = [pad[pl.ds(((y + a) * W + 1 + b) * G, side * G), :] for y in range(1, S - 1)]
            return jnp.concatenate(rows, axis=0).reshape(side * side, G, C)

        mine = pl.ds(pl.multiple_of(g * G, G), G)
        act[mine, :], cen[mine, :] = pixel_math(
            window, side * side, ga[mine, :], taps, gain_ref[...], w_in_ref, gi_ref, gk, gg)


def whole(x):
    return pl.BlockSpec(x.shape, lambda g, *_: (0,) * len(x.shape))


def inner(counts, perm, turn, feat, rows, taps, gain, w_in, w_out):
    f32 = jnp.float32
    outs = [
        jax.ShapeDtypeStruct(shape, f32)
        for shape in ((SLOTS, C), (SLOTS, HID), (SLOTS, HID), (SLOTS, C), (C, HID), (9, G, C), (G, C), (9, G, C))
    ]
    grid_spec = pltpu.PrefetchScalarGridSpec(
        num_scalar_prefetch=3,
        grid=(SLOTS // G,),
        in_specs=[pl.BlockSpec((G, S, S, C), lambda g, *_: (g, 0, 0, 0))]
        + [whole(x) for x in (rows, taps, gain, w_in, w_out)],
        out_specs=[whole(x) for x in outs],
        scratch_shapes=[pltpu.VMEM((W * W * G, C), f32)],
    )
    return pl.pallas_call(
        inner_kernel,
        grid_spec=grid_spec,
        out_shape=outs,
        compiler_params=pltpu.CompilerParams(vmem_limit_bytes=60 << 20),
        cost_estimate=pl.CostEstimate(flops=10_000_000_000, bytes_accessed=100_000_000, transcendentals=0),
        name="inner",
    )(counts, perm, turn, feat, rows, taps, gain, w_in, w_out)


PAIR = 2


def border_kernel(nb_ref, counts_ref, perm_ref, turn_ref, feat_ref, left_ref, own_ref, right_ref, gain_ref, w_in_ref,
                  w_out_ref, ge, ga, act_in, cen_in, gi_in, gk_in, gg_in, taps,
                  send_ref, go_ref, gi_ref, small_ref, where_ref, pad, strips, act, cen, gk, gg, sems):
    g = pl.program_id(0)
    me = lax.axis_index("tile")
    count = counts_ref[me]
    turn = turn_ref[0]
    base = (me - 1) * SLOTS

    @pl.when(g == 0)
    def _():
        copies = [
            pltpu.make_async_copy(ref, strips.at[pl.ds(k * SLOTS, SLOTS)], sems.at[k])
            for k, ref in enumerate((left_ref, own_ref, right_ref))
        ]
        for copy in copies:
            copy.start()
        for ref, old in ((act, act_in), (cen, cen_in), (gi_ref, gi_in), (gk, gk_in), (gg, gg_in)):
            ref[...] = old[...]
        for copy in copies:
            copy.wait()

    @pl.when(g * PAIR * G < count)
    def _():
        for t in range(PAIR * G):
            pair_pad = pad.at[t // G]
            u = t % G
            fill_centre(pair_pad, feat_ref, u, t)

            def strip(k, which):
                n = nb_ref[k, g * PAIR * G + t]
                ok = n >= 0
                x = strips[jnp.where(ok, n - base, 0), which].astype(jnp.float32)
                return jnp.where(ok, x, 0.0)

            pair_pad[pl.ds(1 * G + u, S, stride=G), :] = strip(0, 1)
            pair_pad[pl.ds(((S + 1) * W + 1) * G + u, S, stride=G), :] = strip(1, 0)
            pair_pad[pl.ds(W * G + u, S, stride=G * W), :] = strip(2, 3)
            pair_pad[pl.ds((W + S + 1) * G + u, S, stride=G * W), :] = strip(3, 2)
            pair_pad[pl.ds(u, 1), :] = strip(4, 1)[S - 1:S]
            pair_pad[pl.ds((S + 1) * G + u, 1), :] = strip(5, 1)[0:1]
            pair_pad[pl.ds((S + 1) * W * G + u, 1), :] = strip(6, 0)[S - 1:S]
            pair_pad[pl.ds(((S + 1) * W + S + 1) * G + u, 1), :] = strip(7, 0)[0:1]

        for p in range(PAIR):
            def window(a, b):
                part = pad.at[p]
                rows = [part[pl.ds(((y + a) * W + b) * G, S * G), :] for y in (0, S - 1)]
                for x in (0, S - 1):
                    rows += [part[pl.ds(((y + a) * W + x + b) * G, G), :] for y in range(1, S - 1)]
                return jnp.concatenate(rows, axis=0).reshape(4 * S - 4, G, C)

            mine = pl.ds(pl.multiple_of((g * PAIR + p) * G, G), G)
            act_sum, centre = pixel_math(
                window, 4 * S - 4, ga[mine, :], taps, gain_ref[...], w_in_ref, gi_ref, gk, gg)
            act[mine, :] += act_sum
            cen[mine, :] += centre

    @pl.when(g == pl.num_programs(0) - 1)
    def _():
        go_ref[...] = lax.dot_general(act[...], ge[...], (((0,), (0,)), ((), ())),
                                      precision=HIGHEST, preferred_element_type=jnp.float32)
        embed = jnp.dot(act[...], w_out_ref[...].astype(jnp.float32), precision=HIGHEST,
                        preferred_element_type=jnp.float32)
        cen[...] = (cen[...] + embed) * (1.0 / (S * S))
        small_ref[...] = jnp.zeros_like(small_ref)
        for k in range(9):
            small_ref[k:k + 1, :] = jnp.sum(gk[k], axis=0, keepdims=True)
        small_ref[9:10, :] = jnp.sum(gg[...], axis=0, keepdims=True)
        send_ref[...] = jnp.zeros_like(send_ref)
        first = start_of(counts_ref, me) + turn

        def out_row(i, _):
            rank = (first + i) & (GROUP_TOTAL - 1)
            worker = perm_ref[rank & (PEERS - 1)]
            send_ref[worker, pl.ds(i >> 5, 1), :] = cen[pl.ds(i, 1), :]
            return 0

        lax.fori_loop(0, count, out_row, 0)
        residue = lax.fori_loop(0, PEERS, lambda r, s: jnp.where(perm_ref[r] == me, r, s), jnp.int32(0))

        def arrival(owner, start):
            slot = (residue - start - turn) & (PEERS - 1)
            for k in range(2):
                @pl.when(slot + k * PEERS < counts_ref[owner])
                def _():
                    place = ((start + slot + k * PEERS + turn) & (GROUP_TOTAL - 1)) >> 5
                    where_ref[place] = owner
                    where_ref[WORK + place] = k
            return start + counts_ref[owner]

        lax.fori_loop(0, PEERS, arrival, jnp.int32(0))


def border(nb, counts, perm, turn, feat, left, own, right, gain, w_in, w_out, sums):
    f32 = jnp.float32
    outs = [jax.ShapeDtypeStruct(shape, f32) for shape in ((PEERS, 2, C), (HID, C), (C, HID), (16, C))]
    grid_spec = pltpu.PrefetchScalarGridSpec(
        num_scalar_prefetch=4,
        grid=(SLOTS // (PAIR * G),),
        in_specs=[pl.BlockSpec((PAIR * G, S, S, C), lambda g, *_: (g, 0, 0, 0))]
        + [pl.BlockSpec(memory_space=pl.ANY)] * 3
        + [whole(x) for x in (gain, w_in, w_out, *sums)],
        out_specs=[whole(x) for x in outs] + [pl.BlockSpec(memory_space=pltpu.SMEM)],
        scratch_shapes=[
            pltpu.VMEM((PAIR, W * W * G, C), f32),
            pltpu.VMEM((3 * SLOTS, 4, S, C), jnp.bfloat16),
            pltpu.VMEM((SLOTS, HID), f32),
            pltpu.VMEM((SLOTS, C), f32),
            pltpu.VMEM((9, G, C), f32),
            pltpu.VMEM((G, C), f32),
            pltpu.SemaphoreType.DMA((3,)),
        ],
    )
    return pl.pallas_call(
        border_kernel,
        grid_spec=grid_spec,
        out_shape=outs + [jax.ShapeDtypeStruct((2 * WORK,), jnp.int32)],
        compiler_params=pltpu.CompilerParams(vmem_limit_bytes=60 << 20),
        name="border",
    )(nb, counts, perm, turn, feat, left, own, right, gain, w_in, w_out, *sums)


UNITS = 17


def reduce_kernel(where_ref, rows_ref, go_ref, gi_ref, small_ref, embed_ref, gk_ref, gg_ref, gi_out, go_out,
                  full, result, from_core, half, from_x, piece, from_tile, landed,
                  row_send, row_recv, core_send, core_recv, x_send, x_recv, unit_send, unit_recv,
                  back_send, back_recv, x_back_send, x_back_recv, core_back_send, core_back_recv):
    me = lax.axis_index("tile")
    slide = lax.axis_index("slide")
    x, core = slide // 2, slide % 2
    partner = x * 2 + (1 - core)
    x_peers = [((x + d) % NX) for d in range(1, NX)]

    barrier = pltpu.get_barrier_semaphore()
    for d in range(1, PEERS):
        pl.semaphore_signal(barrier, inc=1, **to_tile((me + d) % PEERS))
    pl.semaphore_signal(barrier, inc=1, **to_slide(partner))
    for peer in x_peers:
        pl.semaphore_signal(barrier, inc=1, **to_slide(peer * 2 + core))

    for s in range(4):
        full[s // 2, s % 2, 0:16] = gi_ref[:, s * C:(s + 1) * C].reshape(16, 8, C)
        full[2 + s // 2, s % 2, 0:16] = go_ref[s * C:(s + 1) * C, :].reshape(16, 8, C)
    for s in range(8):
        full[s // 2, s % 2, 16] = small_ref[8 * s:8 * s + 8, :] if s < 2 else jnp.zeros((8, C), jnp.float32)

    pl.semaphore_wait(barrier, PEERS + NX - 1)

    to_core = pltpu.make_async_remote_copy(
        src_ref=full.at[:, 1 - core], dst_ref=from_core, send_sem=core_send, recv_sem=core_recv, **to_slide(partner))
    to_core.start()
    row_copies = []
    for d in range(1, PEERS):
        peer = (me + d) % PEERS
        row_copies.append(pltpu.make_async_remote_copy(
            src_ref=rows_ref.at[peer], dst_ref=landed.at[me],
            send_sem=row_send.at[d - 1], recv_sem=row_recv.at[d - 1], **to_tile(peer)))
        row_copies[-1].start()
    landed[me] = rows_ref[me]
    to_core.wait()
    half[...] = full[:, core] + from_core[...]

    x_copies = []
    for d in range(1, NX):
        x_copies.append(pltpu.make_async_remote_copy(
            src_ref=half.at[x_peers[d - 1]], dst_ref=from_x.at[d - 1],
            send_sem=x_send.at[d - 1], recv_sem=x_recv.at[d - 1], **to_slide(x_peers[d - 1] * 2 + core)))
        x_copies[-1].start()
    for copy in x_copies:
        copy.wait()
    piece[...] = half[x] + from_x[0] + from_x[1] + from_x[2]

    owners = [2 * u for u in range(16)] + [1]

    def unit_copy(u):
        return pltpu.make_async_remote_copy(
            src_ref=piece.at[u], dst_ref=from_tile.at[me],
            send_sem=unit_send.at[u], recv_sem=unit_recv.at[me], **to_tile(owners[u]))

    def back_copy(u, d):
        return pltpu.make_async_remote_copy(
            src_ref=result.at[x, core, u], dst_ref=result.at[x, core, u],
            send_sem=back_send.at[d - 1], recv_sem=back_recv.at[u], **to_tile((me + d) % PEERS))

    for u in range(UNITS):
        @pl.when(me != owners[u])
        def _():
            unit_copy(u).start()
    for u in range(UNITS):
        @pl.when(me == owners[u])
        def _():
            from_tile[owners[u]] = piece[u]
            for q in range(PEERS):
                if q != owners[u]:
                    pltpu.make_async_remote_copy(
                        src_ref=piece.at[u], dst_ref=from_tile.at[q],
                        send_sem=unit_send.at[u], recv_sem=unit_recv.at[q], **to_tile(q)).wait_recv()
            result[x, core, u] = jnp.sum(from_tile[...], axis=0)
            for d in range(1, PEERS):
                back_copy(u, d).start()
    for u in range(UNITS):
        @pl.when(me != owners[u])
        def _():
            unit_copy(u).wait_send()
            back_copy(u, 1).wait_recv()

    to_partner = []

    def forward(k, where):
        to_partner.append(pltpu.make_async_remote_copy(
            src_ref=result.at[where, core], dst_ref=result.at[where, core],
            send_sem=core_back_send.at[k], recv_sem=core_back_recv.at[k], **to_slide(partner)))
        to_partner[-1].start()

    x_back = []
    for d in range(1, NX):
        x_back.append(pltpu.make_async_remote_copy(
            src_ref=result.at[x, core], dst_ref=result.at[x, core],
            send_sem=x_back_send.at[d - 1], recv_sem=x_back_recv.at[d - 1], **to_slide(x_peers[d - 1] * 2 + core)))
        x_back[-1].start()
    forward(0, x)
    for copy in row_copies:
        copy.wait()
    for j in range(WORK):
        embed_ref[j:j + 1, :] = landed[where_ref[j], pl.ds(where_ref[WORK + j], 1), :]
    for d in range(1, NX):
        x_back[d - 1].wait_recv()
        forward(d, (x + NX - d) % NX)
    for copy in x_back:
        copy.wait_send()
    for u in range(UNITS):
        @pl.when(me == owners[u])
        def _():
            for d in range(1, PEERS):
                back_copy(u, d).wait_send()
    for copy in to_partner:
        copy.wait()

    for s in range(4):
        gi_out[:, s * C:(s + 1) * C] = result[s // 2, s % 2, 0:16].reshape(C, C)
        go_out[s * C:(s + 1) * C, :] = result[2 + s // 2, s % 2, 0:16].reshape(C, C)
    gk_ref[0:8, :] = result[0, 0, 16]
    gk_ref[8:9, :] = result[0, 1, 16, 0:1]
    gg_ref[...] = result[0, 1, 16, 1:2]


def reduce(where, rows, go, gi, small):
    dma = pltpu.SemaphoreType.DMA
    f32 = jnp.float32
    vmem = pl.BlockSpec(memory_space=pltpu.VMEM)
    return pl.pallas_call(
        reduce_kernel,
        in_specs=[pl.BlockSpec(memory_space=pltpu.SMEM)] + [vmem] * 4,
        out_specs=[vmem] * 5,
        out_shape=[
            jax.ShapeDtypeStruct((WORK, C), f32),
            jax.ShapeDtypeStruct((9, C), f32),
            jax.ShapeDtypeStruct((1, C), f32),
            jax.ShapeDtypeStruct((C, HID), f32),
            jax.ShapeDtypeStruct((HID, C), f32),
        ],
        scratch_shapes=[
            pltpu.VMEM((NX, 2, UNITS, 8, C), f32),
            pltpu.VMEM((NX, 2, UNITS, 8, C), f32),
            pltpu.VMEM((NX, UNITS, 8, C), f32),
            pltpu.VMEM((NX, UNITS, 8, C), f32),
            pltpu.VMEM((NX - 1, UNITS, 8, C), f32),
            pltpu.VMEM((UNITS, 8, C), f32),
            pltpu.VMEM((PEERS, 8, C), f32),
            pltpu.VMEM((PEERS, 2, C), f32),
            dma((PEERS - 1,)), dma((PEERS - 1,)), dma, dma, dma((NX - 1,)), dma((NX - 1,)),
            dma((UNITS,)), dma((PEERS,)), dma((PEERS - 1,)), dma((UNITS,)),
            dma((NX - 1,)), dma((NX - 1,)), dma((NX,)), dma((NX,)),
        ],
        compiler_params=pltpu.CompilerParams(
            collective_id=1, has_side_effects=True, vmem_limit_bytes=60 << 20),
        name="reduce",
    )(where, rows, go, gi, small)


def local(features, tissue_count, neighbors, worker_perm, rotation, kernel, gain, w_in, w_out, cotangent):
    feat = features[0]
    strips, rows, counts = exchange(tissue_count, worker_perm, rotation, feat, cotangent[0])
    rows = rows.reshape(PEERS, 2, C)
    peers = lax.axis_size("tile")
    left = lax.ppermute(strips, "tile", [(i, i + 1) for i in range(peers - 1)])
    right = lax.ppermute(strips, "tile", [(i + 1, i) for i in range(peers - 1)])
    sums = inner(counts, worker_perm[0], rotation, feat, rows, kernel, gain[None], w_in, w_out)
    send, go, gi, small, where = border(
        neighbors[0].T, counts, worker_perm[0], rotation, feat, left, strips, right, gain[None], w_in, w_out, sums)
    embed, grad_kernel, grad_gain, grad_in, grad_out = reduce(where, send, go, gi, small)
    return embed[None], grad_kernel, grad_gain[0], grad_in, grad_out


def solution(mesh):
    placed = (
        P("slide", "tile", None, None, None),
        P("slide", "tile"),
        P("slide", "tile", None),
        P("slide", None),
        P("slide"),
        P(),
        P(),
        P(),
        P(),
        P("slide", "tile", None),
    )
    return jax.shard_map(
        local,
        mesh=mesh,
        in_specs=placed,
        out_specs=(P("slide", "tile", None), P(), P(), P(), P()),
        check_vma=False,
    )
```

```python
import functools

import jax
import jax.numpy as jnp
from jax import lax
from jax.experimental import pallas as pl
from jax.experimental.pallas import tpu as pltpu
from jax.sharding import PartitionSpec as P

C = 128
HID = 512
S = 16
W = S + 2
G = 8
SLOTS = 64
WORK = 32
PEERS = 32
NZ, NY = 8, 4
NX = 4
GROUP_TOTAL = PEERS * WORK
MESH = pl.DeviceIdType.MESH
HIGHEST = lax.Precision.HIGHEST


def to_tile(index):
    return dict(device_id={"tile": index}, device_id_type=MESH)


def to_slide(index):
    return dict(device_id={"slide": index}, device_id_type=MESH)


def exchange_kernel(count_ref, perm_ref, turn_ref, feat_hbm, cot_ref, strips_ref, rows_ref, counts_ref,
                    feat_ref, wide, own_count, count_all, count_smem, z_rows, outgoing, feat_sem,
                    count_send, count_recv, county_send, county_recv, send_z, recv_z, send_y, recv_y, smem_sem):
    me = lax.axis_index("tile")
    y, z = me // NZ, me % NZ
    z_peers = [y * NZ + (z + d) % NZ for d in range(1, NZ)]
    y_peers = [((y + d) % NY) * NZ + z for d in range(1, NY)]

    barrier = pltpu.get_barrier_semaphore()
    for peer in z_peers + y_peers:
        pl.semaphore_signal(barrier, inc=1, **to_tile(peer))
    quarter = SLOTS // 4
    feat_copies = [
        pltpu.make_async_copy(feat_hbm.at[pl.ds(q * quarter, quarter)], feat_ref.at[pl.ds(q * quarter, quarter)],
                              feat_sem.at[q])
        for q in range(4)
    ]
    for copy in feat_copies:
        copy.start()
    own_count[...] = jnp.full((1, C), count_ref[0, 0], jnp.int32)
    pl.semaphore_wait(barrier, NZ + NY - 2)

    def remote(src, dst, send, recv, d, peer):
        return pltpu.make_async_remote_copy(
            src_ref=src, dst_ref=dst, send_sem=send.at[d - 1], recv_sem=recv.at[d - 1], **to_tile(peer))

    count_z = [remote(own_count, count_all.at[y, z], count_send, count_recv, d, z_peers[d - 1]) for d in range(1, NZ)]
    rows_z = [remote(cot_ref, z_rows.at[z], send_z, recv_z, d, z_peers[d - 1]) for d in range(1, NZ)]
    for copy in count_z + rows_z:
        copy.start()
    count_all[y, z] = own_count[...]
    z_rows[z] = cot_ref[...]

    def one(t, _):
        strips_ref[t, 0] = feat_ref[t, 0]
        strips_ref[t, 1] = feat_ref[t, S - 1]
        for row in range(S):
            wide[pl.ds(row * S, S), :] = feat_ref[t, row].astype(jnp.float32)
        strips_ref[t, 2] = wide[pl.ds(0, S, stride=S), :].astype(jnp.bfloat16)
        strips_ref[t, 3] = wide[pl.ds(S - 1, S, stride=S), :].astype(jnp.bfloat16)
        return 0

    def strips_of(q):
        feat_copies[q].wait()
        lax.fori_loop(q * quarter, (q + 1) * quarter, one, 0)

    strips_of(0)
    strips_of(1)
    for copy in count_z:
        copy.wait_recv()
    slab = count_all.at[y]
    count_y = [remote(slab, slab, county_send, county_recv, d, y_peers[d - 1]) for d in range(1, NY)]
    for copy in count_y:
        copy.start()
    strips_of(2)

    def find(r, places):
        return tuple(jnp.where(perm_ref[0, r] == y * NZ + k, r, place) for k, place in enumerate(places))

    places = lax.fori_loop(0, PEERS, find, (jnp.int32(0),) * NZ)
    for copy in count_y:
        copy.wait_recv()
    to_smem = pltpu.make_async_copy(count_all, count_smem, smem_sem)
    to_smem.start()
    to_smem.wait()
    turn = turn_ref[0]
    for q in range(PEERS):
        counts_ref[q] = count_smem[q // NZ, q % NZ, 0, 0]
    for copy in rows_z:
        copy.wait_recv()

    def pick(owner, store):
        start = lax.fori_loop(
            0, PEERS, lambda q, t: t + jnp.where(q < owner, count_smem[q // NZ, q % NZ, 0, 0], 0), jnp.int32(0))
        for k in range(NZ):
            slot = (places[k] - start - turn) & (PEERS - 1)
            for j in range(2):
                rank = (start + slot + j * PEERS + turn) & (GROUP_TOTAL - 1)
                store(k, j, z_rows[k, pl.ds(rank >> 5, 1), :])

    rows_y = []
    for d in range(1, NY):
        def store(k, j, row):
            outgoing[d - 1, k, j:j + 1, :] = row

        pick(y_peers[d - 1], store)
        rows_y.append(remote(outgoing.at[d - 1], rows_ref.at[y], send_y, recv_y, d, y_peers[d - 1]))
        rows_y[-1].start()

    def keep(k, j, row):
        rows_ref[y, k, j:j + 1, :] = row

    pick(me, keep)
    strips_of(3)
    for copy in count_z + rows_z + count_y:
        copy.wait_send()
    for copy in rows_y:
        copy.wait()


def exchange(count, perm, turn, feat, cot):
    dma = pltpu.SemaphoreType.DMA
    vmem = pl.BlockSpec(memory_space=pltpu.VMEM)
    smem = pl.BlockSpec(memory_space=pltpu.SMEM)
    f32, i32 = jnp.float32, jnp.int32
    return pl.pallas_call(
        exchange_kernel,
        in_specs=[smem, smem, smem, pl.BlockSpec(memory_space=pl.ANY), vmem],
        out_specs=[vmem, vmem, smem],
        out_shape=[
            jax.ShapeDtypeStruct((SLOTS, 4, S, C), jnp.bfloat16),
            jax.ShapeDtypeStruct((NY, NZ, 2, C), f32),
            jax.ShapeDtypeStruct((PEERS,), i32),
        ],
        scratch_shapes=[
            pltpu.VMEM((SLOTS, S, S, C), jnp.bfloat16),
            pltpu.VMEM((S * S, C), f32),
            pltpu.VMEM((1, C), i32),
            pltpu.VMEM((NY, NZ, 1, C), i32),
            pltpu.SMEM((NY, NZ, 1, C), i32),
            pltpu.VMEM((NZ, WORK, C), f32),
            pltpu.VMEM((NY - 1, NZ, 2, C), f32),
            dma((4,)), dma((NZ - 1,)), dma((NZ - 1,)), dma((NY - 1,)), dma((NY - 1,)),
            dma((NZ - 1,)), dma((NZ - 1,)), dma((NY - 1,)), dma((NY - 1,)), dma,
        ],
        compiler_params=pltpu.CompilerParams(
            collective_id=0, has_side_effects=True, vmem_limit_bytes=56 << 20),
        name="exchange",
    )(count, perm, turn, feat, cot)


def start_of(counts_ref, owner):
    return lax.fori_loop(0, owner, lambda q, s: s + counts_ref[q], jnp.int32(0))


def fill_centre(pad, feat_ref, t, u):
    for y in range(S):
        pad[pl.ds(((y + 1) * W + 1) * G + t, S, stride=G), :] = feat_ref[u, y].astype(jnp.float32)


def pixel_math(windows, pixels, together, slope_scales, taps, gain, w_in_ref, gi_ref, gk, gg):
    n = pixels * G
    half = HID // 2
    sub = lax.broadcasted_iota(jnp.int32, (G, n), 0)
    col = lax.broadcasted_iota(jnp.int32, (G, n), 1)
    select = jnp.where((col & (G - 1)) == sub, 1.0, 0.0).astype(jnp.bfloat16)

    def norm(window):
        depth, centre = None, None
        for a in range(3):
            for b in range(3):
                x = window(a, b)
                if a == 1 and b == 1:
                    centre = jnp.sum(x, axis=0)
                term = x * taps[3 * a + b][None]
                depth = term if depth is None else depth + term
        depth = depth.reshape(n, C)
        centered = depth - jnp.mean(depth, axis=1, keepdims=True)
        inverse = lax.rsqrt(jnp.mean(centered * centered, axis=1, keepdims=True) + 1e-06)
        unit = centered * inverse
        return centre, inverse, unit, (unit * gain).astype(jnp.bfloat16)

    def hidden(normed, slope_scale):
        acts, grads = [], []
        for h in range(0, HID, half):
            v = jnp.dot(normed, w_in_ref[:, h:h + half], preferred_element_type=jnp.float32)
            share = 0.5 * (1.0 + lax.erf(v * 0.7071067811865476))
            slope = share + v * (jnp.exp(-0.5 * v * v) * 0.3989422804014327)
            acts.append((v * share).astype(jnp.bfloat16))
            scaled = slope.reshape(pixels, G, half) * slope_scale[None, :, h:h + half]
            grads.append(scaled.reshape(n, half).astype(jnp.bfloat16))
        return jnp.concatenate(acts, axis=1), jnp.concatenate(grads, axis=1)

    def back(window, inverse, unit, acts, grad_before):
        act_sum = jnp.dot(select, acts, preferred_element_type=jnp.float32)
        grad_normed = lax.dot_general(grad_before, w_in_ref[...], (((1,), (1,)), ((), ())),
                                      preferred_element_type=jnp.float32)
        product = grad_normed * unit
        gg[...] += jnp.sum(product.reshape(pixels, G, C), axis=0)
        grad_unit = grad_normed * gain
        grad_depth = inverse * (
            grad_unit
            - jnp.mean(grad_unit, axis=1, keepdims=True)
            - unit * jnp.mean(product * gain, axis=1, keepdims=True)
        )
        grad_depth = grad_depth.reshape(pixels, G, C)
        for a in range(3):
            for b in range(3):
                gk[3 * a + b] += jnp.sum(grad_depth * window(a, b), axis=0)
        return act_sum

    count = len(windows)
    normal, wide, sums = {}, {}, []
    for i in range(count + 2):
        if i >= 2:
            k = i - 2
            sums.append((back(windows[k], normal[k][1], normal[k][2], *wide[k]), normal[k][0]))
        if 1 <= i <= count:
            wide[i - 1] = hidden(normal[i - 1][3], slope_scales[i - 1])
        if i < count:
            normal[i] = norm(windows[i])
        if i >= 2 and (i - 1) % together == 0:
            ks = range(i - 1 - together, i - 1)
            gi_ref[...] += lax.dot_general(
                jnp.concatenate([normal[k][3] for k in ks], axis=0), jnp.concatenate([wide[k][1] for k in ks], axis=0),
                (((0,), (0,)), ((), ())), preferred_element_type=jnp.float32)
    return sums


def inner_kernel(counts_ref, perm_ref, turn_ref, feat_ref, rows_ref, taps_ref, gain_ref, w_in_ref, w_out_ref,
                 ge, ga, act, cen, gi_ref, gk, gg, taps, pad):
    g = pl.program_id(0)
    me = lax.axis_index("tile")
    count = counts_ref[me]

    @pl.when(g == 0)
    def _():
        for ref in (gk, gg, gi_ref, act, cen, ge):
            ref[...] = jnp.zeros_like(ref)
        for k in range(9):
            taps[k] = jnp.broadcast_to(taps_ref[k:k + 1, :].astype(jnp.float32), (G, C))
        first = start_of(counts_ref, me) + turn_ref[0]

        def row(i, _):
            rank = (first + i) & (GROUP_TOTAL - 1)
            worker = perm_ref[rank & (PEERS - 1)]
            ge[pl.ds(i, 1), :] = rows_ref[worker, pl.ds(i >> 5, 1), :] * (1.0 / (S * S))
            return 0

        lax.fori_loop(0, count, row, 0)
        ga[...] = lax.dot_general(ge[...], w_out_ref[...].astype(jnp.float32), (((1,), (1,)), ((), ())),
                                  precision=HIGHEST, preferred_element_type=jnp.float32)

    @pl.when(g * G < count)
    def _():
        for t in range(G):
            fill_centre(pad, feat_ref, t, t)
        side = S - 2

        lines = 14

        def window_of(top):
            def window(a, b):
                rows = [pad[pl.ds(((y + a) * W + 1 + b) * G, side * G), :] for y in range(top, top + lines)]
                return jnp.concatenate(rows, axis=0).reshape(lines * side, G, C)
            return window

        mine = pl.ds(pl.multiple_of(g * G, G), G)
        windows = [window_of(top) for top in range(1, S - 1, lines)]
        scale = ga[mine, :]
        sums = pixel_math(windows, lines * side, 1, [scale] * len(windows), taps, gain_ref[...], w_in_ref,
                          gi_ref, gk, gg)
        act[mine, :] = sum(part[0] for part in sums)
        cen[mine, :] = sum(part[1] for part in sums)


def whole(x):
    return pl.BlockSpec(x.shape, lambda g, *_: (0,) * len(x.shape))


def inner(counts, perm, turn, feat, rows, taps, gain, w_in, w_out):
    f32 = jnp.float32
    outs = [
        jax.ShapeDtypeStruct(shape, f32)
        for shape in ((SLOTS, C), (SLOTS, HID), (SLOTS, HID), (SLOTS, C), (C, HID), (9, G, C), (G, C), (9, G, C))
    ]
    grid_spec = pltpu.PrefetchScalarGridSpec(
        num_scalar_prefetch=3,
        grid=(SLOTS // G,),
        in_specs=[pl.BlockSpec((G, S, S, C), lambda g, *_: (g, 0, 0, 0))]
        + [whole(x) for x in (rows, taps, gain, w_in, w_out)],
        out_specs=[whole(x) for x in outs],
        scratch_shapes=[pltpu.VMEM((W * W * G, C), f32)],
    )
    return pl.pallas_call(
        inner_kernel,
        grid_spec=grid_spec,
        out_shape=outs,
        compiler_params=pltpu.CompilerParams(vmem_limit_bytes=40 << 20),
        cost_estimate=pl.CostEstimate(flops=10_000_000_000, bytes_accessed=100_000_000, transcendentals=0),
        name="inner",
    )(counts, perm, turn, feat, rows, taps, gain, w_in, w_out)


PAIR = 4


def border_kernel(nb_ref, counts_ref, perm_ref, turn_ref, feat_ref, left_ref, own_ref, right_ref, gain_ref, w_in_ref,
                  w_out_ref, ge, ga, act_in, cen_in, gi_in, gk_in, gg_in, taps,
                  send_ref, go_ref, gi_ref, small_ref, where_ref, pad, strips, act, cen, gk, gg, sems):
    g = pl.program_id(0)
    me = lax.axis_index("tile")
    count = counts_ref[me]
    turn = turn_ref[0]
    base = (me - 1) * SLOTS

    @pl.when(g == 0)
    def _():
        copies = [
            pltpu.make_async_copy(ref, strips.at[pl.ds(k * SLOTS, SLOTS)], sems.at[k])
            for k, ref in enumerate((left_ref, own_ref, right_ref))
        ]
        for copy in copies:
            copy.start()
        for ref, old in ((act, act_in), (cen, cen_in), (gi_ref, gi_in), (gk, gk_in), (gg, gg_in)):
            ref[...] = old[...]
        for copy in copies:
            copy.wait()

    @pl.when(g * PAIR * G < count)
    def _():
        for t in range(PAIR * G):
            pair_pad = pad.at[t // G]
            u = t % G
            fill_centre(pair_pad, feat_ref, u, t)

            def strip(k, which):
                n = nb_ref[k, g * PAIR * G + t]
                ok = n >= 0
                x = strips[jnp.where(ok, n - base, 0), which].astype(jnp.float32)
                return jnp.where(ok, x, 0.0)

            pair_pad[pl.ds(1 * G + u, S, stride=G), :] = strip(0, 1)
            pair_pad[pl.ds(((S + 1) * W + 1) * G + u, S, stride=G), :] = strip(1, 0)
            pair_pad[pl.ds(W * G + u, S, stride=G * W), :] = strip(2, 3)
            pair_pad[pl.ds((W + S + 1) * G + u, S, stride=G * W), :] = strip(3, 2)
            pair_pad[pl.ds(u, 1), :] = strip(4, 1)[S - 1:S]
            pair_pad[pl.ds((S + 1) * G + u, 1), :] = strip(5, 1)[0:1]
            pair_pad[pl.ds((S + 1) * W * G + u, 1), :] = strip(6, 0)[S - 1:S]
            pair_pad[pl.ds(((S + 1) * W + S + 1) * G + u, 1), :] = strip(7, 0)[0:1]

        def window_of(p):
            def window(a, b):
                part = pad.at[p]
                rows = [part[pl.ds(((y + a) * W + b) * G, S * G), :] for y in (0, S - 1)]
                for x in (0, S - 1):
                    rows += [part[pl.ds(((y + a) * W + x + b) * G, G), :] for y in range(1, S - 1)]
                return jnp.concatenate(rows, axis=0).reshape(4 * S - 4, G, C)
            return window

        spans = [pl.ds(pl.multiple_of((g * PAIR + p) * G, G), G) for p in range(PAIR)]
        sums = pixel_math([window_of(p) for p in range(PAIR)], 4 * S - 4, 2, [ga[span, :] for span in spans],
                          taps, gain_ref[...], w_in_ref, gi_ref, gk, gg)
        for span, (act_sum, centre) in zip(spans, sums):
            act[span, :] += act_sum
            cen[span, :] += centre

    @pl.when(g == pl.num_programs(0) - 1)
    def _():
        go_ref[...] = lax.dot_general(act[...], ge[...], (((0,), (0,)), ((), ())),
                                      precision=HIGHEST, preferred_element_type=jnp.float32)
        embed = jnp.dot(act[...], w_out_ref[...].astype(jnp.float32), precision=HIGHEST,
                        preferred_element_type=jnp.float32)
        cen[...] = (cen[...] + embed) * (1.0 / (S * S))
        small_ref[...] = jnp.zeros_like(small_ref)
        for k in range(9):
            small_ref[k:k + 1, :] = jnp.sum(gk[k], axis=0, keepdims=True)
        small_ref[9:10, :] = jnp.sum(gg[...], axis=0, keepdims=True)
        send_ref[...] = jnp.zeros_like(send_ref)
        first = start_of(counts_ref, me) + turn

        def out_row(i, _):
            rank = (first + i) & (GROUP_TOTAL - 1)
            worker = perm_ref[rank & (PEERS - 1)]
            send_ref[worker, pl.ds(i >> 5, 1), :] = cen[pl.ds(i, 1), :]
            return 0

        lax.fori_loop(0, count, out_row, 0)
        residue = lax.fori_loop(0, PEERS, lambda r, s: jnp.where(perm_ref[r] == me, r, s), jnp.int32(0))

        def arrival(owner, start):
            slot = (residue - start - turn) & (PEERS - 1)
            for k in range(2):
                @pl.when(slot + k * PEERS < counts_ref[owner])
                def _():
                    place = ((start + slot + k * PEERS + turn) & (GROUP_TOTAL - 1)) >> 5
                    where_ref[place] = owner
                    where_ref[WORK + place] = k
            return start + counts_ref[owner]

        lax.fori_loop(0, PEERS, arrival, jnp.int32(0))


def border(nb, counts, perm, turn, feat, left, own, right, gain, w_in, w_out, sums):
    f32 = jnp.float32
    outs = [jax.ShapeDtypeStruct(shape, f32) for shape in ((PEERS, 2, C), (HID, C), (C, HID), (16, C))]
    grid_spec = pltpu.PrefetchScalarGridSpec(
        num_scalar_prefetch=4,
        grid=(SLOTS // (PAIR * G),),
        in_specs=[pl.BlockSpec((PAIR * G, S, S, C), lambda g, *_: (g, 0, 0, 0))]
        + [pl.BlockSpec(memory_space=pl.ANY)] * 3
        + [whole(x) for x in (gain, w_in, w_out, *sums)],
        out_specs=[whole(x) for x in outs] + [pl.BlockSpec(memory_space=pltpu.SMEM)],
        scratch_shapes=[
            pltpu.VMEM((PAIR, W * W * G, C), f32),
            pltpu.VMEM((3 * SLOTS, 4, S, C), jnp.bfloat16),
            pltpu.VMEM((SLOTS, HID), f32),
            pltpu.VMEM((SLOTS, C), f32),
            pltpu.VMEM((9, G, C), f32),
            pltpu.VMEM((G, C), f32),
            pltpu.SemaphoreType.DMA((3,)),
        ],
    )
    return pl.pallas_call(
        border_kernel,
        grid_spec=grid_spec,
        out_shape=outs + [jax.ShapeDtypeStruct((2 * WORK,), jnp.int32)],
        compiler_params=pltpu.CompilerParams(vmem_limit_bytes=40 << 20),
        name="border",
    )(nb, counts, perm, turn, feat, left, own, right, gain, w_in, w_out, *sums)


UNITS = 17


def reduce_kernel(rows_ref, go_ref, gi_ref, small_ref, result, landed,
                  full, from_core, half, from_x, piece, from_tile,
                  row_send, row_recv, core_send, core_recv, x_send, x_recv, unit_send, unit_recv,
                  back_send, back_recv, x_back_send, x_back_recv, core_back_send, core_back_recv):
    me = lax.axis_index("tile")
    slide = lax.axis_index("slide")
    x, core = slide // 2, slide % 2
    partner = x * 2 + (1 - core)
    x_peers = [((x + d) % NX) for d in range(1, NX)]

    barrier = pltpu.get_barrier_semaphore()
    for d in range(1, PEERS):
        pl.semaphore_signal(barrier, inc=1, **to_tile((me + d) % PEERS))
    pl.semaphore_signal(barrier, inc=1, **to_slide(partner))
    for peer in x_peers:
        pl.semaphore_signal(barrier, inc=1, **to_slide(peer * 2 + core))

    for s in range(4):
        full[s // 2, s % 2, 0:16] = gi_ref[:, s * C:(s + 1) * C].reshape(16, 8, C)
        full[2 + s // 2, s % 2, 0:16] = go_ref[s * C:(s + 1) * C, :].reshape(16, 8, C)
    for s in range(8):
        full[s // 2, s % 2, 16] = small_ref[8 * s:8 * s + 8, :] if s < 2 else jnp.zeros((8, C), jnp.float32)

    pl.semaphore_wait(barrier, PEERS + NX - 1)

    to_core = pltpu.make_async_remote_copy(
        src_ref=full.at[:, 1 - core], dst_ref=from_core, send_sem=core_send, recv_sem=core_recv, **to_slide(partner))
    to_core.start()
    to_core.wait()
    half[...] = full[:, core] + from_core[...]

    x_copies = []
    for d in range(1, NX):
        x_copies.append(pltpu.make_async_remote_copy(
            src_ref=half.at[x_peers[d - 1]], dst_ref=from_x.at[d - 1],
            send_sem=x_send.at[d - 1], recv_sem=x_recv.at[d - 1], **to_slide(x_peers[d - 1] * 2 + core)))
        x_copies[-1].start()
    row_copies = []
    for d in range(1, PEERS):
        peer = (me + d) % PEERS
        row_copies.append(pltpu.make_async_remote_copy(
            src_ref=rows_ref.at[peer], dst_ref=landed.at[me],
            send_sem=row_send.at[d - 1], recv_sem=row_recv.at[d - 1], **to_tile(peer)))
        row_copies[-1].start()
    landed[me] = rows_ref[me]
    for copy in x_copies:
        copy.wait()
    piece[...] = half[x] + from_x[0] + from_x[1] + from_x[2]

    owners = [2 * u for u in range(16)] + [1]

    def unit_copy(u):
        return pltpu.make_async_remote_copy(
            src_ref=piece.at[u], dst_ref=from_tile.at[me],
            send_sem=unit_send.at[u], recv_sem=unit_recv.at[me], **to_tile(owners[u]))

    def back_copy(u, d):
        return pltpu.make_async_remote_copy(
            src_ref=result.at[x, core, u], dst_ref=result.at[x, core, u],
            send_sem=back_send.at[d - 1], recv_sem=back_recv.at[u], **to_tile((me + d) % PEERS))

    for u in range(UNITS):
        @pl.when(me != owners[u])
        def _():
            unit_copy(u).start()
    for u in range(UNITS):
        @pl.when(me == owners[u])
        def _():
            from_tile[owners[u]] = piece[u]
            for q in range(PEERS):
                if q != owners[u]:
                    pltpu.make_async_remote_copy(
                        src_ref=piece.at[u], dst_ref=from_tile.at[q],
                        send_sem=unit_send.at[u], recv_sem=unit_recv.at[q], **to_tile(q)).wait_recv()
            result[x, core, u] = jnp.sum(from_tile[...], axis=0)
            for d in range(1, PEERS):
                back_copy(u, d).start()
    for u in range(UNITS):
        @pl.when(me != owners[u])
        def _():
            unit_copy(u).wait_send()
            back_copy(u, 1).wait_recv()

    to_partner = []

    def forward(k, where):
        to_partner.append(pltpu.make_async_remote_copy(
            src_ref=result.at[where, core], dst_ref=result.at[where, core],
            send_sem=core_back_send.at[k], recv_sem=core_back_recv.at[k], **to_slide(partner)))
        to_partner[-1].start()

    x_back = []
    for d in range(1, NX):
        x_back.append(pltpu.make_async_remote_copy(
            src_ref=result.at[x, core], dst_ref=result.at[x, core],
            send_sem=x_back_send.at[d - 1], recv_sem=x_back_recv.at[d - 1], **to_slide(x_peers[d - 1] * 2 + core)))
        x_back[-1].start()
    forward(0, x)
    for copy in row_copies:
        copy.wait()
    for d in range(1, NX):
        x_back[d - 1].wait_recv()
        forward(d, (x + NX - d) % NX)
    for copy in x_back:
        copy.wait_send()
    for u in range(UNITS):
        @pl.when(me == owners[u])
        def _():
            for d in range(1, PEERS):
                back_copy(u, d).wait_send()
    for copy in to_partner:
        copy.wait()


def finish_kernel(where_ref, result, landed, embed_ref, gk_ref, gg_ref, gi_out, go_out):
    for j in range(WORK):
        embed_ref[j:j + 1, :] = landed[where_ref[j], pl.ds(where_ref[WORK + j], 1), :]
    for s in range(4):
        gi_out[:, s * C:(s + 1) * C] = result[s // 2, s % 2, 0:16].reshape(C, C)
        go_out[s * C:(s + 1) * C, :] = result[2 + s // 2, s % 2, 0:16].reshape(C, C)
    gk_ref[0:8, :] = result[0, 0, 16]
    gk_ref[8:9, :] = result[0, 1, 16, 0:1]
    gg_ref[...] = result[0, 1, 16, 1:2]


def reduce(where, rows, go, gi, small):
    dma = pltpu.SemaphoreType.DMA
    f32 = jnp.float32
    vmem = pl.BlockSpec(memory_space=pltpu.VMEM)
    result, landed = pl.pallas_call(
        reduce_kernel,
        in_specs=[vmem] * 4,
        out_specs=[vmem] * 2,
        out_shape=[
            jax.ShapeDtypeStruct((NX, 2, UNITS, 8, C), f32),
            jax.ShapeDtypeStruct((PEERS, 2, C), f32),
        ],
        scratch_shapes=[
            pltpu.VMEM((NX, 2, UNITS, 8, C), f32),
            pltpu.VMEM((NX, UNITS, 8, C), f32),
            pltpu.VMEM((NX, UNITS, 8, C), f32),
            pltpu.VMEM((NX - 1, UNITS, 8, C), f32),
            pltpu.VMEM((UNITS, 8, C), f32),
            pltpu.VMEM((PEERS, 8, C), f32),
            dma((PEERS - 1,)), dma((PEERS - 1,)), dma, dma, dma((NX - 1,)), dma((NX - 1,)),
            dma((UNITS,)), dma((PEERS,)), dma((PEERS - 1,)), dma((UNITS,)),
            dma((NX - 1,)), dma((NX - 1,)), dma((NX,)), dma((NX,)),
        ],
        compiler_params=pltpu.CompilerParams(
            collective_id=1, has_side_effects=True, vmem_limit_bytes=32 << 20),
        name="reduce",
    )(rows, go, gi, small)
    return pl.pallas_call(
        finish_kernel,
        in_specs=[pl.BlockSpec(memory_space=pltpu.SMEM), vmem, vmem],
        out_specs=[vmem] * 5,
        out_shape=[
            jax.ShapeDtypeStruct((WORK, C), f32),
            jax.ShapeDtypeStruct((9, C), f32),
            jax.ShapeDtypeStruct((1, C), f32),
            jax.ShapeDtypeStruct((C, HID), f32),
            jax.ShapeDtypeStruct((HID, C), f32),
        ],
        compiler_params=pltpu.CompilerParams(vmem_limit_bytes=16 << 20),
        name="finish",
    )(where, result, landed)


def local(features, tissue_count, neighbors, worker_perm, rotation, kernel, gain, w_in, w_out, cotangent):
    feat = features[0]
    strips, rows, counts = exchange(tissue_count, worker_perm, rotation, feat, cotangent[0])
    rows = rows.reshape(PEERS, 2, C)
    peers = lax.axis_size("tile")
    left = lax.ppermute(strips, "tile", [(i, i + 1) for i in range(peers - 1)])
    right = lax.ppermute(strips, "tile", [(i + 1, i) for i in range(peers - 1)])
    sums = inner(counts, worker_perm[0], rotation, feat, rows, kernel, gain[None], w_in, w_out)
    send, go, gi, small, where = border(
        neighbors[0].T, counts, worker_perm[0], rotation, feat, left, strips, right, gain[None], w_in, w_out, sums)
    embed, grad_kernel, grad_gain, grad_in, grad_out = reduce(where, send, go, gi, small)
    return embed[None], grad_kernel, grad_gain[0], grad_in, grad_out


def solution(mesh):
    placed = (
        P("slide", "tile", None, None, None),
        P("slide", "tile"),
        P("slide", "tile", None),
        P("slide", None),
        P("slide"),
        P(),
        P(),
        P(),
        P(),
        P("slide", "tile", None),
    )
    return jax.shard_map(
        local,
        mesh=mesh,
        in_specs=placed,
        out_specs=(P("slide", "tile", None), P(), P(), P(), P()),
        check_vma=False,
    )
```

```python
import functools

import jax
import jax.numpy as jnp
from jax import lax
from jax.experimental import pallas as pl
from jax.experimental.pallas import tpu as pltpu
from jax.sharding import PartitionSpec as P

C = 128
HID = 512
S = 16
W = S + 2
G = 8
SLOTS = 64
WORK = 32
PEERS = 32
NZ, NY = 8, 4
NX = 4
GROUP_TOTAL = PEERS * WORK
MESH = pl.DeviceIdType.MESH
HIGHEST = lax.Precision.HIGHEST


def to_tile(index):
    return dict(device_id={"tile": index}, device_id_type=MESH)


def to_slide(index):
    return dict(device_id={"slide": index}, device_id_type=MESH)


def exchange_kernel(count_ref, perm_hbm, turn_hbm, feat_hbm, cot_ref, strips_ref, rows_ref, table_ref,
                    perm_ref, turn_ref, small_sem, feat_ref, wide, own_count, count_all, count_smem, z_rows, outgoing, feat_sem,
                    count_send, count_recv, send_z, recv_z, send_y, recv_y, smem_sem):
    me = lax.axis_index("tile")
    y, z = me // NZ, me % NZ
    z_peers = [y * NZ + (z + d) % NZ for d in range(1, NZ)]
    y_peers = [((y + d) % NY) * NZ + z for d in range(1, NY)]

    barrier = pltpu.get_barrier_semaphore()
    everyone = [(me + d) % PEERS for d in range(1, PEERS)]
    for peer in everyone:
        pl.semaphore_signal(barrier, inc=1, **to_tile(peer))
    quarter = SLOTS // 4
    feat_copies = [
        pltpu.make_async_copy(feat_hbm.at[pl.ds(q * quarter, quarter)], feat_ref.at[pl.ds(q * quarter, quarter)],
                              feat_sem.at[q])
        for q in range(4)
    ]
    small_copies = [
        pltpu.make_async_copy(perm_hbm, perm_ref, small_sem.at[0]),
        pltpu.make_async_copy(turn_hbm, turn_ref, small_sem.at[1]),
    ]
    for copy in small_copies + feat_copies:
        copy.start()
    own_count[...] = jnp.broadcast_to(count_ref[...], (1, C))
    pl.semaphore_wait(barrier, PEERS - 1)

    def remote(src, dst, send, recv, d, peer):
        return pltpu.make_async_remote_copy(
            src_ref=src, dst_ref=dst, send_sem=send.at[d - 1], recv_sem=recv.at[d - 1], **to_tile(peer))

    count_copies = [
        remote(own_count, count_all.at[y, z], count_send, count_recv, d, everyone[d - 1]) for d in range(1, PEERS)
    ]
    rows_z = [remote(cot_ref, z_rows.at[z], send_z, recv_z, d, z_peers[d - 1]) for d in range(1, NZ)]
    for copy in count_copies + rows_z:
        copy.start()
    count_all[y, z] = own_count[...]
    z_rows[z] = cot_ref[...]

    def one(t, _):
        strips_ref[t, 0] = feat_ref[t, 0]
        strips_ref[t, 1] = feat_ref[t, S - 1]
        for row in range(S):
            wide[pl.ds(row * S, S), :] = feat_ref[t, row].astype(jnp.float32)
        strips_ref[t, 2] = wide[pl.ds(0, S, stride=S), :].astype(jnp.bfloat16)
        strips_ref[t, 3] = wide[pl.ds(S - 1, S, stride=S), :].astype(jnp.bfloat16)
        return 0

    def strips_of(q):
        feat_copies[q].wait()
        lax.fori_loop(q * quarter, (q + 1) * quarter, one, 0)

    strips_of(0)
    strips_of(1)
    strips_of(2)

    for copy in small_copies:
        copy.wait()

    def find(r, places):
        return tuple(jnp.where(perm_ref[0, r] == y * NZ + k, r, place) for k, place in enumerate(places))

    places = lax.fori_loop(0, PEERS, find, (jnp.int32(0),) * NZ)
    for copy in count_copies:
        copy.wait_recv()
    to_smem = pltpu.make_async_copy(count_all, count_smem, smem_sem)
    to_smem.start()
    to_smem.wait()
    turn = turn_ref[0]
    for q in range(PEERS):
        table_ref[q] = count_smem[q // NZ, q % NZ, 0, 0]
        table_ref[PEERS + q] = perm_ref[0, q]
    table_ref[2 * PEERS] = turn
    for copy in rows_z:
        copy.wait_recv()

    def pick(owner, store):
        start = lax.fori_loop(
            0, PEERS, lambda q, t: t + jnp.where(q < owner, count_smem[q // NZ, q % NZ, 0, 0], 0), jnp.int32(0))
        for k in range(NZ):
            slot = (places[k] - start - turn) & (PEERS - 1)
            for j in range(2):
                rank = (start + slot + j * PEERS + turn) & (GROUP_TOTAL - 1)
                store(k, j, z_rows[k, pl.ds(rank >> 5, 1), :])

    rows_y = []
    for d in range(1, NY):
        def store(k, j, row):
            outgoing[d - 1, k, j:j + 1, :] = row

        pick(y_peers[d - 1], store)
        rows_y.append(remote(outgoing.at[d - 1], rows_ref.at[y], send_y, recv_y, d, y_peers[d - 1]))
        rows_y[-1].start()

    def keep(k, j, row):
        rows_ref[y, k, j:j + 1, :] = row

    pick(me, keep)
    strips_of(3)
    for copy in count_copies + rows_z:
        copy.wait_send()
    for copy in rows_y:
        copy.wait()


def exchange(count, perm, turn, feat, cot):
    dma = pltpu.SemaphoreType.DMA
    vmem = pl.BlockSpec(memory_space=pltpu.VMEM)
    smem = pl.BlockSpec(memory_space=pltpu.SMEM)
    f32, i32 = jnp.float32, jnp.int32
    return pl.pallas_call(
        exchange_kernel,
        in_specs=[vmem] + [pl.BlockSpec(memory_space=pl.ANY)] * 3 + [vmem],
        out_specs=[vmem, vmem, smem],
        out_shape=[
            jax.ShapeDtypeStruct((SLOTS, 4, S, C), jnp.bfloat16),
            jax.ShapeDtypeStruct((NY, NZ, 2, C), f32),
            jax.ShapeDtypeStruct((2 * PEERS + 8,), i32),
        ],
        scratch_shapes=[
            pltpu.SMEM((1, PEERS), i32),
            pltpu.SMEM((1,), i32),
            dma((2,)),
            pltpu.VMEM((SLOTS, S, S, C), jnp.bfloat16),
            pltpu.VMEM((S * S, C), f32),
            pltpu.VMEM((1, C), i32),
            pltpu.VMEM((NY, NZ, 1, C), i32),
            pltpu.SMEM((NY, NZ, 1, C), i32),
            pltpu.VMEM((NZ, WORK, C), f32),
            pltpu.VMEM((NY - 1, NZ, 2, C), f32),
            dma((4,)), dma((PEERS - 1,)), dma((PEERS - 1,)),
            dma((NZ - 1,)), dma((NZ - 1,)), dma((NY - 1,)), dma((NY - 1,)), dma,
        ],
        compiler_params=pltpu.CompilerParams(
            collective_id=0, has_side_effects=True, vmem_limit_bytes=56 << 20),
        name="exchange",
    )(count, perm, turn, feat, cot)


def start_of(counts_ref, owner):
    return lax.fori_loop(0, owner, lambda q, s: s + counts_ref[q], jnp.int32(0))


def fill_centre(pad, feat_ref, t, u):
    for y in range(S):
        pad[pl.ds(((y + 1) * W + 1) * G + t, S, stride=G), :] = feat_ref[u, y].astype(jnp.float32)


def pixel_math(windows, pixels, together, slope_scales, taps, gain, w_in_ref, gi_ref, gk, gg):
    n = pixels * G
    half = HID // 2
    sub = lax.broadcasted_iota(jnp.int32, (G, n), 0)
    col = lax.broadcasted_iota(jnp.int32, (G, n), 1)
    select = jnp.where((col & (G - 1)) == sub, 1.0, 0.0).astype(jnp.bfloat16)

    def norm(window):
        depth, centre = None, None
        for a in range(3):
            for b in range(3):
                x = window(a, b)
                if a == 1 and b == 1:
                    centre = jnp.sum(x, axis=0)
                term = x * taps[3 * a + b][None]
                depth = term if depth is None else depth + term
        depth = depth.reshape(n, C)
        centered = depth - jnp.mean(depth, axis=1, keepdims=True)
        inverse = lax.rsqrt(jnp.mean(centered * centered, axis=1, keepdims=True) + 1e-06)
        unit = centered * inverse
        return centre, inverse, unit, (unit * gain).astype(jnp.bfloat16)

    def hidden(normed, slope_scale):
        acts, grads = [], []
        for h in range(0, HID, half):
            v = jnp.dot(normed, w_in_ref[:, h:h + half], preferred_element_type=jnp.float32)
            share = 0.5 * (1.0 + lax.erf(v * 0.7071067811865476))
            slope = share + v * (jnp.exp(-0.5 * v * v) * 0.3989422804014327)
            acts.append((v * share).astype(jnp.bfloat16))
            scaled = slope.reshape(pixels, G, half) * slope_scale[None, :, h:h + half]
            grads.append(scaled.reshape(n, half).astype(jnp.bfloat16))
        return jnp.concatenate(acts, axis=1), jnp.concatenate(grads, axis=1)

    def back(window, inverse, unit, acts, grad_before):
        act_sum = jnp.dot(select, acts, preferred_element_type=jnp.float32)
        grad_normed = lax.dot_general(grad_before, w_in_ref[...], (((1,), (1,)), ((), ())),
                                      preferred_element_type=jnp.float32)
        product = grad_normed * unit
        gg[...] += jnp.sum(product.reshape(pixels, G, C), axis=0)
        grad_unit = grad_normed * gain
        grad_depth = inverse * (
            grad_unit
            - jnp.mean(grad_unit, axis=1, keepdims=True)
            - unit * jnp.mean(product * gain, axis=1, keepdims=True)
        )
        grad_depth = grad_depth.reshape(pixels, G, C)
        for a in range(3):
            for b in range(3):
                gk[3 * a + b] += jnp.sum(grad_depth * window(a, b), axis=0)
        return act_sum

    count = len(windows)
    normal, wide, sums = {}, {}, []
    for i in range(count + 2):
        if i >= 2:
            k = i - 2
            sums.append((back(windows[k], normal[k][1], normal[k][2], *wide[k]), normal[k][0]))
        if 1 <= i <= count:
            wide[i - 1] = hidden(normal[i - 1][3], slope_scales[i - 1])
        if i < count:
            normal[i] = norm(windows[i])
        if i >= 2 and (i - 1) % together == 0:
            ks = range(i - 1 - together, i - 1)
            gi_ref[...] += lax.dot_general(
                jnp.concatenate([normal[k][3] for k in ks], axis=0), jnp.concatenate([wide[k][1] for k in ks], axis=0),
                (((0,), (0,)), ((), ())), preferred_element_type=jnp.float32)
    return sums


def inner_kernel(table_ref, feat_ref, rows_hbm, taps_ref, gain_ref, w_in_hbm, w_out_hbm,
                 ge, ga, act, cen, gi_ref, gk, gg, taps, pad, rows_ref, w_in_ref, w_out_ref, sems):
    g = pl.program_id(0)
    me = lax.axis_index("tile")
    count = table_ref[me]

    @pl.when(g == 0)
    def _():
        copies = [
            pltpu.make_async_copy(src, dst, sems.at[k])
            for k, (src, dst) in enumerate(((rows_hbm, rows_ref), (w_out_hbm, w_out_ref), (w_in_hbm, w_in_ref)))
        ]
        for copy in copies:
            copy.start()
        for ref in (gk, gg, gi_ref, act, cen, ge):
            ref[...] = jnp.zeros_like(ref)
        for k in range(9):
            taps[k] = jnp.broadcast_to(taps_ref[k:k + 1, :].astype(jnp.float32), (G, C))
        first = start_of(table_ref, me) + table_ref[2 * PEERS]
        for copy in copies:
            copy.wait()

        def row(i, _):
            rank = (first + i) & (GROUP_TOTAL - 1)
            worker = table_ref[PEERS + (rank & (PEERS - 1))]
            ge[pl.ds(i, 1), :] = rows_ref[worker, pl.ds(i >> 5, 1), :] * (1.0 / (S * S))
            return 0

        lax.fori_loop(0, count, row, 0)
        ga[...] = lax.dot_general(ge[...], w_out_ref[...].astype(jnp.float32), (((1,), (1,)), ((), ())),
                                  precision=HIGHEST, preferred_element_type=jnp.float32)

    @pl.when(g * G < count)
    def _():
        for t in range(G):
            fill_centre(pad, feat_ref, t, t)
        side = S - 2

        lines = 14

        def window_of(top):
            def window(a, b):
                rows = [pad[pl.ds(((y + a) * W + 1 + b) * G, side * G), :] for y in range(top, top + lines)]
                return jnp.concatenate(rows, axis=0).reshape(lines * side, G, C)
            return window

        mine = pl.ds(pl.multiple_of(g * G, G), G)
        windows = [window_of(top) for top in range(1, S - 1, lines)]
        scale = ga[mine, :]
        sums = pixel_math(windows, lines * side, 1, [scale] * len(windows), taps, gain_ref[...], w_in_ref,
                          gi_ref, gk, gg)
        act[mine, :] = sum(part[0] for part in sums)
        cen[mine, :] = sum(part[1] for part in sums)


def whole(x):
    return pl.BlockSpec(x.shape, lambda g, *_: (0,) * len(x.shape))


def inner(table, feat, rows, taps, gain, w_in, w_out):
    f32 = jnp.float32
    outs = [
        jax.ShapeDtypeStruct(shape, f32)
        for shape in ((SLOTS, C), (SLOTS, HID), (SLOTS, HID), (SLOTS, C), (C, HID), (9, G, C), (G, C), (9, G, C))
    ]
    grid_spec = pltpu.PrefetchScalarGridSpec(
        num_scalar_prefetch=1,
        grid=(SLOTS // G,),
        in_specs=[pl.BlockSpec((G, S, S, C), lambda g, *_: (g, 0, 0, 0))]
        + [pl.BlockSpec(memory_space=pltpu.HBM), whole(taps), whole(gain)]
        + [pl.BlockSpec(memory_space=pltpu.HBM)] * 2,
        out_specs=[whole(x) for x in outs],
        scratch_shapes=[
            pltpu.VMEM((W * W * G, C), f32),
            pltpu.VMEM(rows.shape, f32),
            pltpu.VMEM(w_in.shape, jnp.bfloat16),
            pltpu.VMEM(w_out.shape, jnp.bfloat16),
            pltpu.SemaphoreType.DMA((3,)),
        ],
    )
    return pl.pallas_call(
        inner_kernel,
        grid_spec=grid_spec,
        out_shape=outs,
        compiler_params=pltpu.CompilerParams(vmem_limit_bytes=40 << 20),
        cost_estimate=pl.CostEstimate(flops=10_000_000_000, bytes_accessed=100_000_000, transcendentals=0),
        name="inner",
    )(table, feat, rows, taps, gain, w_in, w_out)


PAIR = 4


def border_kernel(nb_ref, table_ref, feat_ref, left_ref, own_ref, right_ref, gain_ref, w_in_ref,
                  w_out_ref, ge, ga, act_in, cen_in, gi_in, gk_in, gg_in, taps,
                  send_ref, go_ref, gi_ref, small_ref, where_ref, pad, strips, act, cen, gk, gg, sems):
    g = pl.program_id(0)
    me = lax.axis_index("tile")
    count = table_ref[me]
    turn = table_ref[2 * PEERS]
    base = (me - 1) * SLOTS

    @pl.when(g == 0)
    def _():
        copies = [
            pltpu.make_async_copy(ref, strips.at[pl.ds(k * SLOTS, SLOTS)], sems.at[k])
            for k, ref in enumerate((left_ref, own_ref, right_ref))
        ]
        for copy in copies:
            copy.start()
        for ref, old in ((act, act_in), (cen, cen_in), (gi_ref, gi_in), (gk, gk_in), (gg, gg_in)):
            ref[...] = old[...]
        for copy in copies:
            copy.wait()

    @pl.when(g * PAIR * G < count)
    def _():
        for t in range(PAIR * G):
            pair_pad = pad.at[t // G]
            u = t % G
            fill_centre(pair_pad, feat_ref, u, t)

            def strip(k, which):
                n = nb_ref[k, g * PAIR * G + t]
                ok = n >= 0
                x = strips[jnp.where(ok, n - base, 0), which].astype(jnp.float32)
                return jnp.where(ok, x, 0.0)

            pair_pad[pl.ds(1 * G + u, S, stride=G), :] = strip(0, 1)
            pair_pad[pl.ds(((S + 1) * W + 1) * G + u, S, stride=G), :] = strip(1, 0)
            pair_pad[pl.ds(W * G + u, S, stride=G * W), :] = strip(2, 3)
            pair_pad[pl.ds((W + S + 1) * G + u, S, stride=G * W), :] = strip(3, 2)
            pair_pad[pl.ds(u, 1), :] = strip(4, 1)[S - 1:S]
            pair_pad[pl.ds((S + 1) * G + u, 1), :] = strip(5, 1)[0:1]
            pair_pad[pl.ds((S + 1) * W * G + u, 1), :] = strip(6, 0)[S - 1:S]
            pair_pad[pl.ds(((S + 1) * W + S + 1) * G + u, 1), :] = strip(7, 0)[0:1]

        def window_of(p):
            def window(a, b):
                part = pad.at[p]
                rows = [part[pl.ds(((y + a) * W + b) * G, S * G), :] for y in (0, S - 1)]
                for x in (0, S - 1):
                    rows += [part[pl.ds(((y + a) * W + x + b) * G, G), :] for y in range(1, S - 1)]
                return jnp.concatenate(rows, axis=0).reshape(4 * S - 4, G, C)
            return window

        spans = [pl.ds(pl.multiple_of((g * PAIR + p) * G, G), G) for p in range(PAIR)]
        sums = pixel_math([window_of(p) for p in range(PAIR)], 4 * S - 4, 2, [ga[span, :] for span in spans],
                          taps, gain_ref[...], w_in_ref, gi_ref, gk, gg)
        for span, (act_sum, centre) in zip(spans, sums):
            act[span, :] += act_sum
            cen[span, :] += centre

    @pl.when(g == pl.num_programs(0) - 1)
    def _():
        go_ref[...] = lax.dot_general(act[...], ge[...], (((0,), (0,)), ((), ())),
                                      precision=HIGHEST, preferred_element_type=jnp.float32)
        embed = jnp.dot(act[...], w_out_ref[...].astype(jnp.float32), precision=HIGHEST,
                        preferred_element_type=jnp.float32)
        cen[...] = (cen[...] + embed) * (1.0 / (S * S))
        small_ref[...] = jnp.zeros_like(small_ref)
        for k in range(9):
            small_ref[k:k + 1, :] = jnp.sum(gk[k], axis=0, keepdims=True)
        small_ref[9:10, :] = jnp.sum(gg[...], axis=0, keepdims=True)
        send_ref[...] = jnp.zeros_like(send_ref)
        first = start_of(table_ref, me) + turn

        def out_row(i, _):
            rank = (first + i) & (GROUP_TOTAL - 1)
            worker = table_ref[PEERS + (rank & (PEERS - 1))]
            send_ref[worker, pl.ds(i >> 5, 1), :] = cen[pl.ds(i, 1), :]
            return 0

        lax.fori_loop(0, count, out_row, 0)
        residue = lax.fori_loop(0, PEERS, lambda r, s: jnp.where(table_ref[PEERS + r] == me, r, s), jnp.int32(0))

        def arrival(owner, start):
            slot = (residue - start - turn) & (PEERS - 1)
            for k in range(2):
                @pl.when(slot + k * PEERS < table_ref[owner])
                def _():
                    place = ((start + slot + k * PEERS + turn) & (GROUP_TOTAL - 1)) >> 5
                    where_ref[place] = owner
                    where_ref[WORK + place] = k
            return start + table_ref[owner]

        lax.fori_loop(0, PEERS, arrival, jnp.int32(0))


def border(nb, table, feat, left, own, right, gain, w_in, w_out, sums):
    f32 = jnp.float32
    outs = [jax.ShapeDtypeStruct(shape, f32) for shape in ((PEERS, 2, C), (HID, C), (C, HID), (16, C))]
    grid_spec = pltpu.PrefetchScalarGridSpec(
        num_scalar_prefetch=2,
        grid=(SLOTS // (PAIR * G),),
        in_specs=[pl.BlockSpec((PAIR * G, S, S, C), lambda g, *_: (g, 0, 0, 0))]
        + [pl.BlockSpec(memory_space=pl.ANY)] * 3
        + [whole(x) for x in (gain, w_in, w_out, *sums)],
        out_specs=[whole(x) for x in outs] + [pl.BlockSpec(memory_space=pltpu.SMEM)],
        scratch_shapes=[
            pltpu.VMEM((PAIR, W * W * G, C), f32),
            pltpu.VMEM((3 * SLOTS, 4, S, C), jnp.bfloat16),
            pltpu.VMEM((SLOTS, HID), f32),
            pltpu.VMEM((SLOTS, C), f32),
            pltpu.VMEM((9, G, C), f32),
            pltpu.VMEM((G, C), f32),
            pltpu.SemaphoreType.DMA((3,)),
        ],
    )
    return pl.pallas_call(
        border_kernel,
        grid_spec=grid_spec,
        out_shape=outs + [jax.ShapeDtypeStruct((2 * WORK,), jnp.int32)],
        compiler_params=pltpu.CompilerParams(vmem_limit_bytes=40 << 20),
        name="border",
    )(nb, table, feat, left, own, right, gain, w_in, w_out, *sums)


UNITS = 17


def reduce_kernel(rows_ref, go_ref, gi_ref, small_ref, result, landed,
                  full, from_core, half, from_x, piece, from_tile,
                  row_send, row_recv, core_send, core_recv, x_send, x_recv, unit_send, unit_recv,
                  back_send, back_recv, x_back_send, x_back_recv, core_back_send, core_back_recv):
    me = lax.axis_index("tile")
    slide = lax.axis_index("slide")
    x, core = slide // 2, slide % 2
    partner = x * 2 + (1 - core)
    x_peers = [((x + d) % NX) for d in range(1, NX)]

    barrier = pltpu.get_barrier_semaphore()
    for d in range(1, PEERS):
        pl.semaphore_signal(barrier, inc=1, **to_tile((me + d) % PEERS))
    pl.semaphore_signal(barrier, inc=1, **to_slide(partner))
    for peer in x_peers:
        pl.semaphore_signal(barrier, inc=1, **to_slide(peer * 2 + core))

    for s in range(4):
        full[s // 2, s % 2, 0:16] = gi_ref[:, s * C:(s + 1) * C].reshape(16, 8, C)
        full[2 + s // 2, s % 2, 0:16] = go_ref[s * C:(s + 1) * C, :].reshape(16, 8, C)
    for s in range(8):
        full[s // 2, s % 2, 16] = small_ref[8 * s:8 * s + 8, :] if s < 2 else jnp.zeros((8, C), jnp.float32)

    pl.semaphore_wait(barrier, PEERS + NX - 1)

    to_core = pltpu.make_async_remote_copy(
        src_ref=full.at[:, 1 - core], dst_ref=from_core, send_sem=core_send, recv_sem=core_recv, **to_slide(partner))
    to_core.start()
    to_core.wait()
    half[...] = full[:, core] + from_core[...]

    x_copies = []
    for d in range(1, NX):
        x_copies.append(pltpu.make_async_remote_copy(
            src_ref=half.at[x_peers[d - 1]], dst_ref=from_x.at[d - 1],
            send_sem=x_send.at[d - 1], recv_sem=x_recv.at[d - 1], **to_slide(x_peers[d - 1] * 2 + core)))
        x_copies[-1].start()
    row_copies = []
    for d in range(1, PEERS):
        peer = (me + d) % PEERS
        row_copies.append(pltpu.make_async_remote_copy(
            src_ref=rows_ref.at[peer], dst_ref=landed.at[me],
            send_sem=row_send.at[d - 1], recv_sem=row_recv.at[d - 1], **to_tile(peer)))
        row_copies[-1].start()
    landed[me] = rows_ref[me]
    for copy in x_copies:
        copy.wait()
    piece[...] = half[x] + from_x[0] + from_x[1] + from_x[2]

    owners = [2 * u for u in range(16)] + [1]

    def unit_copy(u):
        return pltpu.make_async_remote_copy(
            src_ref=piece.at[u], dst_ref=from_tile.at[me],
            send_sem=unit_send.at[u], recv_sem=unit_recv.at[me], **to_tile(owners[u]))

    def back_copy(u, d):
        return pltpu.make_async_remote_copy(
            src_ref=result.at[x, core, u], dst_ref=result.at[x, core, u],
            send_sem=back_send.at[d - 1], recv_sem=back_recv.at[u], **to_tile((me + d) % PEERS))

    for u in range(UNITS):
        @pl.when(me != owners[u])
        def _():
            unit_copy(u).start()
    for u in range(UNITS):
        @pl.when(me == owners[u])
        def _():
            from_tile[owners[u]] = piece[u]
            for q in range(PEERS):
                if q != owners[u]:
                    pltpu.make_async_remote_copy(
                        src_ref=piece.at[u], dst_ref=from_tile.at[q],
                        send_sem=unit_send.at[u], recv_sem=unit_recv.at[q], **to_tile(q)).wait_recv()
            result[x, core, u] = jnp.sum(from_tile[...], axis=0)
            for d in range(1, PEERS):
                back_copy(u, d).start()
    for u in range(UNITS):
        @pl.when(me != owners[u])
        def _():
            unit_copy(u).wait_send()
            back_copy(u, 1).wait_recv()

    to_partner = []

    def forward(k, where):
        to_partner.append(pltpu.make_async_remote_copy(
            src_ref=result.at[where, core], dst_ref=result.at[where, core],
            send_sem=core_back_send.at[k], recv_sem=core_back_recv.at[k], **to_slide(partner)))
        to_partner[-1].start()

    x_back = []
    for d in range(1, NX):
        x_back.append(pltpu.make_async_remote_copy(
            src_ref=result.at[x, core], dst_ref=result.at[x, core],
            send_sem=x_back_send.at[d - 1], recv_sem=x_back_recv.at[d - 1], **to_slide(x_peers[d - 1] * 2 + core)))
        x_back[-1].start()
    forward(0, x)
    for copy in row_copies:
        copy.wait()
    for d in range(1, NX):
        x_back[d - 1].wait_recv()
        forward(d, (x + NX - d) % NX)
    for copy in x_back:
        copy.wait_send()
    for u in range(UNITS):
        @pl.when(me == owners[u])
        def _():
            for d in range(1, PEERS):
                back_copy(u, d).wait_send()
    for copy in to_partner:
        copy.wait()


def finish_kernel(where_ref, result, landed, embed_ref, gk_ref, gg_ref, gi_out, go_out):
    for j in range(WORK):
        embed_ref[j:j + 1, :] = landed[where_ref[j], pl.ds(where_ref[WORK + j], 1), :]
    for s in range(4):
        gi_out[:, s * C:(s + 1) * C] = result[s // 2, s % 2, 0:16].reshape(C, C)
        go_out[s * C:(s + 1) * C, :] = result[2 + s // 2, s % 2, 0:16].reshape(C, C)
    gk_ref[0:8, :] = result[0, 0, 16]
    gk_ref[8:9, :] = result[0, 1, 16, 0:1]
    gg_ref[...] = result[0, 1, 16, 1:2]


def reduce(where, rows, go, gi, small):
    dma = pltpu.SemaphoreType.DMA
    f32 = jnp.float32
    vmem = pl.BlockSpec(memory_space=pltpu.VMEM)
    result, landed = pl.pallas_call(
        reduce_kernel,
        in_specs=[vmem] * 4,
        out_specs=[vmem] * 2,
        out_shape=[
            jax.ShapeDtypeStruct((NX, 2, UNITS, 8, C), f32),
            jax.ShapeDtypeStruct((PEERS, 2, C), f32),
        ],
        scratch_shapes=[
            pltpu.VMEM((NX, 2, UNITS, 8, C), f32),
            pltpu.VMEM((NX, UNITS, 8, C), f32),
            pltpu.VMEM((NX, UNITS, 8, C), f32),
            pltpu.VMEM((NX - 1, UNITS, 8, C), f32),
            pltpu.VMEM((UNITS, 8, C), f32),
            pltpu.VMEM((PEERS, 8, C), f32),
            dma((PEERS - 1,)), dma((PEERS - 1,)), dma, dma, dma((NX - 1,)), dma((NX - 1,)),
            dma((UNITS,)), dma((PEERS,)), dma((PEERS - 1,)), dma((UNITS,)),
            dma((NX - 1,)), dma((NX - 1,)), dma((NX,)), dma((NX,)),
        ],
        compiler_params=pltpu.CompilerParams(
            collective_id=1, has_side_effects=True, vmem_limit_bytes=32 << 20),
        name="reduce",
    )(rows, go, gi, small)
    return pl.pallas_call(
        finish_kernel,
        in_specs=[pl.BlockSpec(memory_space=pltpu.SMEM), vmem, vmem],
        out_specs=[vmem] * 5,
        out_shape=[
            jax.ShapeDtypeStruct((WORK, C), f32),
            jax.ShapeDtypeStruct((9, C), f32),
            jax.ShapeDtypeStruct((1, C), f32),
            jax.ShapeDtypeStruct((C, HID), f32),
            jax.ShapeDtypeStruct((HID, C), f32),
        ],
        compiler_params=pltpu.CompilerParams(vmem_limit_bytes=16 << 20),
        name="finish",
    )(where, result, landed)


def local(features, tissue_count, neighbors, worker_perm, rotation, kernel, gain, w_in, w_out, cotangent):
    feat = features[0]
    strips, rows, table = exchange(tissue_count, worker_perm, rotation, feat, cotangent[0])
    rows = rows.reshape(PEERS, 2, C)
    peers = lax.axis_size("tile")
    left = lax.ppermute(strips, "tile", [(i, i + 1) for i in range(peers - 1)])
    right = lax.ppermute(strips, "tile", [(i + 1, i) for i in range(peers - 1)])
    sums = inner(table, feat, rows, kernel, gain[None], w_in, w_out)
    send, go, gi, small, where = border(
        neighbors[0].T, table, feat, left, strips, right, gain[None], w_in, w_out, sums)
    embed, grad_kernel, grad_gain, grad_in, grad_out = reduce(where, send, go, gi, small)
    return embed[None], grad_kernel, grad_gain[0], grad_in, grad_out


def solution(mesh):
    placed = (
        P("slide", "tile", None, None, None),
        P("slide", "tile"),
        P("slide", "tile", None),
        P("slide", None),
        P("slide"),
        P(),
        P(),
        P(),
        P(),
        P("slide", "tile", None),
    )
    return jax.shard_map(
        local,
        mesh=mesh,
        in_specs=placed,
        out_specs=(P("slide", "tile", None), P(), P(), P(), P()),
        check_vma=False,
    )
```

```python
import functools

import jax
import jax.numpy as jnp
from jax import lax
from jax.experimental import pallas as pl
from jax.experimental.pallas import tpu as pltpu
from jax.sharding import PartitionSpec as P

C = 128
HID = 512
S = 16
W = S + 2
G = 8
SLOTS = 64
WORK = 32
PEERS = 32
NZ, NY = 8, 4
NX = 4
GROUP_TOTAL = PEERS * WORK
MESH = pl.DeviceIdType.MESH
HIGHEST = lax.Precision.HIGHEST


def to_tile(index):
    return dict(device_id={"tile": index}, device_id_type=MESH)


def to_slide(index):
    return dict(device_id={"slide": index}, device_id_type=MESH)


def exchange_kernel(count_ref, perm_hbm, turn_hbm, feat_hbm, cot_ref, strips_ref, rows_ref, table_ref,
                    perm_ref, turn_ref, small_sem, feat_ref, wide, own_count, count_all, count_smem, z_rows, outgoing, feat_sem,
                    count_send, count_recv, send_z, recv_z, send_y, recv_y, smem_sem):
    me = lax.axis_index("tile")
    y, z = me // NZ, me % NZ
    z_peers = [y * NZ + (z + d) % NZ for d in range(1, NZ)]
    y_peers = [((y + d) % NY) * NZ + z for d in range(1, NY)]

    barrier = pltpu.get_barrier_semaphore()
    everyone = [(me + d) % PEERS for d in range(1, PEERS)]
    for peer in everyone:
        pl.semaphore_signal(barrier, inc=1, **to_tile(peer))
    quarter = SLOTS // 4
    feat_copies = [
        pltpu.make_async_copy(feat_hbm.at[pl.ds(q * quarter, quarter)], feat_ref.at[pl.ds(q * quarter, quarter)],
                              feat_sem.at[q])
        for q in range(4)
    ]
    small_copies = [
        pltpu.make_async_copy(perm_hbm, perm_ref, small_sem.at[0]),
        pltpu.make_async_copy(turn_hbm, turn_ref, small_sem.at[1]),
    ]
    for copy in small_copies + feat_copies:
        copy.start()
    own_count[...] = jnp.broadcast_to(count_ref[...], (1, C))
    pl.semaphore_wait(barrier, PEERS - 1)

    def remote(src, dst, send, recv, d, peer):
        return pltpu.make_async_remote_copy(
            src_ref=src, dst_ref=dst, send_sem=send.at[d - 1], recv_sem=recv.at[d - 1], **to_tile(peer))

    count_copies = [
        remote(own_count, count_all.at[y, z], count_send, count_recv, d, everyone[d - 1]) for d in range(1, PEERS)
    ]
    rows_z = [remote(cot_ref, z_rows.at[z], send_z, recv_z, d, z_peers[d - 1]) for d in range(1, NZ)]
    for copy in count_copies + rows_z:
        copy.start()
    count_all[y, z] = own_count[...]
    z_rows[z] = cot_ref[...]

    def one(t, _):
        strips_ref[t, 0] = feat_ref[t, 0]
        strips_ref[t, 1] = feat_ref[t, S - 1]
        for row in range(S):
            wide[pl.ds(row * S, S), :] = feat_ref[t, row].astype(jnp.float32)
        strips_ref[t, 2] = wide[pl.ds(0, S, stride=S), :].astype(jnp.bfloat16)
        strips_ref[t, 3] = wide[pl.ds(S - 1, S, stride=S), :].astype(jnp.bfloat16)
        return 0

    def strips_of(q):
        feat_copies[q].wait()
        lax.fori_loop(q * quarter, (q + 1) * quarter, one, 0)

    strips_of(0)
    strips_of(1)
    strips_of(2)

    for copy in small_copies:
        copy.wait()

    def find(r, places):
        return tuple(jnp.where(perm_ref[0, r] == y * NZ + k, r, place) for k, place in enumerate(places))

    places = lax.fori_loop(0, PEERS, find, (jnp.int32(0),) * NZ)
    for copy in count_copies:
        copy.wait_recv()
    to_smem = pltpu.make_async_copy(count_all, count_smem, smem_sem)
    to_smem.start()
    to_smem.wait()
    turn = turn_ref[0]
    for q in range(PEERS):
        table_ref[q] = count_smem[q // NZ, q % NZ, 0, 0]
        table_ref[PEERS + q] = perm_ref[0, q]
    table_ref[2 * PEERS] = turn
    for copy in rows_z:
        copy.wait_recv()

    def pick(owner, store):
        start = lax.fori_loop(
            0, PEERS, lambda q, t: t + jnp.where(q < owner, count_smem[q // NZ, q % NZ, 0, 0], 0), jnp.int32(0))
        for k in range(NZ):
            slot = (places[k] - start - turn) & (PEERS - 1)
            for j in range(2):
                rank = (start + slot + j * PEERS + turn) & (GROUP_TOTAL - 1)
                store(k, j, z_rows[k, pl.ds(rank >> 5, 1), :])

    rows_y = []
    for d in range(1, NY):
        def store(k, j, row):
            outgoing[d - 1, k, j:j + 1, :] = row

        pick(y_peers[d - 1], store)
        rows_y.append(remote(outgoing.at[d - 1], rows_ref.at[y], send_y, recv_y, d, y_peers[d - 1]))
        rows_y[-1].start()

    def keep(k, j, row):
        rows_ref[y, k, j:j + 1, :] = row

    pick(me, keep)
    strips_of(3)
    for copy in count_copies + rows_z:
        copy.wait_send()
    for copy in rows_y:
        copy.wait()


def exchange(count, perm, turn, feat, cot):
    dma = pltpu.SemaphoreType.DMA
    vmem = pl.BlockSpec(memory_space=pltpu.VMEM)
    smem = pl.BlockSpec(memory_space=pltpu.SMEM)
    f32, i32 = jnp.float32, jnp.int32
    return pl.pallas_call(
        exchange_kernel,
        in_specs=[vmem] + [pl.BlockSpec(memory_space=pl.ANY)] * 3 + [vmem],
        out_specs=[vmem, vmem, smem],
        out_shape=[
            jax.ShapeDtypeStruct((SLOTS, 4, S, C), jnp.bfloat16),
            jax.ShapeDtypeStruct((NY, NZ, 2, C), f32),
            jax.ShapeDtypeStruct((2 * PEERS + 8,), i32),
        ],
        scratch_shapes=[
            pltpu.SMEM((1, PEERS), i32),
            pltpu.SMEM((1,), i32),
            dma((2,)),
            pltpu.VMEM((SLOTS, S, S, C), jnp.bfloat16),
            pltpu.VMEM((S * S, C), f32),
            pltpu.VMEM((1, C), i32),
            pltpu.VMEM((NY, NZ, 1, C), i32),
            pltpu.SMEM((NY, NZ, 1, C), i32),
            pltpu.VMEM((NZ, WORK, C), f32),
            pltpu.VMEM((NY - 1, NZ, 2, C), f32),
            dma((4,)), dma((PEERS - 1,)), dma((PEERS - 1,)),
            dma((NZ - 1,)), dma((NZ - 1,)), dma((NY - 1,)), dma((NY - 1,)), dma,
        ],
        compiler_params=pltpu.CompilerParams(
            collective_id=0, has_side_effects=True, vmem_limit_bytes=56 << 20),
        name="exchange",
    )(count, perm, turn, feat, cot)


def start_of(counts_ref, owner):
    return lax.fori_loop(0, owner, lambda q, s: s + counts_ref[q], jnp.int32(0))


def fill_centre(pad, feat_ref, t, u):
    for y in range(S):
        pad[pl.ds(((y + 1) * W + 1) * G + t, S, stride=G), :] = feat_ref[u, y].astype(jnp.float32)


def pixel_math(windows, pixels, together, slope_scales, taps, gain, w_in_ref, gi_ref, gk, gg):
    n = pixels * G
    half = HID // 2
    sub = lax.broadcasted_iota(jnp.int32, (G, n), 0)
    col = lax.broadcasted_iota(jnp.int32, (G, n), 1)
    select = jnp.where((col & (G - 1)) == sub, 1.0, 0.0).astype(jnp.bfloat16)

    def norm(window):
        depth, centre = None, None
        for a in range(3):
            for b in range(3):
                x = window(a, b)
                if a == 1 and b == 1:
                    centre = jnp.sum(x, axis=0)
                term = x * taps[3 * a + b][None]
                depth = term if depth is None else depth + term
        depth = depth.reshape(n, C)
        centered = depth - jnp.mean(depth, axis=1, keepdims=True)
        inverse = lax.rsqrt(jnp.mean(centered * centered, axis=1, keepdims=True) + 1e-06)
        unit = centered * inverse
        return centre, inverse, unit, (unit * gain).astype(jnp.bfloat16)

    def hidden(normed, slope_scale):
        acts, grads = [], []
        for h in range(0, HID, half):
            v = jnp.dot(normed, w_in_ref[:, h:h + half], preferred_element_type=jnp.float32)
            share = 0.5 * (1.0 + lax.erf(v * 0.7071067811865476))
            slope = share + v * (jnp.exp(-0.5 * v * v) * 0.3989422804014327)
            acts.append((v * share).astype(jnp.bfloat16))
            scaled = slope.reshape(pixels, G, half) * slope_scale[None, :, h:h + half]
            grads.append(scaled.reshape(n, half).astype(jnp.bfloat16))
        return jnp.concatenate(acts, axis=1), jnp.concatenate(grads, axis=1)

    def back(window, inverse, unit, acts, grad_before):
        act_sum = jnp.dot(select, acts, preferred_element_type=jnp.float32)
        grad_normed = lax.dot_general(grad_before, w_in_ref[...], (((1,), (1,)), ((), ())),
                                      preferred_element_type=jnp.float32)
        product = grad_normed * unit
        gg[...] += jnp.sum(product.reshape(pixels, G, C), axis=0)
        grad_unit = grad_normed * gain
        grad_depth = inverse * (
            grad_unit
            - jnp.mean(grad_unit, axis=1, keepdims=True)
            - unit * jnp.mean(product * gain, axis=1, keepdims=True)
        )
        grad_depth = grad_depth.reshape(pixels, G, C)
        for a in range(3):
            for b in range(3):
                gk[3 * a + b] += jnp.sum(grad_depth * window(a, b), axis=0)
        return act_sum

    count = len(windows)
    normal, wide, sums = {}, {}, []
    for i in range(count + 2):
        if i >= 2:
            k = i - 2
            sums.append((back(windows[k], normal[k][1], normal[k][2], *wide[k]), normal[k][0]))
        if 1 <= i <= count:
            wide[i - 1] = hidden(normal[i - 1][3], slope_scales[i - 1])
        if i < count:
            normal[i] = norm(windows[i])
        if i >= 2 and (i - 1) % together == 0:
            ks = range(i - 1 - together, i - 1)
            gi_ref[...] += lax.dot_general(
                jnp.concatenate([normal[k][3] for k in ks], axis=0), jnp.concatenate([wide[k][1] for k in ks], axis=0),
                (((0,), (0,)), ((), ())), preferred_element_type=jnp.float32)
    return sums


def inner_kernel(table_ref, feat_ref, rows_hbm, taps_ref, gain_ref, w_in_hbm, w_out_hbm,
                 ge, ga, act, cen, gi_ref, gk, gg, taps, pad, rows_ref, w_in_ref, w_out_ref, sems):
    g = pl.program_id(0)
    me = lax.axis_index("tile")
    count = table_ref[me]

    @pl.when(g == 0)
    def _():
        copies = [
            pltpu.make_async_copy(src, dst, sems.at[k])
            for k, (src, dst) in enumerate(((rows_hbm, rows_ref), (w_out_hbm, w_out_ref), (w_in_hbm, w_in_ref)))
        ]
        for copy in copies:
            copy.start()
        for ref in (gk, gg, gi_ref, act, cen, ge):
            ref[...] = jnp.zeros_like(ref)
        for k in range(9):
            taps[k] = jnp.broadcast_to(taps_ref[k:k + 1, :].astype(jnp.float32), (G, C))
        first = start_of(table_ref, me) + table_ref[2 * PEERS]
        for copy in copies:
            copy.wait()

        def row(i, _):
            rank = (first + i) & (GROUP_TOTAL - 1)
            worker = table_ref[PEERS + (rank & (PEERS - 1))]
            ge[pl.ds(i, 1), :] = rows_ref[worker, pl.ds(i >> 5, 1), :] * (1.0 / (S * S))
            return 0

        lax.fori_loop(0, count, row, 0)
        ga[...] = lax.dot_general(ge[...], w_out_ref[...].astype(jnp.float32), (((1,), (1,)), ((), ())),
                                  precision=HIGHEST, preferred_element_type=jnp.float32)

    @pl.when(g * G < count)
    def _():
        for t in range(G):
            fill_centre(pad, feat_ref, t, t)
        side = S - 2

        lines = 14

        def window_of(top):
            def window(a, b):
                rows = [pad[pl.ds(((y + a) * W + 1 + b) * G, side * G), :] for y in range(top, top + lines)]
                return jnp.concatenate(rows, axis=0).reshape(lines * side, G, C)
            return window

        mine = pl.ds(pl.multiple_of(g * G, G), G)
        windows = [window_of(top) for top in range(1, S - 1, lines)]
        scale = ga[mine, :]
        sums = pixel_math(windows, lines * side, 1, [scale] * len(windows), taps, gain_ref[...], w_in_ref,
                          gi_ref, gk, gg)
        act[mine, :] = sum(part[0] for part in sums)
        cen[mine, :] = sum(part[1] for part in sums)


def whole(x):
    return pl.BlockSpec(x.shape, lambda g, *_: (0,) * len(x.shape))


def inner(table, feat, rows, taps, gain, w_in, w_out):
    f32 = jnp.float32
    outs = [
        jax.ShapeDtypeStruct(shape, f32)
        for shape in ((SLOTS, C), (SLOTS, HID), (SLOTS, HID), (SLOTS, C), (C, HID), (9, G, C), (G, C), (9, G, C))
    ]
    grid_spec = pltpu.PrefetchScalarGridSpec(
        num_scalar_prefetch=1,
        grid=(SLOTS // G,),
        in_specs=[pl.BlockSpec((G, S, S, C), lambda g, *_: (g, 0, 0, 0))]
        + [pl.BlockSpec(memory_space=pltpu.HBM), whole(taps), whole(gain)]
        + [pl.BlockSpec(memory_space=pltpu.HBM)] * 2,
        out_specs=[whole(x) for x in outs],
        scratch_shapes=[
            pltpu.VMEM((W * W * G, C), f32),
            pltpu.VMEM(rows.shape, f32),
            pltpu.VMEM(w_in.shape, jnp.bfloat16),
            pltpu.VMEM(w_out.shape, jnp.bfloat16),
            pltpu.SemaphoreType.DMA((3,)),
        ],
    )
    return pl.pallas_call(
        inner_kernel,
        grid_spec=grid_spec,
        out_shape=outs,
        compiler_params=pltpu.CompilerParams(vmem_limit_bytes=50 << 20),
        cost_estimate=pl.CostEstimate(flops=10_000_000_000, bytes_accessed=100_000_000, transcendentals=0),
        name="inner",
    )(table, feat, rows, taps, gain, w_in, w_out)


PAIR = 4


def border_kernel(nb_ref, table_ref, feat_ref, left_ref, own_ref, right_ref, gain_ref, w_in_ref,
                  w_out_ref, ge, ga, act_in, cen_in, gi_in, gk_in, gg_in, taps,
                  send_ref, go_ref, gi_ref, small_ref, where_ref, pad, strips, act, cen, gk, gg, sems):
    g = pl.program_id(0)
    me = lax.axis_index("tile")
    count = table_ref[me]
    turn = table_ref[2 * PEERS]
    base = (me - 1) * SLOTS

    @pl.when(g == 0)
    def _():
        copies = [
            pltpu.make_async_copy(ref, strips.at[pl.ds(k * SLOTS, SLOTS)], sems.at[k])
            for k, ref in enumerate((left_ref, own_ref, right_ref))
        ]
        for copy in copies:
            copy.start()
        for ref, old in ((act, act_in), (cen, cen_in), (gi_ref, gi_in), (gk, gk_in), (gg, gg_in)):
            ref[...] = old[...]
        for copy in copies:
            copy.wait()

    @pl.when(g * PAIR * G < count)
    def _():
        for t in range(PAIR * G):
            pair_pad = pad.at[t // G]
            u = t % G
            fill_centre(pair_pad, feat_ref, u, t)

            def strip(k, which):
                n = nb_ref[k, g * PAIR * G + t]
                ok = n >= 0
                x = strips[jnp.where(ok, n - base, 0), which].astype(jnp.float32)
                return jnp.where(ok, x, 0.0)

            pair_pad[pl.ds(1 * G + u, S, stride=G), :] = strip(0, 1)
            pair_pad[pl.ds(((S + 1) * W + 1) * G + u, S, stride=G), :] = strip(1, 0)
            pair_pad[pl.ds(W * G + u, S, stride=G * W), :] = strip(2, 3)
            pair_pad[pl.ds((W + S + 1) * G + u, S, stride=G * W), :] = strip(3, 2)
            pair_pad[pl.ds(u, 1), :] = strip(4, 1)[S - 1:S]
            pair_pad[pl.ds((S + 1) * G + u, 1), :] = strip(5, 1)[0:1]
            pair_pad[pl.ds((S + 1) * W * G + u, 1), :] = strip(6, 0)[S - 1:S]
            pair_pad[pl.ds(((S + 1) * W + S + 1) * G + u, 1), :] = strip(7, 0)[0:1]

        def window_of(p):
            def window(a, b):
                part = pad.at[p]
                rows = [part[pl.ds(((y + a) * W + b) * G, S * G), :] for y in (0, S - 1)]
                for x in (0, S - 1):
                    rows += [part[pl.ds(((y + a) * W + x + b) * G, G), :] for y in range(1, S - 1)]
                return jnp.concatenate(rows, axis=0).reshape(4 * S - 4, G, C)
            return window

        spans = [pl.ds(pl.multiple_of((g * PAIR + p) * G, G), G) for p in range(PAIR)]
        sums = pixel_math([window_of(p) for p in range(PAIR)], 4 * S - 4, 2, [ga[span, :] for span in spans],
                          taps, gain_ref[...], w_in_ref, gi_ref, gk, gg)
        for span, (act_sum, centre) in zip(spans, sums):
            act[span, :] += act_sum
            cen[span, :] += centre

    @pl.when(g == pl.num_programs(0) - 1)
    def _():
        go_ref[...] = lax.dot_general(act[...], ge[...], (((0,), (0,)), ((), ())),
                                      precision=HIGHEST, preferred_element_type=jnp.float32)
        embed = jnp.dot(act[...], w_out_ref[...].astype(jnp.float32), precision=HIGHEST,
                        preferred_element_type=jnp.float32)
        cen[...] = (cen[...] + embed) * (1.0 / (S * S))
        small_ref[...] = jnp.zeros_like(small_ref)
        for k in range(9):
            small_ref[k:k + 1, :] = jnp.sum(gk[k], axis=0, keepdims=True)
        small_ref[9:10, :] = jnp.sum(gg[...], axis=0, keepdims=True)
        send_ref[...] = jnp.zeros_like(send_ref)
        first = start_of(table_ref, me) + turn

        def out_row(i, _):
            rank = (first + i) & (GROUP_TOTAL - 1)
            worker = table_ref[PEERS + (rank & (PEERS - 1))]
            send_ref[worker, pl.ds(i >> 5, 1), :] = cen[pl.ds(i, 1), :]
            return 0

        lax.fori_loop(0, count, out_row, 0)
        residue = lax.fori_loop(0, PEERS, lambda r, s: jnp.where(table_ref[PEERS + r] == me, r, s), jnp.int32(0))

        def arrival(owner, start):
            slot = (residue - start - turn) & (PEERS - 1)
            for k in range(2):
                @pl.when(slot + k * PEERS < table_ref[owner])
                def _():
                    place = ((start + slot + k * PEERS + turn) & (GROUP_TOTAL - 1)) >> 5
                    where_ref[place] = owner
                    where_ref[WORK + place] = k
            return start + table_ref[owner]

        lax.fori_loop(0, PEERS, arrival, jnp.int32(0))


def border(nb, table, feat, left, own, right, gain, w_in, w_out, sums):
    f32 = jnp.float32
    outs = [jax.ShapeDtypeStruct(shape, f32) for shape in ((PEERS, 2, C), (HID, C), (C, HID), (16, C))]
    grid_spec = pltpu.PrefetchScalarGridSpec(
        num_scalar_prefetch=2,
        grid=(SLOTS // (PAIR * G),),
        in_specs=[pl.BlockSpec((PAIR * G, S, S, C), lambda g, *_: (g, 0, 0, 0))]
        + [pl.BlockSpec(memory_space=pl.ANY)] * 3
        + [whole(x) for x in (gain, w_in, w_out, *sums)],
        out_specs=[whole(x) for x in outs] + [pl.BlockSpec(memory_space=pltpu.SMEM)],
        scratch_shapes=[
            pltpu.VMEM((PAIR, W * W * G, C), f32),
            pltpu.VMEM((3 * SLOTS, 4, S, C), jnp.bfloat16),
            pltpu.VMEM((SLOTS, HID), f32),
            pltpu.VMEM((SLOTS, C), f32),
            pltpu.VMEM((9, G, C), f32),
            pltpu.VMEM((G, C), f32),
            pltpu.SemaphoreType.DMA((3,)),
        ],
    )
    return pl.pallas_call(
        border_kernel,
        grid_spec=grid_spec,
        out_shape=outs + [jax.ShapeDtypeStruct((2 * WORK,), jnp.int32)],
        compiler_params=pltpu.CompilerParams(vmem_limit_bytes=40 << 20),
        name="border",
    )(nb, table, feat, left, own, right, gain, w_in, w_out, *sums)


UNITS = 17


def reduce_kernel(rows_ref, go_ref, gi_ref, small_ref, result, landed,
                  full, from_core, half, from_x, piece, from_tile,
                  row_send, row_recv, core_send, core_recv, x_send, x_recv, unit_send, unit_recv,
                  back_send, back_recv, x_back_send, x_back_recv, core_back_send, core_back_recv):
    me = lax.axis_index("tile")
    slide = lax.axis_index("slide")
    x, core = slide // 2, slide % 2
    partner = x * 2 + (1 - core)
    x_peers = [((x + d) % NX) for d in range(1, NX)]

    barrier = pltpu.get_barrier_semaphore()
    for d in range(1, PEERS):
        pl.semaphore_signal(barrier, inc=1, **to_tile((me + d) % PEERS))
    pl.semaphore_signal(barrier, inc=1, **to_slide(partner))
    for peer in x_peers:
        pl.semaphore_signal(barrier, inc=1, **to_slide(peer * 2 + core))

    for s in range(4):
        full[s // 2, s % 2, 0:16] = gi_ref[:, s * C:(s + 1) * C].reshape(16, 8, C)
        full[2 + s // 2, s % 2, 0:16] = go_ref[s * C:(s + 1) * C, :].reshape(16, 8, C)
    for s in range(8):
        full[s // 2, s % 2, 16] = small_ref[8 * s:8 * s + 8, :] if s < 2 else jnp.zeros((8, C), jnp.float32)

    pl.semaphore_wait(barrier, PEERS + NX - 1)

    to_core = pltpu.make_async_remote_copy(
        src_ref=full.at[:, 1 - core], dst_ref=from_core, send_sem=core_send, recv_sem=core_recv, **to_slide(partner))
    to_core.start()
    to_core.wait()
    half[...] = full[:, core] + from_core[...]

    x_copies = []
    for d in range(1, NX):
        x_copies.append(pltpu.make_async_remote_copy(
            src_ref=half.at[x_peers[d - 1]], dst_ref=from_x.at[d - 1],
            send_sem=x_send.at[d - 1], recv_sem=x_recv.at[d - 1], **to_slide(x_peers[d - 1] * 2 + core)))
        x_copies[-1].start()
    row_copies = []
    for d in range(1, PEERS):
        peer = (me + d) % PEERS
        row_copies.append(pltpu.make_async_remote_copy(
            src_ref=rows_ref.at[peer], dst_ref=landed.at[me],
            send_sem=row_send.at[d - 1], recv_sem=row_recv.at[d - 1], **to_tile(peer)))
        row_copies[-1].start()
    landed[me] = rows_ref[me]
    for copy in x_copies:
        copy.wait()
    piece[...] = half[x] + from_x[0] + from_x[1] + from_x[2]

    owners = [2 * u for u in range(16)] + [1]

    def unit_copy(u):
        return pltpu.make_async_remote_copy(
            src_ref=piece.at[u], dst_ref=from_tile.at[me],
            send_sem=unit_send.at[u], recv_sem=unit_recv.at[me], **to_tile(owners[u]))

    def back_copy(u, d):
        return pltpu.make_async_remote_copy(
            src_ref=result.at[x, core, u], dst_ref=result.at[x, core, u],
            send_sem=back_send.at[d - 1], recv_sem=back_recv.at[u], **to_tile((me + d) % PEERS))

    for u in range(UNITS):
        @pl.when(me != owners[u])
        def _():
            unit_copy(u).start()
    for u in range(UNITS):
        @pl.when(me == owners[u])
        def _():
            from_tile[owners[u]] = piece[u]
            for q in range(PEERS):
                if q != owners[u]:
                    pltpu.make_async_remote_copy(
                        src_ref=piece.at[u], dst_ref=from_tile.at[q],
                        send_sem=unit_send.at[u], recv_sem=unit_recv.at[q], **to_tile(q)).wait_recv()
            result[x, core, u] = jnp.sum(from_tile[...], axis=0)
            for d in range(1, PEERS):
                back_copy(u, d).start()
    for u in range(UNITS):
        @pl.when(me != owners[u])
        def _():
            unit_copy(u).wait_send()
            back_copy(u, 1).wait_recv()

    to_partner = []

    def forward(k, where):
        to_partner.append(pltpu.make_async_remote_copy(
            src_ref=result.at[where, core], dst_ref=result.at[where, core],
            send_sem=core_back_send.at[k], recv_sem=core_back_recv.at[k], **to_slide(partner)))
        to_partner[-1].start()

    x_back = []
    for d in range(1, NX):
        x_back.append(pltpu.make_async_remote_copy(
            src_ref=result.at[x, core], dst_ref=result.at[x, core],
            send_sem=x_back_send.at[d - 1], recv_sem=x_back_recv.at[d - 1], **to_slide(x_peers[d - 1] * 2 + core)))
        x_back[-1].start()
    forward(0, x)
    for copy in row_copies:
        copy.wait()
    for d in range(1, NX):
        x_back[d - 1].wait_recv()
        forward(d, (x + NX - d) % NX)
    for copy in x_back:
        copy.wait_send()
    for u in range(UNITS):
        @pl.when(me == owners[u])
        def _():
            for d in range(1, PEERS):
                back_copy(u, d).wait_send()
    for copy in to_partner:
        copy.wait()


def finish_kernel(where_ref, result, landed, embed_ref, gk_ref, gg_ref, gi_out, go_out):
    for j in range(WORK):
        embed_ref[j:j + 1, :] = landed[where_ref[j], pl.ds(where_ref[WORK + j], 1), :]
    for s in range(4):
        gi_out[:, s * C:(s + 1) * C] = result[s // 2, s % 2, 0:16].reshape(C, C)
        go_out[s * C:(s + 1) * C, :] = result[2 + s // 2, s % 2, 0:16].reshape(C, C)
    gk_ref[0:8, :] = result[0, 0, 16]
    gk_ref[8:9, :] = result[0, 1, 16, 0:1]
    gg_ref[...] = result[0, 1, 16, 1:2]


def reduce(where, rows, go, gi, small):
    dma = pltpu.SemaphoreType.DMA
    f32 = jnp.float32
    vmem = pl.BlockSpec(memory_space=pltpu.VMEM)
    result, landed = pl.pallas_call(
        reduce_kernel,
        in_specs=[vmem] * 4,
        out_specs=[vmem] * 2,
        out_shape=[
            jax.ShapeDtypeStruct((NX, 2, UNITS, 8, C), f32),
            jax.ShapeDtypeStruct((PEERS, 2, C), f32),
        ],
        scratch_shapes=[
            pltpu.VMEM((NX, 2, UNITS, 8, C), f32),
            pltpu.VMEM((NX, UNITS, 8, C), f32),
            pltpu.VMEM((NX, UNITS, 8, C), f32),
            pltpu.VMEM((NX - 1, UNITS, 8, C), f32),
            pltpu.VMEM((UNITS, 8, C), f32),
            pltpu.VMEM((PEERS, 8, C), f32),
            dma((PEERS - 1,)), dma((PEERS - 1,)), dma, dma, dma((NX - 1,)), dma((NX - 1,)),
            dma((UNITS,)), dma((PEERS,)), dma((PEERS - 1,)), dma((UNITS,)),
            dma((NX - 1,)), dma((NX - 1,)), dma((NX,)), dma((NX,)),
        ],
        compiler_params=pltpu.CompilerParams(
            collective_id=1, has_side_effects=True, vmem_limit_bytes=32 << 20),
        name="reduce",
    )(rows, go, gi, small)
    return pl.pallas_call(
        finish_kernel,
        in_specs=[pl.BlockSpec(memory_space=pltpu.SMEM), vmem, vmem],
        out_specs=[vmem] * 5,
        out_shape=[
            jax.ShapeDtypeStruct((WORK, C), f32),
            jax.ShapeDtypeStruct((9, C), f32),
            jax.ShapeDtypeStruct((1, C), f32),
            jax.ShapeDtypeStruct((C, HID), f32),
            jax.ShapeDtypeStruct((HID, C), f32),
        ],
        compiler_params=pltpu.CompilerParams(vmem_limit_bytes=16 << 20),
        name="finish",
    )(where, result, landed)


def local(features, tissue_count, neighbors, worker_perm, rotation, kernel, gain, w_in, w_out, cotangent):
    feat = features[0]
    strips, rows, table = exchange(tissue_count, worker_perm, rotation, feat, cotangent[0])
    rows = rows.reshape(PEERS, 2, C)
    peers = lax.axis_size("tile")
    left = lax.ppermute(strips, "tile", [(i, i + 1) for i in range(peers - 1)])
    right = lax.ppermute(strips, "tile", [(i + 1, i) for i in range(peers - 1)])
    sums = inner(table, feat, rows, kernel, gain[None], w_in, w_out)
    send, go, gi, small, where = border(
        neighbors[0].T, table, feat, left, strips, right, gain[None], w_in, w_out, sums)
    embed, grad_kernel, grad_gain, grad_in, grad_out = reduce(where, send, go, gi, small)
    return embed[None], grad_kernel, grad_gain[0], grad_in, grad_out


def solution(mesh):
    placed = (
        P("slide", "tile", None, None, None),
        P("slide", "tile"),
        P("slide", "tile", None),
        P("slide", None),
        P("slide"),
        P(),
        P(),
        P(),
        P(),
        P("slide", "tile", None),
    )
    return jax.shard_map(
        local,
        mesh=mesh,
        in_specs=placed,
        out_specs=(P("slide", "tile", None), P(), P(), P(), P()),
        check_vma=False,
    )
```
